32 devices in a mesh: grp: 2 (over x), px: 4 (over y, core), py: 4 (over z).
Axes of the slice: x: 2, y: 2, z: 4, core: 2. Of those that a mesh axis runs over, the one named last changes fastest.
Arguments:
- multiplier: float32 [3, 32, 16, 256, 256], P(None, 'py', None, ('grp', 'px')), may hold values from -6 to 6
- auxiliary: float32 [3, 32, 16, 256, 256], P(None, 'py', None, ('grp', 'px')), may hold values from -6 to 6
- density_start: float32 [16, 256, 256], P(None, ('grp', 'px')), may hold values from 0.5 to 2
- density_end: float32 [16, 256, 256], P(None, ('grp', 'px')), may hold values from 0.5 to 2
Outputs:
- multiplier_next: float32 [3, 32, 16, 256, 256], P(None, 'py', None, ('grp', 'px'))
- auxiliary_next: float32 [3, 32, 16, 256, 256], P(None, 'py', None, ('grp', 'px'))
The draws below stay inside these ranges and needn't reach their ends.
All inputs are finite; a program needn't handle non-finite values.
Results may differ from the reference program's by a relative error of at most 0.0003.
Values sent between devices are 32-bit elements; how exact they have to be, the bound alone decides.
A program may use at most 128 MiB of HBM per device.

```python
import math
import jax
import jax.numpy as jnp
from jax import lax

NX = 256
NY = 256
LEVELS = 32
BATCH = 16
NEWTON = 4


def wave_field(key):
    keys = jax.random.split(key, 4)
    problem = jnp.arange(BATCH, dtype=jnp.int32)
    low_shift = jax.random.randint(keys[0], (), 0, 9)
    high_shift = jax.random.randint(keys[1], (), 0, 13)
    low_wave = 12 + (problem * 9 // BATCH + low_shift) % 9
    high_wave = 28 + (problem * 13 // BATCH + high_shift) % 13
    phases = jax.random.uniform(keys[2], (2, BATCH, 1, 1), jnp.float32, -math.pi, math.pi)
    row_signs = jnp.where(jax.random.bernoulli(keys[3], 0.5, (2, BATCH, NX, 1)), 1.0, -1.0).astype(jnp.float32)
    column = jnp.arange(NY, dtype=jnp.int32)
    low_phase = (low_wave[:, None] * column[None, :] % NY).astype(jnp.float32) * (2.0 * math.pi / NY)
    high_phase = (high_wave[:, None] * column[None, :] % NY).astype(jnp.float32) * (2.0 * math.pi / NY)
    low_part = jnp.cos(low_phase[:, None, :] + phases[0]) * row_signs[0]
    high_part = jnp.cos(high_phase[:, None, :] + phases[1]) * row_signs[1]
    return 1.5 * (low_part + high_part)


def field_draw(key):
    base_key = jax.random.fold_in(key, 101)
    wave_key = jax.random.fold_in(key, 202)
    shape = (3, LEVELS, BATCH, NX, NY)
    base = jax.random.normal(base_key, shape, jnp.float32)
    wave = wave_field(wave_key)
    second = base[2] + wave[None]
    whole = jnp.concatenate([base[:2], second[None]], axis=0)
    return jnp.clip(whole, -6.0, 6.0).astype(jnp.float32)


def draw_multiplier(key, part):
    return field_draw(jax.random.fold_in(key, 11))


def draw_auxiliary(key, part):
    return field_draw(jax.random.fold_in(key, 23))


def block_scale(stream_key, extent, cuts, least, high):
    def one(position, parts):
        draws = jax.random.uniform(jax.random.fold_in(jax.random.fold_in(stream_key, 6), position), (parts,), jnp.float32, least / len(cuts), high / len(cuts))
        return jnp.repeat(jnp.exp(draws), extent[position] // parts).reshape((-1,) + (1,) * (len(extent) - position - 1))

    gain = one(*cuts[0])
    for cut in cuts[1:]:
        gain = gain * one(*cut)
    return gain


def setup_inputs(seed: int = 0) -> dict:
    key_of = jax.random.split(jax.random.key(seed), 5)
    return {
        "multiplier": draw_multiplier(jax.random.fold_in(key_of[4], 71), 0),
        "auxiliary": draw_auxiliary(jax.random.fold_in(key_of[4], 71), 0),
        "density_start": jnp.clip(jnp.exp(math.log(2.0) - 1.3862944 * jax.random.uniform(key_of[2], (BATCH, NX, NY), jnp.float32) ** block_scale(key_of[2], (BATCH, NX, NY), ((1, 8),), -0.2, 0.2)), 0.5, 2.0),
        "density_end": jnp.clip(jnp.exp(math.log(2.0) - 1.3862944 * jax.random.uniform(key_of[3], (BATCH, NX, NY), jnp.float32) ** block_scale(key_of[3], (BATCH, NX, NY), ((1, 8),), -0.2, 0.2)), 0.5, 2.0),
    }


PENALTY = 1.0
PRECISE = lax.Precision.HIGHEST

def cosine_table(levels):
    mode_index = lax.broadcasted_iota(jnp.int32, (levels, levels), 0)
    time_index = lax.broadcasted_iota(jnp.int32, (levels, levels), 1)
    phase_index = mode_index * (2 * time_index + 1) % (4 * levels)
    angles = phase_index.astype(jnp.float32) * (math.pi / (2 * levels))
    weights = jnp.where(mode_index == 0, math.sqrt(1.0 / levels), math.sqrt(2.0 / levels))
    return weights * jnp.cos(angles)

def eigenvalues(levels, row_start, row_total, row_count, col_count):
    time_modes = lax.broadcasted_iota(jnp.int32, (levels, 1, 1, 1), 0).astype(jnp.float32)
    row_modes = (row_start + lax.broadcasted_iota(jnp.int32, (1, 1, row_total, 1), 2)).astype(jnp.float32)
    col_modes = lax.broadcasted_iota(jnp.int32, (1, 1, 1, col_count), 3).astype(jnp.float32)
    time_part = 4.0 * jnp.sin(time_modes * (math.pi / (2 * levels))) ** 2
    row_part = 4.0 * jnp.sin(row_modes * (math.pi / row_count)) ** 2
    col_part = 4.0 * jnp.sin(col_modes * (math.pi / col_count)) ** 2
    return time_part + row_part + col_part

def project(target):
    time_part = target[0]
    space_first = target[1]
    space_second = target[2]
    kinetic = 0.5 * (space_first * space_first + space_second * space_second)
    offset_one = 1.0 + time_part
    scaling = jnp.maximum(offset_one, 1.0) + jnp.cbrt(kinetic)
    for newton_step in range(NEWTON):
        residue = scaling * scaling * (scaling - offset_one) - kinetic
        derivative = scaling * (3.0 * scaling - 2.0 * offset_one)
        scaling = jnp.maximum(scaling - residue / derivative, 1.0)
    feasible = time_part + kinetic <= 0.0
    return jnp.stack([jnp.where(feasible, time_part, time_part - (scaling - 1.0)), jnp.where(feasible, space_first, space_first / scaling), jnp.where(feasible, space_second, space_second / scaling)])

def reference(multiplier, auxiliary, density_start, density_end):
    offset_field = auxiliary - multiplier / PENALTY
    level_index = lax.broadcasted_iota(jnp.int32, (LEVELS, 1, 1, 1), 0)
    offset_time = jnp.where(level_index == LEVELS - 1, 0.0, offset_field[0])
    earlier = jnp.concatenate([jnp.zeros_like(offset_time[:1]), offset_time[:-1]], axis=0)
    boundary = jnp.where(level_index == 0, -density_start / PENALTY, 0.0) + jnp.where(level_index == LEVELS - 1, density_end / PENALTY, 0.0)
    offset_first = offset_field[1]
    offset_second = offset_field[2]
    source = earlier - offset_time + jnp.roll(offset_first, 1, axis=2) - offset_first + jnp.roll(offset_second, 1, axis=3) - offset_second + boundary
    cosine = cosine_table(LEVELS)
    transformed = jnp.einsum('kt,tbxy->kbxy', cosine, source, precision=PRECISE)
    spectrum = jnp.fft.fft2(transformed, axes=(2, 3))
    eigen = eigenvalues(LEVELS, 0, NX, NX, NY)
    positive = eigen > 0.0
    inverse = jnp.where(positive, 1.0 / jnp.where(positive, eigen, 1.0), 0.0)
    potential_modes = jnp.real(jnp.fft.ifft2(spectrum * inverse, axes=(2, 3))).astype(source.dtype)
    potential = jnp.einsum('kt,kbxy->tbxy', cosine, potential_modes, precision=PRECISE)
    time_rate = jnp.concatenate([potential[1:] - potential[:-1], jnp.zeros_like(potential[:1])], axis=0)
    gradient = jnp.stack([time_rate, jnp.roll(potential, -1, axis=2) - potential, jnp.roll(potential, -1, axis=3) - potential])
    target = gradient + multiplier / PENALTY
    auxiliary_next = project(target)
    multiplier_next = multiplier + PENALTY * (gradient - auxiliary_next)
    return (multiplier_next, auxiliary_next)
```

```python
import functools
import math

import jax
import jax.numpy as jnp
import ml_dtypes
import numpy as np
from jax import lax
from jax.experimental import pallas as pl
from jax.experimental.pallas import tpu as pltpu
from jax.sharding import PartitionSpec as P

NEWTON = 4
PENALTY = 1.0
VMEM_LIMIT = 60 * 1024 * 1024
SPACE = ("grp", "px")
EVERY = ("grp", "px", "py")
MESH = pl.DeviceIdType.MESH
bf16 = jnp.bfloat16
f32 = jnp.float32


def halves(table):
    high = table.astype(ml_dtypes.bfloat16)
    low = (table - high.astype(np.float64)).astype(ml_dtypes.bfloat16)
    return np.stack([high, low])


def hartley(length):
    angles = 2.0 * np.pi / length * (np.outer(np.arange(length), np.arange(length)) % length)
    return (np.cos(angles) + np.sin(angles)) / np.sqrt(length)


def cosines(length):
    k = np.arange(length)[:, None]
    x = np.arange(length)[None, :]
    weights = np.where(k == 0, np.sqrt(1.0 / length), np.sqrt(2.0 / length))
    return weights * np.cos(np.pi * k * (2 * x + 1) / (2 * length))


def slab_tables(rows, cols, here, blocks):
    j = np.arange(rows)[:, None]
    n = np.arange(cols)[None, :]
    lam = 4.0 * np.sin(np.pi * j / (2 * rows)) ** 2 + 4.0 * np.sin(np.pi * n / cols) ** 2
    sinh = np.sqrt(lam * (1.0 + 0.25 * lam))
    ratio = 1.0 / (1.0 + 0.5 * lam + sinh)
    positive = lam > 0.0
    full = ratio ** (2 * here * blocks)
    scale = np.where(positive, 0.5 / np.where(positive, sinh * (1.0 - full), 1.0), 0.0)
    edge = cosines(rows)[:, :1]
    low, high, down, low_q, high_q = [], [], [], [], []
    for block in range(blocks):
        first = block * here
        lows = [1.0 + ratio ** (2 * (first + v) + 1) for v in range(here + 1)]
        highs = [1.0 + ratio ** (2.0 * (blocks * here - 1 - first - v) + 1.0) for v in range(here + 1)]
        low.append(lows)
        high.append(highs)
        down.append([ratio**v * highs[v] for v in range(here + 1)])
        low_q.append([edge * ratio ** (here - v) * lows[v] for v in range(here)])
        high_q.append([edge * ratio**v * highs[v] for v in range(here)])
    single = np.stack([ratio, ratio**here, scale, edge * scale, np.broadcast_to(edge, lam.shape)])
    pack = lambda parts: np.asarray(parts, np.float32)
    per_block = np.concatenate(
        [pack(low), pack(high), pack(down), pack(low_q), pack(high_q)], axis=1
    )
    return single.astype(np.float32), per_block


def ring_tables(rows, cols, group, levels):
    r = np.arange(group)[:, None, None]
    k = np.arange(levels)[None, :, None]
    n = np.arange(cols)[None, None, :]
    tau = 4.0 * np.sin(np.pi * k / (2 * levels)) ** 2
    kappa = tau + 4.0 * np.sin(np.pi * n / cols) ** 2
    turn = 2.0 * np.sin(np.pi * r / group) ** 2
    positive = kappa > 0.0
    safe = np.where(positive, kappa, 1.0)
    shrink = 1.0 / (1.0 + 0.5 * safe + np.sqrt(safe * (1.0 + 0.25 * safe)))
    far = shrink**rows
    inverse = (1.0 - shrink) * (1.0 - far * far) / (
        (1.0 + shrink) * ((1.0 - far) ** 2 + 2.0 * far * turn)
    )
    inverse = np.where(positive, inverse, np.where(r == 0, 1.0 / rows, 0.0))
    edge = math.sqrt(1.0 / rows)
    flat = inverse[:, :, :1]
    moving = edge * flat / np.where(tau > 0.0, tau, 1.0)
    still = rows * edge / np.where(r > 0, 2.0 * turn, 1.0) * (r > 0)
    extra = np.where(tau > 0.0, moving, still)
    mix = np.kron(hartley(group), cosines(levels))
    flat_rows = group * levels
    return (
        mix.astype(np.float32),
        inverse.reshape(flat_rows, cols).astype(np.float32),
        extra.reshape(flat_rows, 1).astype(np.float32),
    )


def split(x):
    high = x.astype(bf16)
    return high, (x - high.astype(f32)).astype(bf16)


def mm(a, b):
    return jnp.dot(a, b, preferred_element_type=f32)


def times_table(x, table):
    high, low = split(x)
    return mm(high, table[0]) + (mm(low, table[0]) + mm(high, table[1]))


def table_times(table, x):
    high, low = split(x)
    return mm(table[0], high) + (mm(table[0], low) + mm(table[1], high))


def precise(a, b):
    return jnp.dot(a, b, precision=lax.Precision.HIGHEST, preferred_element_type=f32)


def over_rows(table, x, out):
    problems, rows, cols = x.shape
    size = table.shape[1]
    bunch = size // rows
    for g in range(problems // bunch):
        part = x[g * bunch : (g + 1) * bunch].reshape(size, cols)
        out[g * bunch : (g + 1) * bunch] = table_times(table, part).reshape(bunch, rows, cols)


def source_kernel(
    mult, aux, start, end, col_table, row_table, single, per_block,
    modes, up, down, rims, prev, body, tail, *, levels, here
):
    t = pl.program_id(0)
    problems, rows, cols = body.shape
    level = lax.axis_index("py") * here + t
    row = lax.broadcasted_iota(jnp.int32, (rows, cols), 0)

    @pl.when(t == 0)
    def _():
        prev[...] = jnp.zeros_like(prev)
        tail[...] = jnp.zeros_like(tail)
        up[...] = jnp.zeros_like(up)
        down[...] = jnp.zeros_like(down)

    @pl.when(t < here)
    def _():
        keep = jnp.where(level == levels - 1, 0.0, 1.0)
        begin = jnp.where(level == 0, -1.0 / PENALTY, 0.0)
        finish = jnp.where(level == levels - 1, 1.0 / PENALTY, 0.0)

        def one(b, carry):
            along = aux[1, 0, b] - mult[1, 0, b] / PENALTY
            tail[b, pl.ds(t, 1), :] = along[rows - 1 :, :]
            beside = jnp.where(row == 0, 0.0, pltpu.roll(along, 1, 0))
            along = jnp.where(row == rows - 1, 0.0, along)
            second = aux[2, 0, b] - mult[2, 0, b] / PENALTY
            across = pltpu.roll(second, 1, 1) - second
            now = (aux[0, 0, b] - mult[0, 0, b] / PENALTY) * keep
            boundary = begin * start[b] + finish * end[b]
            body[b] = prev[b] - now + beside - along + across + boundary
            prev[b] = now
            return carry

        lax.fori_loop(0, problems, one, 0, unroll=4)

    @pl.when(t == here)
    def _():
        body[...] = prev[...]
        held = tail.shape[1]
        flat = tail[...].reshape(problems * held, cols)
        rims[...] = times_table(flat, col_table).reshape(problems, held, cols)

    spread = times_table(body[...].reshape(problems * rows, cols), col_table)
    over_rows(row_table, spread.reshape(problems, rows, cols), modes.at[0])
    ratio = single[0]
    low = per_block[t]
    falling = per_block[2 * (here + 1) + t]

    def add(b, carry):
        value = modes[0, b]
        up[b] = ratio * up[b] + low * value
        down[b] = down[b] + falling * value
        return carry

    lax.fori_loop(0, problems, add, 0, unroll=4)


def carry_kernel(up_own, down_own, step, up_in, down_in, up_got, down_got, up_out, down_out,
                 up_sent, up_came, down_sent, down_came, *, blocks, pieces, lag):
    me = lax.axis_index("py")
    size = up_own.shape[0] // pieces
    has_lower = me > 0
    has_upper = me < blocks - 1

    def copy(source, target, sent, came, k, other):
        cut = pl.ds(k * size, size)
        return pltpu.make_async_remote_copy(
            src_ref=source.at[cut],
            dst_ref=target.at[cut],
            send_sem=sent.at[k],
            recv_sem=came.at[k],
            device_id={"py": other},
            device_id_type=MESH,
        )

    barrier = pltpu.get_barrier_semaphore()

    @pl.when(has_lower)
    def _():
        pl.semaphore_signal(barrier, inc=1, device_id={"py": me - 1}, device_id_type=MESH)

    @pl.when(has_upper)
    def _():
        pl.semaphore_signal(barrier, inc=1, device_id={"py": me + 1}, device_id_type=MESH)

    @pl.when(has_lower & has_upper)
    def _():
        pl.semaphore_wait(barrier, 2)

    @pl.when(jnp.logical_not(has_lower & has_upper))
    def _():
        pl.semaphore_wait(barrier, 1)

    def relay(k, own, got, out, sent, came, first, last, ahead):
        cut = pl.ds(k * size, size)

        @pl.when(jnp.logical_not(first))
        def _():
            copy(out, got, sent, came, k, ahead).wait_recv()

            @pl.when(jnp.logical_not(last))
            def _():
                out[cut] = own[cut] + step[...] * got[cut]
                copy(out, got, sent, came, k, ahead).start()

    up = (up_own, up_got, up_out, up_sent, up_came, me == 0, me == blocks - 1,
          (me + 1) % blocks)
    down = (down_own, down_got, down_out, down_sent, down_came, me == blocks - 1, me == 0,
            (me + blocks - 1) % blocks)

    @pl.when(me == 0)
    def _():
        for k in range(pieces):
            copy(up_own, up_got, up_sent, up_came, k, me + 1).start()

    @pl.when(me == blocks - 1)
    def _():
        for k in range(pieces):
            copy(down_own, down_got, down_sent, down_came, k, me - 1).start()

    def weave(early, late):
        for k in range(pieces + lag):
            if k < pieces:
                relay(k, *early)
            if k >= lag:
                relay(k - lag, *late)

    lower_half = me < blocks // 2

    @pl.when(lower_half)
    def _():
        weave(up, down)

    @pl.when(jnp.logical_not(lower_half))
    def _():
        weave(down, up)

    @pl.when(has_lower)
    def _():
        up_in[...] = up_got[...]
        for k in range(pieces):
            copy(down_out, down_got, down_sent, down_came, k, me - 1).wait_send()

    @pl.when(me == 0)
    def _():
        up_in[...] = jnp.zeros_like(up_in)

    @pl.when(has_upper)
    def _():
        down_in[...] = down_got[...]
        for k in range(pieces):
            copy(up_out, up_got, up_sent, up_came, k, me + 1).wait_send()

    @pl.when(me == blocks - 1)
    def _():
        down_in[...] = jnp.zeros_like(down_in)


def trace_kernel(modes, up, down, rims, single, per_block, pay, *, here):
    _, problems, rows, cols = modes.shape
    lane = lax.broadcasted_iota(jnp.int32, (1, cols), 1)
    parity = lax.broadcasted_iota(jnp.int32, (8, cols), 0) % 2 == 0

    def one(b, carry):
        total = [jnp.zeros((8, cols), f32) for _ in range(here)]
        for c in range(rows // 8):
            cut = slice(c * 8, c * 8 + 8)
            ratio, weight = single[0, cut, :], single[3, cut, :]
            lows = [per_block[v, cut, :] for v in range(here + 1)]
            highs = [per_block[here + 1 + v, cut, :] for v in range(here + 1)]
            value = up[b, cut, :]
            sums = []
            for v in range(here):
                if v:
                    value = ratio * value
                value = value + lows[v] * modes[v, b, cut, :]
                sums.append(highs[v] * value)
            behind = down[b, cut, :]
            for v in range(here, -1, -1):
                if v < here:
                    total[v] = total[v] + weight * (sums[v] + lows[v] * behind)
                behind = ratio * (behind + highs[v] * modes[v, b, cut, :])
        for v in range(here):
            even = jnp.sum(jnp.where(parity, total[v], 0.0), axis=0, keepdims=True)
            odd = jnp.sum(jnp.where(parity, 0.0, total[v]), axis=0, keepdims=True)
            pay[b, v : v + 1, :] = even + odd
            pay[b, here + v : here + v + 1, :] = even - odd + rims[b, v : v + 1, :]
            flat = jnp.where(lane == 0, modes[v, b, 0:1, :], 0.0)
            if v == 0:
                beyond = pltpu.roll(modes[here, b, 0:8, :], 1, 1)[0:1]
                flat = flat + jnp.where(lane == 1, beyond, 0.0)
            pay[b, 2 * here + v : 2 * here + v + 1, :] = flat
        return carry

    lax.fori_loop(0, problems, one, 0)


def ring_kernel(left, right, flat, mix, mix_back, inverse, extra, out, *, here, levels):
    total, width = left.shape
    lane = lax.broadcasted_iota(jnp.int32, (total, width), 1)
    ahead = total - levels
    jump = pltpu.roll(left[...], ahead, 0) - right[...]
    beyond = pltpu.roll(pltpu.roll(flat[...], here, 0), width - 1, 1)
    whole = jnp.where(lane == 0, flat[...] + beyond, 0.0)
    jump_flat = pltpu.roll(whole, ahead, 0) - whole
    solved = precise(mix[...], jump) * inverse[...] + precise(mix[...], jump_flat) * extra[...]
    out[...] = precise(mix_back[...], solved)


def flux_kernel(flux, per_block, up, down, *, here):
    problems, rows, cols = up.shape
    sign = jnp.where(lax.broadcasted_iota(jnp.int32, (rows, cols), 0) % 2 == 0, 1.0, -1.0)
    base = 3 * (here + 1)

    def one(b, carry):
        rise = jnp.zeros((rows, cols), f32)
        fall = jnp.zeros((rows, cols), f32)
        for v in range(here):
            mine = jnp.broadcast_to(flux[b, v : v + 1, :], (rows, cols))
            other = jnp.broadcast_to(flux[b, here + v : here + v + 1, :], (rows, cols))
            both = sign * mine - other
            rise = rise + per_block[base + v] * both
            fall = fall + per_block[base + here + v] * both
        up[b] = rise
        down[b] = fall
        return carry

    lax.fori_loop(0, problems, one, 0)


def project_kernel(
    modes, flux, rims, up1, down1, up2, down2, col_table, row_back, single, per_block, mult,
    next_mult, next_aux, wave, phi, following, edges, *, levels, here
):
    t = pl.program_id(0)
    problems, rows, cols = phi.shape
    first = lax.axis_index("py") * here
    moving = jnp.where(first + t == levels - 1, 0.0, 1.0)

    def field(at, to):
        over_rows(row_back, wave[at], to)
        flat = to[...].reshape(problems * rows, cols)
        to[...] = times_table(flat, col_table).reshape(problems, rows, cols)

    def sweep(b, carry):
        for c in range(rows // 8):
            cut = slice(c * 8, c * 8 + 8)
            ratio, scale, edge = single[0, cut, :], single[2, cut, :], single[4, cut, :]
            sign = jnp.where(
                lax.broadcasted_iota(jnp.int32, (8, cols), 0) % 2 == 0, edge, -edge
            )
            lows = [per_block[v, cut, :] for v in range(here + 1)]
            highs = [per_block[here + 1 + v, cut, :] for v in range(here + 1)]
            value = up1[b, cut, :] + up2[b, cut, :]
            source, sums = [], []
            for v in range(here + 1):
                now = modes[v, b, cut, :]
                if v < here:
                    mine = jnp.broadcast_to(flux[b, v : v + 1, :], (8, cols))
                    other = jnp.broadcast_to(flux[b, here + v : here + v + 1, :], (8, cols))
                    now = now + (sign * mine - edge * other)
                source.append(now)
                if v:
                    value = ratio * value
                value = value + lows[v] * now
                sums.append(highs[v] * value)
            behind = down1[b, cut, :] + down2[b, cut, :]
            for v in range(here, -1, -1):
                wave[v, b, cut, :] = scale * (sums[v] + lows[v] * behind)
                behind = ratio * (behind + highs[v] * source[v])
            if c == 0:
                spot = (lax.broadcasted_iota(jnp.int32, (8, 128), 0) == 0) & (
                    lax.broadcasted_iota(jnp.int32, (8, 128), 1) == 0
                )
                below = 0.5 * (up1[b, 0:8, 0:128] + up2[b, 0:8, 0:128])
                whole = below + 0.5 * (down1[b, 0:8, 0:128] + down2[b, 0:8, 0:128])
                for v in range(here + 1):
                    whole = whole + source[v][:, 0:128]
                mean = whole * (1.0 / levels)
                level_value = jnp.zeros((8, 128), f32)
                for v in range(here + 1):
                    wave[v, b, 0:8, 0:128] = jnp.where(spot, level_value, wave[v, b, 0:8, 0:128])
                    if v < here:
                        below = below + source[v][:, 0:128]
                        count = (first + (v + 1)).astype(f32)
                        level_value = level_value - (below - count * mean)
        return carry

    @pl.when(t == 0)
    def _():
        lax.fori_loop(0, problems, sweep, 0)
        field(0, following)
        held = edges.shape[1]
        flat = (flux[:, 0:here, :] + rims[:, 0:here, :]).reshape(problems * here, cols)
        edges[:, 0:here, :] = times_table(flat, col_table).reshape(problems, here, cols)

    phi[...] = following[...]
    field(t + 1, following)
    row = lax.broadcasted_iota(jnp.int32, (rows, cols), 0)

    def one(b, carry):
        here_phi = phi[b]
        rim = jnp.broadcast_to(edges[b, pl.ds(t, 1), :], (rows, cols))
        grad_time = (following[b] - here_phi) * moving
        grad_first = jnp.where(
            row == rows - 1, rim, pltpu.roll(here_phi, rows - 1, 0) - here_phi
        )
        grad_second = pltpu.roll(here_phi, cols - 1, 1) - here_phi
        mult_time, mult_first, mult_second = (mult[k, 0, b] for k in range(3))
        time_part = grad_time + mult_time / PENALTY
        along = grad_first + mult_first / PENALTY
        beside = grad_second + mult_second / PENALTY
        kinetic = 0.5 * (along * along + beside * beside)
        offset_one = 1.0 + time_part
        solid = kinetic > 1e-37
        root = jnp.exp(jnp.log(jnp.where(solid, kinetic, 1.0)) * (1.0 / 3.0))
        scaling = jnp.maximum(offset_one, 1.0) + jnp.where(solid, root, 0.0)
        twice = 2.0 * offset_one
        for newton_step in range(NEWTON):
            above = scaling * scaling * (2.0 * scaling - offset_one) + kinetic
            derivative = scaling * (3.0 * scaling - twice)
            scaling = jnp.maximum(above / derivative, 1.0)
        feasible = time_part + kinetic <= 0.0
        shrink = jnp.where(feasible, 1.0, 1.0 / scaling)
        out_time = jnp.where(feasible, time_part, time_part - (scaling - 1.0))
        out_along = along * shrink
        out_beside = beside * shrink
        next_aux[0, 0, b] = out_time
        next_aux[1, 0, b] = out_along
        next_aux[2, 0, b] = out_beside
        next_mult[0, 0, b] = mult_time + PENALTY * (grad_time - out_time)
        next_mult[1, 0, b] = mult_first + PENALTY * (grad_first - out_along)
        next_mult[2, 0, b] = mult_second + PENALTY * (grad_second - out_beside)
        return carry

    lax.fori_loop(0, problems, one, 0, unroll=2)


def params():
    return pltpu.CompilerParams(vmem_limit_bytes=VMEM_LIMIT)


def whole_block(shape):
    return pl.BlockSpec(shape, lambda *_: (0,) * len(shape))


def local(multiplier, auxiliary, density_start, density_end):
    _, here, problems, rows, cols = multiplier.shape
    blocks = lax.axis_size("py")
    group = lax.axis_size("grp") * lax.axis_size("px")
    devices = group * blocks
    levels = here * blocks
    held = -(-here // 8) * 8
    bunch = min(problems, max(1, 256 // rows))
    shape = lambda *s: jax.ShapeDtypeStruct(s, f32)

    col_table = jnp.asarray(halves(hartley(cols)))
    cosine = np.kron(np.eye(bunch), cosines(rows))
    row_table = jnp.asarray(halves(cosine))
    row_back = jnp.asarray(halves(cosine.T))
    single, per_block = slab_tables(rows, cols, here, blocks)
    single = jnp.asarray(single)
    me = lax.axis_index("py")
    per_block = lax.dynamic_index_in_dim(jnp.asarray(per_block), me, 0, keepdims=False)
    mix, inverse, extra = ring_tables(rows, cols, group, levels)
    width = problems * cols // devices
    parts = cols // width
    flat_id = lax.axis_index(SPACE) * blocks + me
    slot = flat_id % parts
    inverse = lax.dynamic_slice_in_dim(jnp.asarray(inverse), slot * width, width, 1)
    extra = jnp.where(slot == 0, jnp.asarray(extra), 0.0)

    plane = (problems, rows, cols)
    level_block = pl.BlockSpec(
        (3, 1, problems, rows, cols), lambda t: (0, jnp.minimum(t, here - 1), 0, 0, 0)
    )
    modes, up_own, down_own, rims = pl.pallas_call(
        functools.partial(source_kernel, levels=levels, here=here),
        out_shape=(shape(here + 1, *plane), shape(*plane), shape(*plane),
                   shape(problems, held, cols)),
        grid=(here + 1,),
        in_specs=[level_block, level_block, whole_block(plane), whole_block(plane),
                  whole_block(col_table.shape), whole_block(row_table.shape),
                  whole_block(single.shape), whole_block(per_block.shape)],
        out_specs=(pl.BlockSpec((1, *plane), lambda t: (t, 0, 0, 0)), whole_block(plane),
                   whole_block(plane), whole_block((problems, held, cols))),
        scratch_shapes=[pltpu.VMEM(plane, f32), pltpu.VMEM(plane, f32),
                        pltpu.VMEM((problems, held, cols), f32)],
        compiler_params=params(),
        name="source",
    )(multiplier, auxiliary, density_start, density_end, col_table, row_table, single, per_block)

    vmem = pl.BlockSpec(memory_space=pltpu.VMEM)

    def carry(up, down, which):
        pieces = math.gcd(problems, 8)
        return pl.pallas_call(
            functools.partial(carry_kernel, blocks=blocks, pieces=pieces, lag=min(3, pieces)),
            out_shape=(shape(*plane), shape(*plane)),
            in_specs=[vmem, vmem, vmem],
            out_specs=(vmem, vmem),
            scratch_shapes=[pltpu.VMEM(plane, f32)] * 4 + [pltpu.SemaphoreType.DMA((pieces,))] * 4,
            compiler_params=pltpu.CompilerParams(
                collective_id=which, has_side_effects=True, vmem_limit_bytes=24 * 1024 * 1024
            ),
            name="carry%d" % which,
        )(up, down, single[1])

    up1, down1 = carry(up_own, down_own, 0)

    half = problems // 2
    pay = pl.pallas_call(
        functools.partial(trace_kernel, here=here),
        out_shape=shape(problems, 3 * here, cols),
        grid=(2,),
        in_specs=[pl.BlockSpec((here + 1, half, rows, cols), lambda i: (0, i, 0, 0)),
                  pl.BlockSpec((half, rows, cols), lambda i: (i, 0, 0)),
                  pl.BlockSpec((half, rows, cols), lambda i: (i, 0, 0)),
                  pl.BlockSpec((half, held, cols), lambda i: (i, 0, 0)),
                  whole_block(single.shape), whole_block(per_block.shape)],
        out_specs=pl.BlockSpec((half, 3 * here, cols), lambda i: (i, 0, 0)),
        compiler_params=params(),
        name="trace",
    )(modes, up1, down1, rims, single, per_block)

    pay = pay.reshape(problems, 3 * here, parts, width).transpose(0, 2, 1, 3)
    pay = pay.reshape(devices, 3 * here, width)
    pay = lax.all_to_all(pay, EVERY, split_axis=0, concat_axis=0, tiled=True)
    pay = pay.reshape(devices, 3, here, width).transpose(1, 0, 2, 3).reshape(3, devices * here, width)
    total = devices * here

    flux = pl.pallas_call(
        functools.partial(ring_kernel, here=here, levels=levels),
        out_shape=shape(total, width),
        compiler_params=params(),
        name="ring",
    )(pay[0], pay[1], pay[2], jnp.asarray(mix), jnp.asarray(mix.T.copy()), inverse, extra)

    flux = jnp.stack([flux, jnp.roll(flux, levels, axis=0)])
    flux = flux.reshape(2, devices, here, width).transpose(1, 0, 2, 3).reshape(devices, 2 * here, width)
    flux = lax.all_to_all(flux, EVERY, split_axis=0, concat_axis=0, tiled=True)
    flux = flux.reshape(problems, parts, 2 * here, width).transpose(0, 2, 1, 3)
    flux = flux.reshape(problems, 2 * here, cols)

    up2, down2 = pl.pallas_call(
        functools.partial(flux_kernel, here=here),
        out_shape=(shape(*plane), shape(*plane)),
        compiler_params=params(),
        name="flux",
    )(flux, per_block)
    up2, down2 = carry(up2, down2, 1)

    once = lambda s: pl.BlockSpec(s, lambda t: (0,) * len(s), pipeline_mode=pl.Buffered(1))
    out_shape = shape(*multiplier.shape)
    level_block = pl.BlockSpec((3, 1, problems, rows, cols), lambda t: (0, t, 0, 0, 0))
    return pl.pallas_call(
        functools.partial(project_kernel, levels=levels, here=here),
        out_shape=(out_shape, out_shape),
        grid=(here,),
        in_specs=[once((here + 1, *plane)), once(flux.shape), once(rims.shape), once(plane),
                  once(plane), once(plane), once(plane), once(col_table.shape),
                  once(row_back.shape), once(single.shape), once(per_block.shape), level_block],
        out_specs=(level_block, level_block),
        scratch_shapes=[pltpu.VMEM((here + 1, *plane), f32), pltpu.VMEM(plane, f32),
                        pltpu.VMEM(plane, f32), pltpu.VMEM((problems, held, cols), f32)],
        compiler_params=params(),
        name="project",
    )(modes, flux, rims, up1, down1, up2, down2, col_table, row_back, single, per_block, multiplier)


def solution(mesh):
    placed = (
        P(None, "py", None, ("grp", "px"), None),
        P(None, "py", None, ("grp", "px"), None),
        P(None, ("grp", "px"), None),
        P(None, ("grp", "px"), None),
    )
    return jax.shard_map(
        local,
        mesh=mesh,
        in_specs=placed,
        out_specs=(
            P(None, "py", None, ("grp", "px"), None),
            P(None, "py", None, ("grp", "px"), None),
        ),
        check_vma=False,
    )
```

```python
import functools
import math

import jax
import jax.numpy as jnp
import ml_dtypes
import numpy as np
from jax import lax
from jax.experimental import pallas as pl
from jax.experimental.pallas import tpu as pltpu
from jax.sharding import PartitionSpec as P

NEWTON = 4
PENALTY = 1.0
VMEM_LIMIT = 60 * 1024 * 1024
SPACE = ("grp", "px")
EVERY = ("grp", "px", "py")
MESH = pl.DeviceIdType.MESH
bf16 = jnp.bfloat16
f32 = jnp.float32


def halves(table):
    high = table.astype(ml_dtypes.bfloat16)
    low = (table - high.astype(np.float64)).astype(ml_dtypes.bfloat16)
    return np.stack([high, low])


def hartley(length):
    angles = 2.0 * np.pi / length * (np.outer(np.arange(length), np.arange(length)) % length)
    return (np.cos(angles) + np.sin(angles)) / np.sqrt(length)


def cosines(length):
    k = np.arange(length)[:, None]
    x = np.arange(length)[None, :]
    weights = np.where(k == 0, np.sqrt(1.0 / length), np.sqrt(2.0 / length))
    return weights * np.cos(np.pi * k * (2 * x + 1) / (2 * length))


def slab_tables(rows, cols, here, blocks):
    j = np.arange(rows)[:, None]
    n = np.arange(cols)[None, :]
    lam = 4.0 * np.sin(np.pi * j / (2 * rows)) ** 2 + 4.0 * np.sin(np.pi * n / cols) ** 2
    sinh = np.sqrt(lam * (1.0 + 0.25 * lam))
    ratio = 1.0 / (1.0 + 0.5 * lam + sinh)
    positive = lam > 0.0
    full = ratio ** (2 * here * blocks)
    scale = np.where(positive, 0.5 / np.where(positive, sinh * (1.0 - full), 1.0), 0.0)
    edge = cosines(rows)[:, :1]
    low, high, down, low_q, high_q = [], [], [], [], []
    for block in range(blocks):
        first = block * here
        lows = [1.0 + ratio ** (2 * (first + v) + 1) for v in range(here + 1)]
        highs = [1.0 + ratio ** (2.0 * (blocks * here - 1 - first - v) + 1.0) for v in range(here + 1)]
        low.append(lows)
        high.append(highs)
        down.append([ratio**v * highs[v] for v in range(here + 1)])
        low_q.append([edge * ratio ** (here - v) * lows[v] for v in range(here)])
        high_q.append([edge * ratio**v * highs[v] for v in range(here)])
    single = np.stack([ratio, ratio**here, scale, edge * scale, np.broadcast_to(edge, lam.shape)])
    pack = lambda parts: np.asarray(parts, np.float32)
    ahead = np.concatenate([pack(low), pack(high), pack(down)], axis=1)
    after = np.concatenate([pack(low), pack(high), pack(low_q), pack(high_q)], axis=1)
    return single.astype(np.float32), ahead, after


def ring_tables(rows, cols, group, levels):
    r = np.arange(group)[:, None, None]
    k = np.arange(levels)[None, :, None]
    n = np.arange(cols)[None, None, :]
    tau = 4.0 * np.sin(np.pi * k / (2 * levels)) ** 2
    kappa = tau + 4.0 * np.sin(np.pi * n / cols) ** 2
    turn = 2.0 * np.sin(np.pi * r / group) ** 2
    positive = kappa > 0.0
    safe = np.where(positive, kappa, 1.0)
    shrink = 1.0 / (1.0 + 0.5 * safe + np.sqrt(safe * (1.0 + 0.25 * safe)))
    far = shrink**rows
    inverse = (1.0 - shrink) * (1.0 - far * far) / (
        (1.0 + shrink) * ((1.0 - far) ** 2 + 2.0 * far * turn)
    )
    inverse = np.where(positive, inverse, np.where(r == 0, 1.0 / rows, 0.0))
    edge = math.sqrt(1.0 / rows)
    flat = inverse[:, :, :1]
    moving = edge * flat / np.where(tau > 0.0, tau, 1.0)
    still = rows * edge / np.where(r > 0, 2.0 * turn, 1.0) * (r > 0)
    extra = np.where(tau > 0.0, moving, still)
    mix = np.kron(hartley(group), cosines(levels))
    flat_rows = group * levels
    return (
        mix.astype(np.float32),
        inverse.reshape(flat_rows, cols).astype(np.float32),
        extra.reshape(flat_rows, 1).astype(np.float32),
    )


def split(x):
    high = x.astype(bf16)
    return high, (x - high.astype(f32)).astype(bf16)


def mm(a, b):
    return jnp.dot(a, b, preferred_element_type=f32)


def times_table(x, table):
    high, low = split(x)
    return mm(high, table[0]) + (mm(low, table[0]) + mm(high, table[1]))


def table_times(table, x):
    high, low = split(x)
    return mm(table[0], high) + (mm(table[0], low) + mm(table[1], high))


def precise(a, b):
    return jnp.dot(a, b, precision=lax.Precision.HIGHEST, preferred_element_type=f32)


def over_rows(table, x):
    units, rows, cols = x.shape
    size = table.shape[1]
    bunch = size // rows
    parts = []
    for g in range(units // bunch):
        part = x[g * bunch : (g + 1) * bunch].reshape(size, cols)
        parts.append(table_times(table, part).reshape(bunch, rows, cols))
    return parts[0] if len(parts) == 1 else jnp.concatenate(parts, axis=0)


def steps_from(me, blocks):
    return me, blocks - 1 - me


class Chain:
    def __init__(self, up, down, step, size, blocks):
        self.me = lax.axis_index("py")
        self.blocks, self.size, self.step = blocks, size, step
        self.far = steps_from(self.me, blocks)
        self.next = ((self.me + 1) % blocks, (self.me + blocks - 1) % blocks)
        self.refs = (up, down)

    def copy(self, way, source, k):
        _, got, _, sent, came = self.refs[way]
        cut = pl.ds(k * self.size, self.size)
        return pltpu.make_async_remote_copy(
            src_ref=source.at[cut],
            dst_ref=got.at[cut],
            send_sem=sent.at[k],
            recv_sem=came.at[k],
            device_id={"py": self.next[way]},
            device_id_type=MESH,
        )

    def greet(self):
        barrier = pltpu.get_barrier_semaphore()
        lower, upper = self.me > 0, self.me < self.blocks - 1

        @pl.when(lower)
        def _():
            pl.semaphore_signal(barrier, inc=1, device_id={"py": self.me - 1}, device_id_type=MESH)

        @pl.when(upper)
        def _():
            pl.semaphore_signal(barrier, inc=1, device_id={"py": self.me + 1}, device_id_type=MESH)

        @pl.when(lower & upper)
        def _():
            pl.semaphore_wait(barrier, 2)

        @pl.when(jnp.logical_not(lower & upper))
        def _():
            pl.semaphore_wait(barrier, 1)

    def clear(self):
        for way in range(2):
            got = self.refs[way][1]

            @pl.when(self.far[way] == 0)
            def _():
                got[...] = jnp.zeros_like(got)

    def begin(self, k):
        for way in range(2):

            @pl.when(self.far[way] == 0)
            def _():
                self.copy(way, self.refs[way][0], k).start()

    def relay(self, way, k, low, high):
        own, got, out, _, _ = self.refs[way]

        @pl.when((self.far[way] > 0) & (k >= low) & (k < high))
        def _():
            self.copy(way, out, k).wait_recv()

            @pl.when(self.far[way] < self.blocks - 1)
            def _():
                for q in range(self.size):
                    at = k * self.size + q
                    out[at] = own[at] + self.step[...] * got[at]
                self.copy(way, out, k).start()

    def finish(self, pieces):
        for way in range(2):

            @pl.when(self.far[way] < self.blocks - 1)
            def _():
                def one(k, carry):
                    self.copy(way, self.refs[way][2], k).wait_send()
                    return carry

                lax.fori_loop(0, pieces, one, 0)


def trace_problem(b, modes, up, down, rims, single, tables, pay, *, here):
    rows, cols = up.shape[1], up.shape[2]
    width = pay.shape[3]
    parts = cols // width
    lane = lax.broadcasted_iota(jnp.int32, (1, cols), 1)
    parity = lax.broadcasted_iota(jnp.int32, (8, cols), 0) % 2 == 0
    total = [jnp.zeros((8, cols), f32) for _ in range(here)]
    for c in range(rows // 8):
        cut = slice(c * 8, c * 8 + 8)
        ratio, weight = single[0, cut, :], single[3, cut, :]
        value = up[b, cut, :]
        sums = []
        for v in range(here):
            if v:
                value = ratio * value
            value = value + tables[v, cut, :] * modes[v, b, cut, :]
            sums.append(tables[here + 1 + v, cut, :] * value)
        behind = down[b, cut, :]
        for v in range(here, -1, -1):
            if v < here:
                total[v] = total[v] + weight * (sums[v] + tables[v, cut, :] * behind)
            behind = ratio * (behind + tables[here + 1 + v, cut, :] * modes[v, b, cut, :])

    def put(kind, v, row):
        for n in range(parts):
            pay[b * parts + n, kind, v : v + 1, :] = row[:, n * width : (n + 1) * width]

    for v in range(here):
        even = jnp.sum(jnp.where(parity, total[v], 0.0), axis=0, keepdims=True)
        odd = jnp.sum(jnp.where(parity, 0.0, total[v]), axis=0, keepdims=True)
        put(0, v, even + odd)
        put(1, v, even - odd + rims[b, v : v + 1, :])
        flat = jnp.where(lane == 0, modes[v, b, 0:1, :], 0.0)
        if v == 0:
            beyond = pltpu.roll(modes[here, b, 0:8, :], 1, 1)[0:1]
            flat = flat + jnp.where(lane == 1, beyond, 0.0)
        put(2, v, flat)


def source_kernel(
    mult, aux, start, end, col_table, row_table, single, tables_all,
    modes_out, up_all, down_all, rims, pay,
    modes, prev, body, tail, tables, up_own, down_own, up_got, down_got, up_out, down_out,
    up_sent, up_came, down_sent, down_came, moved, table_sem,
    *, levels, here, blocks, chunks, pieces, delay
):
    chunk_index, t = pl.program_id(0), pl.program_id(1)
    chunk, rows, cols = body.shape
    steps = here + 1
    g = chunk_index * steps + t
    me = lax.axis_index("py")
    level = me * here + t
    base = chunk_index * chunk
    size = chunk // pieces
    row = lax.broadcasted_iota(jnp.int32, (rows, cols), 0)
    chain = Chain(
        (up_own, up_got, up_out, up_sent, up_came),
        (down_own, down_got, down_out, down_sent, down_came),
        single.at[1], size, blocks,
    )
    fetch = pltpu.make_async_copy(tables_all.at[me], tables, table_sem)

    @pl.when(g == 0)
    def _():
        fetch.start()
        chain.clear()
        chain.greet()

    @pl.when(t == 0)
    def _():
        prev[...] = jnp.zeros_like(prev)
        tail[...] = jnp.zeros_like(tail)
        up_own[pl.ds(base, chunk)] = jnp.zeros((chunk, rows, cols), f32)
        down_own[pl.ds(base, chunk)] = jnp.zeros((chunk, rows, cols), f32)

    @pl.when(t < here)
    def _():
        keep = jnp.where(level == levels - 1, 0.0, 1.0)
        begin = jnp.where(level == 0, -1.0 / PENALTY, 0.0)
        finish = jnp.where(level == levels - 1, 1.0 / PENALTY, 0.0)

        def one(b, carry):
            along = aux[1, 0, b] - mult[1, 0, b] / PENALTY
            tail[b, pl.ds(t, 1), :] = along[rows - 1 :, :]
            beside = jnp.where(row == 0, 0.0, pltpu.roll(along, 1, 0))
            along = jnp.where(row == rows - 1, 0.0, along)
            second = aux[2, 0, b] - mult[2, 0, b] / PENALTY
            across = pltpu.roll(second, 1, 1) - second
            now = (aux[0, 0, b] - mult[0, 0, b] / PENALTY) * keep
            boundary = begin * start[b] + finish * end[b]
            body[b] = prev[b] - now + beside - along + across + boundary
            prev[b] = now
            return carry

        lax.fori_loop(0, chunk, one, 0, unroll=4)

    @pl.when(t == here)
    def _():
        body[...] = prev[...]
        held = tail.shape[1]
        flat = tail[...].reshape(chunk * held, cols)
        rims[pl.ds(base, chunk)] = times_table(flat, col_table).reshape(chunk, held, cols)

    spread = times_table(body[...].reshape(chunk * rows, cols), col_table)
    modes[t, pl.ds(base, chunk)] = over_rows(row_table, spread.reshape(chunk, rows, cols))

    @pl.when(g == 0)
    def _():
        fetch.wait()

    ratio = single[0]
    low = tables[t]
    falling = tables[2 * steps + t]

    def add(b, carry):
        value = modes[t, b]
        up_own[b] = ratio * up_own[b] + low * value
        down_own[b] = down_own[b] + falling * value
        return carry

    lax.fori_loop(base, base + chunk, add, 0)

    def relays(at, owner):
        for way in range(2):
            k = at - ((owner + 1) * steps - 1) - delay * chain.far[way]
            chain.relay(way, k + owner * pieces, owner * pieces, (owner + 1) * pieces)

    for owner in range(chunks - 1):
        relays(g, owner)

    def move(c):
        cut = pl.ds(c * chunk, chunk)
        return pltpu.make_async_copy(modes.at[:, cut], modes_out.at[:, cut], moved.at[c])

    @pl.when(t == here)
    def _():
        move(chunk_index).start()

        def one(k, carry):
            chain.begin(chunk_index * pieces + k)
            return carry

        lax.fori_loop(0, pieces, one, 0)

    @pl.when(g == chunks * steps - 1)
    def _():
        final = chunks * steps - 1
        reach = delay * (blocks - 1)
        open_at = [max(1, (owner + 1) * steps - 1 + reach - final) for owner in range(chunks)]

        def slot(i, carry):
            for owner in range(chunks):
                if (owner + 1) * steps - 1 + reach + pieces - 1 > final:
                    relays(final + i, owner)
            for owner in range(chunks):
                k = i - open_at[owner]

                @pl.when((k >= 0) & (k < pieces))
                def _():
                    def one(q, carry):
                        trace_problem(
                            (owner * pieces + k) * size + q, modes, up_got, down_got, rims,
                            single, tables, pay, here=here,
                        )
                        return carry

                    lax.fori_loop(0, size, one, 0)

            return carry

        lax.fori_loop(1, max(open_at) + pieces, slot, 0)
        ups = pltpu.make_async_copy(up_got, up_all, moved.at[chunks])
        downs = pltpu.make_async_copy(down_got, down_all, moved.at[chunks + 1])
        ups.start()
        downs.start()
        chain.finish(chunks * pieces)
        ups.wait()
        downs.wait()
        for c in range(chunks):
            move(c).wait()


def sweep_problem(b, modes, flux, up1, up2, down1, down2, single, tables, wave, *, here, levels):
    rows, cols = up1.shape[1], up1.shape[2]
    first = lax.axis_index("py") * here
    for c in range(rows // 8):
        cut = slice(c * 8, c * 8 + 8)
        ratio, scale, edge = single[0, cut, :], single[2, cut, :], single[4, cut, :]
        sign = jnp.where(
            lax.broadcasted_iota(jnp.int32, (8, cols), 0) % 2 == 0, edge, -edge
        )
        value = up1[b, cut, :] + up2[b, cut, :]
        source, sums = [], []
        for v in range(here + 1):
            now = modes[v, b, cut, :]
            if v < here:
                mine = jnp.broadcast_to(flux[b, v : v + 1, :], (8, cols))
                other = jnp.broadcast_to(flux[b, here + v : here + v + 1, :], (8, cols))
                now = now + (sign * mine - edge * other)
            source.append(now)
            if v:
                value = ratio * value
            value = value + tables[v, cut, :] * now
            sums.append(tables[here + 1 + v, cut, :] * value)
        behind = down1[b, cut, :] + down2[b, cut, :]
        for v in range(here, -1, -1):
            wave[v, b, cut, :] = scale * (sums[v] + tables[v, cut, :] * behind)
            behind = ratio * (behind + tables[here + 1 + v, cut, :] * source[v])
        if c == 0:
            spot = (lax.broadcasted_iota(jnp.int32, (8, 128), 0) == 0) & (
                lax.broadcasted_iota(jnp.int32, (8, 128), 1) == 0
            )
            below = 0.5 * (up1[b, 0:8, 0:128] + up2[b, 0:8, 0:128])
            whole = below + 0.5 * (down1[b, 0:8, 0:128] + down2[b, 0:8, 0:128])
            for v in range(here + 1):
                whole = whole + source[v][:, 0:128]
            mean = whole * (1.0 / levels)
            level_value = jnp.zeros((8, 128), f32)
            for v in range(here + 1):
                wave[v, b, 0:8, 0:128] = jnp.where(spot, level_value, wave[v, b, 0:8, 0:128])
                if v < here:
                    below = below + source[v][:, 0:128]
                    count = (first + (v + 1)).astype(f32)
                    level_value = level_value - (below - count * mean)


def flux_problem(b, flux, tables, up, down, *, here):
    rows, cols = up.shape[1], up.shape[2]
    sign = jnp.where(lax.broadcasted_iota(jnp.int32, (rows, cols), 0) % 2 == 0, 1.0, -1.0)
    base = 2 * (here + 1)
    rise = jnp.zeros((rows, cols), f32)
    fall = jnp.zeros((rows, cols), f32)
    for v in range(here):
        mine = jnp.broadcast_to(flux[b, v : v + 1, :], (rows, cols))
        other = jnp.broadcast_to(flux[b, here + v : here + v + 1, :], (rows, cols))
        both = sign * mine - other
        rise = rise + tables[base + v] * both
        fall = fall + tables[base + here + v] * both
    up[b] = rise
    down[b] = fall


def flat_rows(ref, kind, here):
    devices, width = ref.shape[0], ref.shape[3]
    if here % 8 == 0:
        return ref[:, kind].reshape(devices * here, width)
    return jnp.concatenate([ref[i, kind] for i in range(devices)], axis=0)


def solve_kernel(
    pay, modes_all, up_all, down_all, rims, single, tables_all, mix, mix_back, ring,
    col_table, row_back,
    phi_all, edges,
    recv, back, came, flux, modes, wave, tables, up1, down1,
    up_own, down_own, up_got, down_got, up_out, down_out,
    up_sent, up_came, down_sent, down_came, sent1, came1, sent2, came2, loaded, moved,
    *, levels, here, blocks, group, inner, pieces, delay
):
    problems, rows, cols = up1.shape
    devices, width = pay.shape[0], pay.shape[3]
    parts = cols // width
    size = problems // pieces
    me_py = lax.axis_index("py")
    me = (lax.axis_index("grp") * inner + lax.axis_index("px")) * blocks + me_py
    chain = Chain(
        (up_own, up_got, up_out, up_sent, up_came),
        (down_own, down_got, down_out, down_sent, down_came),
        single.at[1], size, blocks,
    )

    def place(i):
        other = (me + i) % devices
        where = {
            "grp": other // (inner * blocks),
            "px": other // blocks % inner,
            "py": other % blocks,
        }
        return other, where

    loads = [
        pltpu.make_async_copy(modes_all, modes, loaded.at[0]),
        pltpu.make_async_copy(up_all, up1, loaded.at[1]),
        pltpu.make_async_copy(down_all, down1, loaded.at[2]),
        pltpu.make_async_copy(tables_all.at[me_py], tables, loaded.at[3]),
    ]

    barrier = pltpu.get_barrier_semaphore()

    def hail(i, carry):
        _, where = place(i)
        pl.semaphore_signal(barrier, inc=1, device_id=where, device_id_type=MESH)
        return carry

    lax.fori_loop(1, devices, hail, 0)
    for load in loads:
        load.start()
    chain.clear()
    pl.semaphore_wait(barrier, devices - 1)

    def exchange(source, target, sent, arrived, i):
        other, where = place(i)
        return pltpu.make_async_remote_copy(
            src_ref=source.at[other],
            dst_ref=target.at[me],
            send_sem=sent.at[i],
            recv_sem=arrived.at[i],
            device_id=where,
            device_id_type=MESH,
        )

    def every(action):
        def one(i, carry):
            action(i)
            return carry

        lax.fori_loop(1, devices, one, 0)

    first = lambda i: exchange(pay, recv, sent1, came1, i)
    second = lambda i: exchange(back, came, sent2, came2, i)
    every(lambda i: first(i).start())
    recv[me] = pay[me]
    every(lambda i: first(i).wait_recv())

    total = devices * here
    lane = lax.broadcasted_iota(jnp.int32, (total, width), 1)
    slot_id = me % parts
    jump = pltpu.roll(flat_rows(recv, 0, here), total - levels, 0) - flat_rows(recv, 1, here)
    flat = flat_rows(recv, 2, here)
    beyond = pltpu.roll(pltpu.roll(flat, here, 0), width - 1, 1)
    whole = jnp.where(lane == 0, flat + beyond, 0.0)
    jump_flat = pltpu.roll(whole, total - levels, 0) - whole
    solved = precise(mix[...], jump) * ring[0, slot_id]
    solved = solved + precise(mix[...], jump_flat) * ring[1, slot_id]
    mine = precise(mix_back[...], solved)
    other = pltpu.roll(mine, levels, 0)
    if here % 8 == 0:
        back[:, 0] = mine.reshape(devices, here, width)
        back[:, 1] = other.reshape(devices, here, width)
    else:
        for i in range(devices):
            back[i, 0] = mine[i * here : (i + 1) * here]
            back[i, 1] = other[i * here : (i + 1) * here]
    every(lambda i: second(i).start())
    came[me] = back[me]
    every(lambda i: second(i).wait_recv())
    for i in range(devices):
        b, n = i // parts, i % parts
        for kind in range(2):
            flux[b, kind * here : (kind + 1) * here, n * width : (n + 1) * width] = came[i, kind]
    for load in loads:
        load.wait()

    reach = delay * (blocks - 1)

    def send_out(k):
        cut = pl.ds(k * size, size)
        return pltpu.make_async_copy(
            wave.at[pl.ds(0, here), cut], phi_all.at[pl.ds(0, here), cut], moved.at[k]
        )

    def slot(i, carry):
        @pl.when(i < pieces)
        def _():
            def one(q, carry):
                flux_problem(i * size + q, flux, tables, up_own, down_own, here=here)
                return carry

            lax.fori_loop(0, size, one, 0)
            chain.begin(i)

        for way in range(2):
            chain.relay(way, i - delay * chain.far[way], 0, pieces)

        k = i - reach

        @pl.when(k >= 0)
        def _():
            def one(q, carry):
                sweep_problem(
                    k * size + q, modes, flux, up1, up_got, down1, down_got, single, tables,
                    wave, here=here, levels=levels,
                )
                return carry

            lax.fori_loop(0, size, one, 0)
            cut = pl.ds(k * size, size)
            part = over_rows(row_back, wave[0:here, cut].reshape(here * size, rows, cols))
            part = times_table(part.reshape(here * size * rows, cols), col_table)
            wave[0:here, cut] = part.reshape(here, size, rows, cols)
            send_out(k).start()

        return carry

    lax.fori_loop(0, pieces + reach, slot, 0)
    last = over_rows(row_back, wave[here])
    last = times_table(last.reshape(problems * rows, cols), col_table)
    wave[here] = last.reshape(problems, rows, cols)
    tip = pltpu.make_async_copy(wave.at[here], phi_all.at[here], moved.at[pieces])
    tip.start()
    if here % 8 == 0:
        rim = (flux[:, 0:here, :] + rims[:, 0:here, :]).reshape(problems * here, cols)
        edges[...] = times_table(rim, col_table).reshape(problems, here, cols)
    else:
        for b in range(problems):
            edges[b] = times_table(flux[b, 0:here, :] + rims[b, 0:here, :], col_table)
    chain.finish(pieces)
    every(lambda i: first(i).wait_send())
    every(lambda i: second(i).wait_send())
    for k in range(pieces):
        send_out(k).wait()
    tip.wait()


def project_kernel(phi, following, edges, mult, next_mult, next_aux, *, levels):
    t = pl.program_id(0)
    here = pl.num_programs(0)
    _, problems, rows, cols = phi.shape
    moving = jnp.where(lax.axis_index("py") * here + t == levels - 1, 0.0, 1.0)
    row = lax.broadcasted_iota(jnp.int32, (rows, cols), 0)

    def one(b, carry):
        here_phi = phi[0, b]
        rim = jnp.broadcast_to(edges[b, pl.ds(t, 1), :], (rows, cols))
        grad_time = (following[0, b] - here_phi) * moving
        grad_first = jnp.where(
            row == rows - 1, rim, pltpu.roll(here_phi, rows - 1, 0) - here_phi
        )
        grad_second = pltpu.roll(here_phi, cols - 1, 1) - here_phi
        mult_time, mult_first, mult_second = (mult[k, 0, b] for k in range(3))
        time_part = grad_time + mult_time / PENALTY
        along = grad_first + mult_first / PENALTY
        beside = grad_second + mult_second / PENALTY
        kinetic = 0.5 * (along * along + beside * beside)
        offset_one = 1.0 + time_part
        solid = kinetic > 1e-37
        root = jnp.exp(jnp.log(jnp.where(solid, kinetic, 1.0)) * (1.0 / 3.0))
        scaling = jnp.maximum(offset_one, 1.0) + jnp.where(solid, root, 0.0)
        twice = 2.0 * offset_one
        for newton_step in range(NEWTON):
            above = scaling * scaling * (2.0 * scaling - offset_one) + kinetic
            derivative = scaling * (3.0 * scaling - twice)
            scaling = jnp.maximum(above / derivative, 1.0)
        feasible = time_part + kinetic <= 0.0
        shrink = jnp.where(feasible, 1.0, 1.0 / scaling)
        out_time = jnp.where(feasible, time_part, time_part - (scaling - 1.0))
        out_along = along * shrink
        out_beside = beside * shrink
        next_aux[0, 0, b] = out_time
        next_aux[1, 0, b] = out_along
        next_aux[2, 0, b] = out_beside
        next_mult[0, 0, b] = mult_time + PENALTY * (grad_time - out_time)
        next_mult[1, 0, b] = mult_first + PENALTY * (grad_first - out_along)
        next_mult[2, 0, b] = mult_second + PENALTY * (grad_second - out_beside)
        return carry

    lax.fori_loop(0, problems, one, 0, unroll=2)


def params(which=None):
    if which is None:
        return pltpu.CompilerParams(vmem_limit_bytes=VMEM_LIMIT)
    return pltpu.CompilerParams(
        collective_id=which, has_side_effects=True, vmem_limit_bytes=VMEM_LIMIT
    )


def whole_block(shape):
    return pl.BlockSpec(shape, lambda *_: (0,) * len(shape))


def local(multiplier, auxiliary, density_start, density_end):
    _, here, problems, rows, cols = multiplier.shape
    blocks = lax.axis_size("py")
    inner = lax.axis_size("px")
    group = lax.axis_size("grp") * inner
    devices = group * blocks
    levels = here * blocks
    held = -(-here // 8) * 8
    width = problems * cols // devices
    parts = cols // width
    shape = lambda *s: jax.ShapeDtypeStruct(s, f32)
    vector = lambda *s: pltpu.VMEM(s, f32)
    anywhere = pl.BlockSpec(memory_space=pl.ANY)
    vmem = pl.BlockSpec(memory_space=pltpu.VMEM)
    dma = lambda n: pltpu.SemaphoreType.DMA((n,))
    delay = 2

    chunks = 2
    chunk = problems // chunks
    pieces = math.gcd(chunk, 4)
    bunch = math.gcd(chunk, max(1, 256 // rows))
    col_table = jnp.asarray(halves(hartley(cols)))
    row_table = jnp.asarray(halves(np.kron(np.eye(bunch), cosines(rows))))
    single, ahead, after = slab_tables(rows, cols, here, blocks)
    single, ahead, after = jnp.asarray(single), jnp.asarray(ahead), jnp.asarray(after)

    plane = (problems, rows, cols)
    level_block = pl.BlockSpec(
        (3, 1, chunk, rows, cols), lambda c, t: (0, jnp.minimum(t, here - 1), c, 0, 0)
    )
    density_block = pl.BlockSpec((chunk, rows, cols), lambda c, t: (c, 0, 0))
    modes, up1, down1, rims, pay = pl.pallas_call(
        functools.partial(source_kernel, levels=levels, here=here, blocks=blocks, chunks=chunks,
                          pieces=pieces, delay=delay),
        out_shape=(shape(here + 1, *plane), shape(*plane), shape(*plane),
                   shape(problems, held, cols), shape(devices, 3, here, width)),
        grid=(chunks, here + 1),
        in_specs=[level_block, level_block, density_block, density_block,
                  whole_block(col_table.shape), whole_block(row_table.shape),
                  whole_block(single.shape), anywhere],
        out_specs=(anywhere, anywhere, anywhere, whole_block((problems, held, cols)),
                   whole_block((devices, 3, here, width))),
        scratch_shapes=[vector(here + 1, *plane), vector(chunk, rows, cols),
                        vector(chunk, rows, cols), vector(chunk, held, cols),
                        vector(*ahead.shape[1:])] + [vector(*plane)] * 6
        + [dma(chunks * pieces)] * 4 + [dma(chunks + 2), pltpu.SemaphoreType.DMA],
        compiler_params=params(0),
        name="source",
    )(multiplier, auxiliary, density_start, density_end, col_table, row_table, single, ahead)

    mix, inverse, extra = ring_tables(rows, cols, group, levels)
    total = devices * here
    wide = np.zeros((total, cols), np.float32)
    wide[:, :1] = extra
    ring = np.stack([inverse, wide]).reshape(2, total, parts, width).transpose(0, 2, 1, 3).copy()
    pieces = math.gcd(problems, 8)
    size = problems // pieces
    bunch = math.gcd(math.gcd(size * here, problems), max(1, 256 // rows))
    row_back = jnp.asarray(halves(np.kron(np.eye(bunch), cosines(rows).T)))
    phi, edges = pl.pallas_call(
        functools.partial(solve_kernel, levels=levels, here=here, blocks=blocks, group=group,
                          inner=inner, pieces=pieces, delay=delay),
        out_shape=(shape(here + 1, *plane), shape(problems, here, cols)),
        in_specs=[vmem, anywhere, anywhere, anywhere, vmem, vmem, anywhere, vmem, vmem, vmem,
                  vmem, vmem],
        out_specs=(anywhere, vmem),
        scratch_shapes=[vector(devices, 3, here, width), vector(devices, 2, here, width),
                        vector(devices, 2, here, width), vector(problems, 2 * here, cols),
                        vector(here + 1, *plane), vector(here + 1, *plane),
                        vector(*after.shape[1:])] + [vector(*plane)] * 8
        + [dma(pieces)] * 4 + [dma(devices)] * 4 + [dma(4), dma(pieces + 1)],
        compiler_params=params(1),
        name="solve",
    )(pay, modes, up1, down1, rims, single, after, jnp.asarray(mix), jnp.asarray(mix.T.copy()),
      jnp.asarray(ring), col_table, row_back)

    out_shape = shape(*multiplier.shape)
    level_block = pl.BlockSpec((3, 1, *plane), lambda t: (0, t, 0, 0, 0))
    phi_block = pl.BlockSpec((1, *plane), lambda t: (t, 0, 0, 0))
    next_block = pl.BlockSpec((1, *plane), lambda t: (t + 1, 0, 0, 0))
    return pl.pallas_call(
        functools.partial(project_kernel, levels=levels),
        out_shape=(out_shape, out_shape),
        grid=(here,),
        in_specs=[phi_block, next_block, whole_block(edges.shape), level_block],
        out_specs=(level_block, level_block),
        compiler_params=params(),
        name="project",
    )(phi, phi, edges, multiplier)


def solution(mesh):
    placed = (
        P(None, "py", None, ("grp", "px"), None),
        P(None, "py", None, ("grp", "px"), None),
        P(None, ("grp", "px"), None),
        P(None, ("grp", "px"), None),
    )
    return jax.shard_map(
        local,
        mesh=mesh,
        in_specs=placed,
        out_specs=(
            P(None, "py", None, ("grp", "px"), None),
            P(None, "py", None, ("grp", "px"), None),
        ),
        check_vma=False,
    )
```

```python
import functools
import math
import types

import jax
import jax.numpy as jnp
import ml_dtypes
import numpy as np
from jax import lax
from jax.experimental import pallas as pl
from jax.experimental.pallas import tpu as pltpu
from jax.sharding import PartitionSpec as P

NEWTON = 4
PENALTY = 1.0
VMEM_LIMIT = 60 * 1024 * 1024
SPACE = ("grp", "px")
EVERY = ("grp", "px", "py")
MESH = pl.DeviceIdType.MESH
bf16 = jnp.bfloat16
f32 = jnp.float32


def halves(table):
    high = table.astype(ml_dtypes.bfloat16)
    low = (table - high.astype(np.float64)).astype(ml_dtypes.bfloat16)
    return np.stack([high, low])


def hartley(length):
    angles = 2.0 * np.pi / length * (np.outer(np.arange(length), np.arange(length)) % length)
    return (np.cos(angles) + np.sin(angles)) / np.sqrt(length)


def cosines(length):
    k = np.arange(length)[:, None]
    x = np.arange(length)[None, :]
    weights = np.where(k == 0, np.sqrt(1.0 / length), np.sqrt(2.0 / length))
    return weights * np.cos(np.pi * k * (2 * x + 1) / (2 * length))


def slab_tables(rows, cols, here, blocks):
    j = np.arange(rows)[:, None]
    n = np.arange(cols)[None, :]
    lam = 4.0 * np.sin(np.pi * j / (2 * rows)) ** 2 + 4.0 * np.sin(np.pi * n / cols) ** 2
    sinh = np.sqrt(lam * (1.0 + 0.25 * lam))
    ratio = 1.0 / (1.0 + 0.5 * lam + sinh)
    positive = lam > 0.0
    full = ratio ** (2 * here * blocks)
    scale = np.where(positive, 0.5 / np.where(positive, sinh * (1.0 - full), 1.0), 0.0)
    edge = cosines(rows)[:, :1]
    low, high, down, low_q, high_q = [], [], [], [], []
    for block in range(blocks):
        first = block * here
        lows = [1.0 + ratio ** (2 * (first + v) + 1) for v in range(here + 1)]
        highs = [1.0 + ratio ** (2.0 * (blocks * here - 1 - first - v) + 1.0) for v in range(here + 1)]
        low.append(lows)
        high.append(highs)
        down.append([ratio**v * highs[v] for v in range(here + 1)])
        low_q.append([edge * ratio ** (here - v) * lows[v] for v in range(here)])
        high_q.append([edge * ratio**v * highs[v] for v in range(here)])
    single = np.stack([ratio, ratio**here, scale, edge * scale, np.broadcast_to(edge, lam.shape)])
    pack = lambda parts: np.asarray(parts, np.float32)
    ahead = np.concatenate([pack(low), pack(high), pack(down)], axis=1)
    after = np.concatenate([pack(low), pack(high), pack(low_q), pack(high_q)], axis=1)
    return single.astype(np.float32), ahead, after


def ring_tables(rows, cols, group, levels):
    r = np.arange(group)[:, None, None]
    k = np.arange(levels)[None, :, None]
    n = np.arange(cols)[None, None, :]
    tau = 4.0 * np.sin(np.pi * k / (2 * levels)) ** 2
    kappa = tau + 4.0 * np.sin(np.pi * n / cols) ** 2
    turn = 2.0 * np.sin(np.pi * r / group) ** 2
    positive = kappa > 0.0
    safe = np.where(positive, kappa, 1.0)
    shrink = 1.0 / (1.0 + 0.5 * safe + np.sqrt(safe * (1.0 + 0.25 * safe)))
    far = shrink**rows
    inverse = (1.0 - shrink) * (1.0 - far * far) / (
        (1.0 + shrink) * ((1.0 - far) ** 2 + 2.0 * far * turn)
    )
    inverse = np.where(positive, inverse, np.where(r == 0, 1.0 / rows, 0.0))
    edge = math.sqrt(1.0 / rows)
    flat = inverse[:, :, :1]
    moving = edge * flat / np.where(tau > 0.0, tau, 1.0)
    still = rows * edge / np.where(r > 0, 2.0 * turn, 1.0) * (r > 0)
    extra = np.where(tau > 0.0, moving, still)
    mix = np.kron(hartley(group), cosines(levels))
    flat_rows = group * levels
    return (
        mix.astype(np.float32),
        inverse.reshape(flat_rows, cols).astype(np.float32),
        extra.reshape(flat_rows, 1).astype(np.float32),
    )


def split(x):
    high = x.astype(bf16)
    return high, (x - high.astype(f32)).astype(bf16)


def mm(a, b):
    return jnp.dot(a, b, preferred_element_type=f32)


def times_table(x, table):
    high, low = split(x)
    return mm(high, table[0]) + (mm(low, table[0]) + mm(high, table[1]))


def table_times(table, x):
    high, low = split(x)
    return mm(table[0], high) + (mm(table[0], low) + mm(table[1], high))


def precise(a, b):
    return jnp.dot(a, b, precision=lax.Precision.HIGHEST, preferred_element_type=f32)


def over_rows(table, x):
    units, rows, cols = x.shape
    size = table.shape[1]
    bunch = size // rows
    parts = []
    for g in range(units // bunch):
        part = x[g * bunch : (g + 1) * bunch].reshape(size, cols)
        parts.append(table_times(table, part).reshape(bunch, rows, cols))
    return parts[0] if len(parts) == 1 else jnp.concatenate(parts, axis=0)


def steps_from(me, blocks):
    return me, blocks - 1 - me


class Chain:
    def __init__(self, up, down, step, size, blocks):
        self.me = lax.axis_index("py")
        self.blocks, self.size, self.step = blocks, size, step
        self.far = steps_from(self.me, blocks)
        self.next = ((self.me + 1) % blocks, (self.me + blocks - 1) % blocks)
        self.refs = (up, down)

    def copy(self, way, source, k):
        _, got, _, sent, came = self.refs[way]
        cut = pl.ds(k * self.size, self.size)
        return pltpu.make_async_remote_copy(
            src_ref=source.at[cut],
            dst_ref=got.at[cut],
            send_sem=sent.at[k],
            recv_sem=came.at[k],
            device_id={"py": self.next[way]},
            device_id_type=MESH,
        )

    def greet(self):
        barrier = pltpu.get_barrier_semaphore()
        lower, upper = self.me > 0, self.me < self.blocks - 1

        @pl.when(lower)
        def _():
            pl.semaphore_signal(barrier, inc=1, device_id={"py": self.me - 1}, device_id_type=MESH)

        @pl.when(upper)
        def _():
            pl.semaphore_signal(barrier, inc=1, device_id={"py": self.me + 1}, device_id_type=MESH)

        @pl.when(lower & upper)
        def _():
            pl.semaphore_wait(barrier, 2)

        @pl.when(jnp.logical_not(lower & upper))
        def _():
            pl.semaphore_wait(barrier, 1)

    def clear(self):
        for way in range(2):
            got = self.refs[way][1]

            @pl.when(self.far[way] == 0)
            def _():
                got[...] = jnp.zeros_like(got)

    def begin(self, k):
        for way in range(2):

            @pl.when(self.far[way] == 0)
            def _():
                self.copy(way, self.refs[way][0], k).start()

    def relay(self, way, k, low, high):
        own, got, out, _, _ = self.refs[way]

        @pl.when((self.far[way] > 0) & (k >= low) & (k < high))
        def _():
            self.copy(way, out, k).wait_recv()

            @pl.when(self.far[way] < self.blocks - 1)
            def _():
                for q in range(self.size):
                    at = k * self.size + q
                    out[at] = own[at] + self.step[...] * got[at]
                self.copy(way, out, k).start()

    def finish(self, pieces):
        for way in range(2):

            @pl.when(self.far[way] < self.blocks - 1)
            def _():
                def one(k, carry):
                    self.copy(way, self.refs[way][2], k).wait_send()
                    return carry

                lax.fori_loop(0, pieces, one, 0)


def trace_problem(b, modes, up, down, rims, single, tables, pay, *, here):
    rows, cols = up.shape[1], up.shape[2]
    width = pay.shape[3]
    parts = cols // width
    lane = lax.broadcasted_iota(jnp.int32, (1, cols), 1)
    parity = lax.broadcasted_iota(jnp.int32, (8, cols), 0) % 2 == 0
    total = [jnp.zeros((8, cols), f32) for _ in range(here)]
    for c in range(rows // 8):
        cut = slice(c * 8, c * 8 + 8)
        ratio, weight = single[0, cut, :], single[3, cut, :]
        value = up[b, cut, :]
        sums = []
        for v in range(here):
            if v:
                value = ratio * value
            value = value + tables[v, cut, :] * modes[v, b, cut, :]
            sums.append(tables[here + 1 + v, cut, :] * value)
        behind = down[b, cut, :]
        for v in range(here, -1, -1):
            if v < here:
                total[v] = total[v] + weight * (sums[v] + tables[v, cut, :] * behind)
            behind = ratio * (behind + tables[here + 1 + v, cut, :] * modes[v, b, cut, :])

    def put(kind, v, row):
        for n in range(parts):
            pay[b * parts + n, kind, v : v + 1, :] = row[:, n * width : (n + 1) * width]

    for v in range(here):
        even = jnp.sum(jnp.where(parity, total[v], 0.0), axis=0, keepdims=True)
        odd = jnp.sum(jnp.where(parity, 0.0, total[v]), axis=0, keepdims=True)
        put(0, v, even + odd)
        put(1, v, even - odd + rims[b, v : v + 1, :])
        flat = jnp.where(lane == 0, modes[v, b, 0:1, :], 0.0)
        if v == 0:
            beyond = pltpu.roll(modes[here, b, 0:8, :], 1, 1)[0:1]
            flat = flat + jnp.where(lane == 1, beyond, 0.0)
        put(2, v, flat)


def sweep_problem(b, modes, flux, up1, up2, down1, down2, single, tables, wave, *, here, levels):
    rows, cols = up1.shape[1], up1.shape[2]
    first = lax.axis_index("py") * here
    for c in range(rows // 8):
        cut = slice(c * 8, c * 8 + 8)
        ratio, scale, edge = single[0, cut, :], single[2, cut, :], single[4, cut, :]
        sign = jnp.where(
            lax.broadcasted_iota(jnp.int32, (8, cols), 0) % 2 == 0, edge, -edge
        )
        value = up1[b, cut, :] + up2[b, cut, :]
        source, sums = [], []
        for v in range(here + 1):
            now = modes[v, b, cut, :]
            if v < here:
                mine = jnp.broadcast_to(flux[b, v : v + 1, :], (8, cols))
                other = jnp.broadcast_to(flux[b, here + v : here + v + 1, :], (8, cols))
                now = now + (sign * mine - edge * other)
            source.append(now)
            if v:
                value = ratio * value
            value = value + tables[v, cut, :] * now
            sums.append(tables[here + 1 + v, cut, :] * value)
        behind = down1[b, cut, :] + down2[b, cut, :]
        for v in range(here, -1, -1):
            wave[v, b, cut, :] = scale * (sums[v] + tables[v, cut, :] * behind)
            behind = ratio * (behind + tables[here + 1 + v, cut, :] * source[v])
        if c == 0:
            spot = (lax.broadcasted_iota(jnp.int32, (8, 128), 0) == 0) & (
                lax.broadcasted_iota(jnp.int32, (8, 128), 1) == 0
            )
            below = 0.5 * (up1[b, 0:8, 0:128] + up2[b, 0:8, 0:128])
            whole = below + 0.5 * (down1[b, 0:8, 0:128] + down2[b, 0:8, 0:128])
            for v in range(here + 1):
                whole = whole + source[v][:, 0:128]
            mean = whole * (1.0 / levels)
            level_value = jnp.zeros((8, 128), f32)
            for v in range(here + 1):
                wave[v, b, 0:8, 0:128] = jnp.where(spot, level_value, wave[v, b, 0:8, 0:128])
                if v < here:
                    below = below + source[v][:, 0:128]
                    count = (first + (v + 1)).astype(f32)
                    level_value = level_value - (below - count * mean)


def flux_problem(b, flux, tables, up, down, *, here):
    rows, cols = up.shape[1], up.shape[2]
    sign = jnp.where(lax.broadcasted_iota(jnp.int32, (rows, cols), 0) % 2 == 0, 1.0, -1.0)
    base = 2 * (here + 1)
    rise = jnp.zeros((rows, cols), f32)
    fall = jnp.zeros((rows, cols), f32)
    for v in range(here):
        mine = jnp.broadcast_to(flux[b, v : v + 1, :], (rows, cols))
        other = jnp.broadcast_to(flux[b, here + v : here + v + 1, :], (rows, cols))
        both = sign * mine - other
        rise = rise + tables[base + v] * both
        fall = fall + tables[base + here + v] * both
    up[b] = rise
    down[b] = fall


def flat_rows(ref, kind, here):
    devices, width = ref.shape[0], ref.shape[3]
    if here % 8 == 0:
        return ref[:, kind].reshape(devices * here, width)
    return jnp.concatenate([ref[i, kind] for i in range(devices)], axis=0)


SCRATCH = (
    "mult", "aux", "start", "end", "col", "row", "home", "single", "ahead", "after", "mix",
    "mix_back", "ring",
    "prev", "body", "tail", "rims", "modes", "pay", "recv", "back", "came", "flux",
    "own_up1", "own_down1", "got_up1", "got_down1", "out_up1", "out_down1",
    "own_up2", "own_down2", "got_up2", "got_down2", "out_up2", "out_down2",
    "streamed", "fetched", "moved",
    "sent_up1", "sent_down1", "came_up1", "came_down1",
    "sent_up2", "sent_down2", "came_up2", "came_down2",
    "sent1", "came1", "sent2", "came2",
)


def loop(low, high, action, unroll=1):
    def one(i, carry):
        action(i)
        return carry

    if not (isinstance(low, int) and isinstance(high, int) and high <= low):
        lax.fori_loop(low, high, one, 0, unroll=unroll)


def solve_kernel(
    mult_all, aux_all, start_all, end_all, col_all, row_all, home_all, single_all, ahead_all,
    after_all, mix_all, mix_back_all, ring_all, phi_all, edges, *scratch,
    levels, here, blocks, inner, pieces, delay, depth
):
    s = types.SimpleNamespace(**dict(zip(SCRATCH, scratch)))
    problems, rows, cols = s.start.shape
    devices, width = s.pay.shape[0], s.pay.shape[3]
    chunk, per, half = problems // 2, pieces // 2, devices // 2
    size = problems // pieces
    parts = cols // width
    reach = delay * (blocks - 1)
    me_py = lax.axis_index("py")
    me_space = lax.axis_index("grp") * inner + lax.axis_index("px")
    me = me_space * blocks + me_py
    my_half = me_space % 2
    my_chunk = my_half * half + (me_space // 2) * blocks + me_py
    tables, after = s.ahead, s.after

    def where(flat):
        return {
            "grp": flat // (inner * blocks),
            "px": flat // blocks % inner,
            "py": flat % blocks,
        }

    def solver(c):
        i = c % half
        return (2 * (i // blocks) + c // half) * blocks + i % blocks

    def chain(n):
        part = lambda name: getattr(s, name % n)
        return Chain(
            *((part("own_%s%%d" % way), part("got_%s%%d" % way), part("out_%s%%d" % way),
               part("sent_%s%%d" % way), part("came_%s%%d" % way)) for way in ("up", "down")),
            s.single.at[1], size, blocks,
        )

    chain1, chain2 = chain(1), chain(2)

    def relays(which, i, owner):
        for way in range(2):
            k = i - delay * which.far[way]
            which.relay(way, owner * per + k, owner * per, (owner + 1) * per)

    def stream(g):
        c, t, at = g // here, g % here, g % depth
        cut = pl.ds(c * chunk, chunk)
        return [
            pltpu.make_async_copy(mult_all.at[:, t, cut], s.mult.at[at], s.streamed.at[0, at]),
            pltpu.make_async_copy(aux_all.at[:, t, cut], s.aux.at[at], s.streamed.at[1, at]),
        ]

    pairs = [
        (start_all, s.start), (end_all, s.end), (col_all, s.col), (row_all, s.row),
        (single_all, s.single), (ahead_all.at[me_py], s.ahead), (after_all.at[me_py], s.after),
        (mix_all, s.mix), (mix_back_all, s.mix_back), (ring_all.at[:, my_chunk % parts], s.ring),
        (home_all, s.home),
    ]
    fetches = [pltpu.make_async_copy(x, y, s.fetched.at[i]) for i, (x, y) in enumerate(pairs)]
    early = 6
    for g in range(min(depth, 2 * here)):
        for copy in stream(g):
            copy.start()
        if g == 0:
            for fetch in fetches[:early]:
                fetch.start()
    for fetch in fetches[early:]:
        fetch.start()
    barrier = pltpu.get_barrier_semaphore()

    def hail(i):
        pl.semaphore_signal(
            barrier, inc=1, device_id=where((me + i) % devices), device_id_type=MESH
        )

    loop(1, devices, hail)
    chain1.clear()
    chain2.clear()
    for fetch in fetches[:early]:
        fetch.wait()
    row = lax.broadcasted_iota(jnp.int32, (rows, cols), 0)

    def transform(c, t):
        base = c * chunk
        spread = times_table(s.body[...].reshape(chunk * rows, cols), s.col)
        s.modes[t, base : base + chunk] = over_rows(s.row, spread.reshape(chunk, rows, cols))
        ratio, low, falling = s.single[0], tables[t], tables[2 * (here + 1) + t]

        def add(b):
            value = s.modes[t, b]
            s.own_up1[b] = ratio * s.own_up1[b] + low * value
            s.own_down1[b] = s.own_down1[b] + falling * value

        loop(base, base + chunk, add, unroll=4)

    def source(c, t):
        g = c * here + t
        at = g % depth
        level = me_py * here + t
        for copy in stream(g):
            copy.wait()
        keep = jnp.where(level == levels - 1, 0.0, 1.0)
        begin = jnp.where(level == 0, -1.0 / PENALTY, 0.0)
        finish = jnp.where(level == levels - 1, 1.0 / PENALTY, 0.0)

        def one(b):
            along = s.aux[at, 1, b] - s.mult[at, 1, b] / PENALTY
            s.tail[b, pl.ds(t, 1), :] = along[rows - 1 :, :]
            beside = jnp.where(row == 0, 0.0, pltpu.roll(along, 1, 0))
            along = jnp.where(row == rows - 1, 0.0, along)
            second = s.aux[at, 2, b] - s.mult[at, 2, b] / PENALTY
            across = pltpu.roll(second, 1, 1) - second
            now = (s.aux[at, 0, b] - s.mult[at, 0, b] / PENALTY) * keep
            boundary = begin * s.start[c * chunk + b] + finish * s.end[c * chunk + b]
            s.body[b] = s.prev[b] - now + beside - along + across + boundary
            s.prev[b] = now

        loop(0, chunk, one, unroll=4)

        @pl.when(g + depth < 2 * here)
        def _():
            for copy in stream(g + depth):
                copy.start()

        transform(c, t)
        if c == 1:
            relays(chain1, t + 1, 0)

    for c in range(2):
        cut = slice(c * chunk, c * chunk + chunk)
        s.prev[...] = jnp.zeros_like(s.prev)
        s.tail[...] = jnp.zeros_like(s.tail)
        s.own_up1[cut] = jnp.zeros((chunk, rows, cols), f32)
        s.own_down1[cut] = jnp.zeros((chunk, rows, cols), f32)
        loop(0, here, functools.partial(source, c))
        s.body[...] = s.prev[...]
        transform(c, here)
        held = s.tail.shape[1]
        if c == 0:
            pl.semaphore_wait(barrier, devices - 1)
        loop(c * per, (c + 1) * per, chain1.begin)
        if c == 1:
            relays(chain1, here + 1, 0)
        flat = s.tail[...].reshape(chunk * held, cols)
        s.rims[cut] = times_table(flat, s.col).reshape(chunk, held, cols)

    def ask(c):
        other = solver(c)

        @pl.when(other == me)
        def _():
            s.recv[me] = s.pay[c]

        @pl.when(other != me)
        def _():
            pltpu.make_async_remote_copy(
                src_ref=s.pay.at[c], dst_ref=s.recv.at[me], send_sem=s.sent1.at[c],
                recv_sem=s.came1.at[me], device_id=where(other), device_id_type=MESH,
            ).start()

    def trace(k):
        def one(b):
            trace_problem(
                b, s.modes, s.got_up1, s.got_down1, s.rims, s.single, tables, s.pay, here=here
            )
            for n in range(parts):
                ask(b * parts + n)

        loop(k * size, k * size + size, one)

    def answer(i):
        other = (me + i) % devices
        return pltpu.make_async_remote_copy(
            src_ref=s.back.at[other], dst_ref=s.came.at[my_chunk], send_sem=s.sent2.at[i],
            recv_sem=s.came2.at[my_chunk], device_id=where(other), device_id_type=MESH,
        )

    def solve_ring(h):
        @pl.when(my_half == h)
        def _():
            def arrive(i):
                other = (me + i) % devices
                pltpu.make_async_remote_copy(
                    src_ref=s.pay.at[0], dst_ref=s.recv.at[other], send_sem=s.sent1.at[0],
                    recv_sem=s.came1.at[other], device_id=where(other), device_id_type=MESH,
                ).wait_recv()

            loop(1, devices, arrive)
            total = devices * here
            lane = lax.broadcasted_iota(jnp.int32, (total, width), 1)
            ahead = total - levels
            jump = pltpu.roll(flat_rows(s.recv, 0, here), ahead, 0) - flat_rows(s.recv, 1, here)
            flat = flat_rows(s.recv, 2, here)
            beyond = pltpu.roll(pltpu.roll(flat, here, 0), width - 1, 1)
            whole = jnp.where(lane == 0, flat + beyond, 0.0)
            jump_flat = pltpu.roll(whole, ahead, 0) - whole
            solved = precise(s.mix[...], jump) * s.ring[0]
            solved = solved + precise(s.mix[...], jump_flat) * s.ring[1]
            mine = precise(s.mix_back[...], solved)
            other = pltpu.roll(mine, levels, 0)
            if here % 8 == 0:
                s.back[:, 0] = mine.reshape(devices, here, width)
                s.back[:, 1] = other.reshape(devices, here, width)
            else:
                for i in range(devices):
                    s.back[i, 0] = mine[i * here : (i + 1) * here]
                    s.back[i, 1] = other[i * here : (i + 1) * here]
            loop(1, devices, lambda i: answer(i).start())
            s.came[my_chunk] = s.back[me]

    def fluxes(h):
        def arrive(c):
            other = solver(c)

            @pl.when(other != me)
            def _():
                pltpu.make_async_remote_copy(
                    src_ref=s.back.at[0], dst_ref=s.came.at[c], send_sem=s.sent2.at[0],
                    recv_sem=s.came2.at[c], device_id=where(other), device_id_type=MESH,
                ).wait_recv()

        loop(h * half, (h + 1) * half, arrive)
        for c in range(h * half, (h + 1) * half):
            b, n = c // parts, c % parts
            for kind in range(2):
                s.flux[b, kind * here : (kind + 1) * here, n * width : (n + 1) * width] = (
                    s.came[c, kind]
                )

        def own(k):
            loop(k * size, k * size + size, lambda b: flux_problem(
                b, s.flux, after, s.own_up2, s.own_down2, here=here))
            chain2.begin(k)

        loop(h * per, (h + 1) * per, own)

    def send_out(k):
        cut = pl.ds(k * size, size)
        return pltpu.make_async_copy(
            s.modes.at[pl.ds(0, here), cut], phi_all.at[pl.ds(0, here), cut], s.moved.at[k]
        )

    def send_tip(h):
        cut = pl.ds(h * chunk, chunk)
        return pltpu.make_async_copy(
            s.modes.at[here, cut], phi_all.at[here, cut], s.moved.at[pieces + h]
        )

    def sweep(k):
        loop(k * size, k * size + size, lambda b: sweep_problem(
            b, s.modes, s.flux, s.got_up1, s.got_up2, s.got_down1, s.got_down2, s.single, after,
            s.modes, here=here, levels=levels))
        cut = pl.ds(k * size, size)
        part = over_rows(s.home, s.modes[0:here, cut].reshape(here * size, rows, cols))
        part = times_table(part.reshape(here * size * rows, cols), s.col)
        s.modes[0:here, cut] = part.reshape(here, size, rows, cols)
        send_out(k).start()

    def tip(h):
        cut = slice(h * chunk, h * chunk + chunk)
        last = over_rows(s.home, s.modes[here, cut])
        last = times_table(last.reshape(chunk * rows, cols), s.col)
        s.modes[here, cut] = last.reshape(chunk, rows, cols)
        send_tip(h).start()
        for b in range(h * chunk, h * chunk + chunk):
            edges[b] = times_table(s.flux[b, 0:here, :] + s.rims[b, 0:here, :], s.col)

    filled = max(per, reach - 1)

    def drain1(i):
        relays(chain1, i, 1)

        @pl.when(i <= per)
        def _():
            trace(i - 1)

    def drain2(k):
        @pl.when(reach + k > filled)
        def _():
            relays(chain1, reach + k, 1)

        trace(per + k)

    loop(here + 2, reach + per, lambda i: relays(chain1, i, 0))
    loop(1, filled + 1, drain1)
    for fetch in fetches[early:]:
        fetch.wait()
    solve_ring(0)
    loop(0, per, drain2)
    fluxes(0)
    loop(1, 3, lambda i: relays(chain2, i, 0))
    solve_ring(1)
    loop(3, reach + per, lambda i: relays(chain2, i, 0))
    fluxes(1)

    def drain3(i):
        relays(chain2, i, 1)

        @pl.when(i <= per)
        def _():
            sweep(i - 1)

    def drain4(k):
        @pl.when(reach + k > filled)
        def _():
            relays(chain2, reach + k, 1)

        sweep(per + k)

    loop(1, filled + 1, drain3)
    tip(0)
    loop(0, per, drain4)
    tip(1)

    chain1.finish(pieces)
    chain2.finish(pieces)

    def asked(c):
        other = solver(c)

        @pl.when(other != me)
        def _():
            pltpu.make_async_remote_copy(
                src_ref=s.pay.at[c], dst_ref=s.recv.at[me], send_sem=s.sent1.at[c],
                recv_sem=s.came1.at[me], device_id=where(other), device_id_type=MESH,
            ).wait_send()

    loop(0, devices, asked)
    loop(1, devices, lambda i: answer(i).wait_send())
    loop(0, pieces, lambda k: send_out(k).wait())
    for h in range(2):
        send_tip(h).wait()


def project_kernel(phi, following, edges, mult, next_mult, next_aux, *, levels):
    t = pl.program_id(0)
    here = pl.num_programs(0)
    _, problems, rows, cols = phi.shape
    moving = jnp.where(lax.axis_index("py") * here + t == levels - 1, 0.0, 1.0)
    row = lax.broadcasted_iota(jnp.int32, (rows, cols), 0)

    def one(b, carry):
        here_phi = phi[0, b]
        rim = jnp.broadcast_to(edges[b, pl.ds(t, 1), :], (rows, cols))
        grad_time = (following[0, b] - here_phi) * moving
        grad_first = jnp.where(
            row == rows - 1, rim, pltpu.roll(here_phi, rows - 1, 0) - here_phi
        )
        grad_second = pltpu.roll(here_phi, cols - 1, 1) - here_phi
        mult_time, mult_first, mult_second = (mult[k, 0, b] for k in range(3))
        time_part = grad_time + mult_time / PENALTY
        along = grad_first + mult_first / PENALTY
        beside = grad_second + mult_second / PENALTY
        kinetic = 0.5 * (along * along + beside * beside)
        offset_one = 1.0 + time_part
        solid = kinetic > 1e-37
        root = jnp.exp(jnp.log(jnp.where(solid, kinetic, 1.0)) * (1.0 / 3.0))
        scaling = jnp.maximum(offset_one, 1.0) + jnp.where(solid, root, 0.0)
        twice = 2.0 * offset_one
        for newton_step in range(NEWTON):
            above = scaling * scaling * (2.0 * scaling - offset_one) + kinetic
            derivative = scaling * (3.0 * scaling - twice)
            scaling = jnp.maximum(above / derivative, 1.0)
        feasible = time_part + kinetic <= 0.0
        shrink = jnp.where(feasible, 1.0, 1.0 / scaling)
        out_time = jnp.where(feasible, time_part, time_part - (scaling - 1.0))
        out_along = along * shrink
        out_beside = beside * shrink
        next_aux[0, 0, b] = out_time
        next_aux[1, 0, b] = out_along
        next_aux[2, 0, b] = out_beside
        next_mult[0, 0, b] = mult_time + PENALTY * (grad_time - out_time)
        next_mult[1, 0, b] = mult_first + PENALTY * (grad_first - out_along)
        next_mult[2, 0, b] = mult_second + PENALTY * (grad_second - out_beside)
        return carry

    lax.fori_loop(0, problems, one, 0, unroll=2)


def params(which=None):
    if which is None:
        return pltpu.CompilerParams(vmem_limit_bytes=VMEM_LIMIT)
    return pltpu.CompilerParams(
        collective_id=which, has_side_effects=True, vmem_limit_bytes=VMEM_LIMIT
    )


def whole_block(shape):
    return pl.BlockSpec(shape, lambda *_: (0,) * len(shape))


def local(multiplier, auxiliary, density_start, density_end):
    _, here, problems, rows, cols = multiplier.shape
    blocks = lax.axis_size("py")
    inner = lax.axis_size("px")
    group = lax.axis_size("grp") * inner
    devices = group * blocks
    levels = here * blocks
    held = -(-here // 8) * 8
    width = problems * cols // devices
    parts = cols // width
    total = devices * here
    delay, depth = 2, 4
    chunk = problems // 2
    pieces = 2 * math.gcd(chunk, 4)
    size = problems // pieces
    fit = max(1, 256 // rows)
    shape = lambda *dims: jax.ShapeDtypeStruct(dims, f32)
    vector = lambda *dims: pltpu.VMEM(dims, f32)
    anywhere = pl.BlockSpec(memory_space=pl.ANY)
    dma = lambda *dims: pltpu.SemaphoreType.DMA(dims)

    col_table = halves(hartley(cols))
    row_table = halves(np.kron(np.eye(math.gcd(chunk, fit)), cosines(rows)))
    row_back = halves(np.kron(np.eye(math.gcd(math.gcd(size * here, chunk), fit)), cosines(rows).T))
    single, ahead, after = slab_tables(rows, cols, here, blocks)
    mix, inverse, extra = ring_tables(rows, cols, group, levels)
    wide = np.zeros((total, cols), np.float32)
    wide[:, :1] = extra
    ring = np.stack([inverse, wide]).reshape(2, total, parts, width).transpose(0, 2, 1, 3).copy()
    tables = [col_table, row_table, row_back, single, ahead, after, mix, mix.T.copy(), ring]

    plane = (problems, rows, cols)
    part = (chunk, rows, cols)
    table = lambda x: pltpu.VMEM(x.shape, x.dtype)
    scratch = [
        vector(depth, 3, *part), vector(depth, 3, *part), vector(*plane), vector(*plane),
        table(col_table), table(row_table), table(row_back), table(single), table(ahead[0]),
        table(after[0]), table(mix), table(mix), table(ring[:, 0]),
        vector(*part), vector(*part), vector(chunk, held, cols), vector(problems, held, cols),
        vector(here + 1, *plane), vector(devices, 3, here, width),
        vector(devices, 3, here, width), vector(devices, 2, here, width),
        vector(devices, 2, here, width), vector(problems, 2 * here, cols),
    ] + [vector(*plane)] * 12 + [dma(2, depth), dma(11), dma(pieces + 2)]
    scratch += [dma(pieces)] * 8 + [dma(devices)] * 4
    phi, edges = pl.pallas_call(
        functools.partial(solve_kernel, levels=levels, here=here, blocks=blocks, inner=inner,
                          pieces=pieces, delay=delay, depth=depth),
        out_shape=(shape(here + 1, *plane), shape(problems, here, cols)),
        in_specs=[anywhere] * 13,
        out_specs=(anywhere, pl.BlockSpec(memory_space=pltpu.VMEM)),
        scratch_shapes=scratch,
        compiler_params=params(0),
        name="solve",
    )(multiplier, auxiliary, density_start, density_end, *(jnp.asarray(x) for x in tables))

    out_shape = shape(*multiplier.shape)
    level_block = pl.BlockSpec((3, 1, *plane), lambda t: (0, t, 0, 0, 0))
    phi_block = pl.BlockSpec((1, *plane), lambda t: (t, 0, 0, 0))
    next_block = pl.BlockSpec((1, *plane), lambda t: (t + 1, 0, 0, 0))
    return pl.pallas_call(
        functools.partial(project_kernel, levels=levels),
        out_shape=(out_shape, out_shape),
        grid=(here,),
        in_specs=[phi_block, next_block, whole_block(edges.shape), level_block],
        out_specs=(level_block, level_block),
        compiler_params=params(),
        name="project",
    )(phi, phi, edges, multiplier)


def solution(mesh):
    placed = (
        P(None, "py", None, ("grp", "px"), None),
        P(None, "py", None, ("grp", "px"), None),
        P(None, ("grp", "px"), None),
        P(None, ("grp", "px"), None),
    )
    return jax.shard_map(
        local,
        mesh=mesh,
        in_specs=placed,
        out_specs=(
            P(None, "py", None, ("grp", "px"), None),
            P(None, "py", None, ("grp", "px"), None),
        ),
        check_vma=False,
    )
```

```python
import functools
import math
import types

import jax
import jax.numpy as jnp
import ml_dtypes
import numpy as np
from jax import lax
from jax.experimental import pallas as pl
from jax.experimental.pallas import tpu as pltpu
from jax.sharding import PartitionSpec as P

NEWTON = 4
PENALTY = 1.0
VMEM_LIMIT = 60 * 1024 * 1024
SPACE = ("grp", "px")
EVERY = ("grp", "px", "py")
MESH = pl.DeviceIdType.MESH
bf16 = jnp.bfloat16
f32 = jnp.float32


def halves(table):
    high = table.astype(ml_dtypes.bfloat16)
    low = (table - high.astype(np.float64)).astype(ml_dtypes.bfloat16)
    return np.stack([high, low])


def hartley(length):
    angles = 2.0 * np.pi / length * (np.outer(np.arange(length), np.arange(length)) % length)
    return (np.cos(angles) + np.sin(angles)) / np.sqrt(length)


def cosines(length):
    k = np.arange(length)[:, None]
    x = np.arange(length)[None, :]
    weights = np.where(k == 0, np.sqrt(1.0 / length), np.sqrt(2.0 / length))
    return weights * np.cos(np.pi * k * (2 * x + 1) / (2 * length))


def slab_tables(rows, cols, here, blocks):
    j = np.arange(rows)[:, None]
    n = np.arange(cols)[None, :]
    lam = 4.0 * np.sin(np.pi * j / (2 * rows)) ** 2 + 4.0 * np.sin(np.pi * n / cols) ** 2
    sinh = np.sqrt(lam * (1.0 + 0.25 * lam))
    ratio = 1.0 / (1.0 + 0.5 * lam + sinh)
    positive = lam > 0.0
    full = ratio ** (2 * here * blocks)
    scale = np.where(positive, 0.5 / np.where(positive, sinh * (1.0 - full), 1.0), 0.0)
    edge = cosines(rows)[:, :1]
    low, high, down, low_q, high_q = [], [], [], [], []
    for block in range(blocks):
        first = block * here
        lows = [1.0 + ratio ** (2 * (first + v) + 1) for v in range(here + 1)]
        highs = [1.0 + ratio ** (2.0 * (blocks * here - 1 - first - v) + 1.0) for v in range(here + 1)]
        low.append(lows)
        high.append(highs)
        down.append([ratio**v * highs[v] for v in range(here + 1)])
        low_q.append([edge * ratio ** (here - v) * lows[v] for v in range(here)])
        high_q.append([edge * ratio**v * highs[v] for v in range(here)])
    single = np.stack([ratio, ratio**here, scale, edge * scale, np.broadcast_to(edge, lam.shape)])
    pack = lambda parts: np.asarray(parts, np.float32)
    ahead = np.concatenate([pack(low), pack(high), pack(down)], axis=1)
    after = np.concatenate([pack(low), pack(high), pack(low_q), pack(high_q)], axis=1)
    return single.astype(np.float32), ahead, after


def ring_tables(rows, cols, group, levels):
    r = np.arange(group)[:, None, None]
    k = np.arange(levels)[None, :, None]
    n = np.arange(cols)[None, None, :]
    tau = 4.0 * np.sin(np.pi * k / (2 * levels)) ** 2
    kappa = tau + 4.0 * np.sin(np.pi * n / cols) ** 2
    turn = 2.0 * np.sin(np.pi * r / group) ** 2
    positive = kappa > 0.0
    safe = np.where(positive, kappa, 1.0)
    shrink = 1.0 / (1.0 + 0.5 * safe + np.sqrt(safe * (1.0 + 0.25 * safe)))
    far = shrink**rows
    inverse = (1.0 - shrink) * (1.0 - far * far) / (
        (1.0 + shrink) * ((1.0 - far) ** 2 + 2.0 * far * turn)
    )
    inverse = np.where(positive, inverse, np.where(r == 0, 1.0 / rows, 0.0))
    edge = math.sqrt(1.0 / rows)
    flat = inverse[:, :, :1]
    moving = edge * flat / np.where(tau > 0.0, tau, 1.0)
    still = rows * edge / np.where(r > 0, 2.0 * turn, 1.0) * (r > 0)
    extra = np.where(tau > 0.0, moving, still)
    mix = np.kron(hartley(group), cosines(levels))
    flat_rows = group * levels
    return (
        mix.astype(np.float32),
        inverse.reshape(flat_rows, cols).astype(np.float32),
        extra.reshape(flat_rows, 1).astype(np.float32),
    )


def split(x):
    high = x.astype(bf16)
    return high, (x - high.astype(f32)).astype(bf16)


def mm(a, b):
    return jnp.dot(a, b, preferred_element_type=f32)


def times_table(x, table):
    high, low = split(x)
    return mm(high, table[0]) + (mm(low, table[0]) + mm(high, table[1]))


def table_times(table, x):
    high, low = split(x)
    return mm(table[0], high) + (mm(table[0], low) + mm(table[1], high))


def precise(a, b):
    return jnp.dot(a, b, precision=lax.Precision.HIGHEST, preferred_element_type=f32)


def over_rows(table, x):
    units, rows, cols = x.shape
    size = table.shape[1]
    bunch = size // rows
    parts = []
    for g in range(units // bunch):
        part = x[g * bunch : (g + 1) * bunch].reshape(size, cols)
        parts.append(table_times(table, part).reshape(bunch, rows, cols))
    return parts[0] if len(parts) == 1 else jnp.concatenate(parts, axis=0)


def steps_from(me, blocks):
    return me, blocks - 1 - me


class Chain:
    def __init__(self, up, down, step, size, blocks):
        self.me = lax.axis_index("py")
        self.blocks, self.size, self.step = blocks, size, step
        self.far = steps_from(self.me, blocks)
        self.next = ((self.me + 1) % blocks, (self.me + blocks - 1) % blocks)
        self.refs = (up, down)

    def copy(self, way, source, k):
        _, got, _, sent, came = self.refs[way]
        cut = pl.ds(k * self.size, self.size)
        return pltpu.make_async_remote_copy(
            src_ref=source.at[cut],
            dst_ref=got.at[cut],
            send_sem=sent.at[k],
            recv_sem=came.at[k],
            device_id={"py": self.next[way]},
            device_id_type=MESH,
        )

    def greet(self):
        barrier = pltpu.get_barrier_semaphore()
        lower, upper = self.me > 0, self.me < self.blocks - 1

        @pl.when(lower)
        def _():
            pl.semaphore_signal(barrier, inc=1, device_id={"py": self.me - 1}, device_id_type=MESH)

        @pl.when(upper)
        def _():
            pl.semaphore_signal(barrier, inc=1, device_id={"py": self.me + 1}, device_id_type=MESH)

        @pl.when(lower & upper)
        def _():
            pl.semaphore_wait(barrier, 2)

        @pl.when(jnp.logical_not(lower & upper))
        def _():
            pl.semaphore_wait(barrier, 1)

    def clear(self):
        for way in range(2):
            got = self.refs[way][1]

            @pl.when(self.far[way] == 0)
            def _():
                got[...] = jnp.zeros_like(got)

    def begin(self, k):
        for way in range(2):

            @pl.when(self.far[way] == 0)
            def _():
                self.copy(way, self.refs[way][0], k).start()

    def relay(self, way, k, low, high):
        own, got, out, _, _ = self.refs[way]

        @pl.when((self.far[way] > 0) & (k >= low) & (k < high))
        def _():
            self.copy(way, out, k).wait_recv()

            @pl.when(self.far[way] < self.blocks - 1)
            def _():
                for q in range(self.size):
                    at = k * self.size + q
                    out[at] = own[at] + self.step[...] * got[at]
                self.copy(way, out, k).start()

    def finish(self, pieces):
        for way in range(2):

            @pl.when(self.far[way] < self.blocks - 1)
            def _():
                def one(k, carry):
                    self.copy(way, self.refs[way][2], k).wait_send()
                    return carry

                lax.fori_loop(0, pieces, one, 0)


def trace_problem(b, modes, up, down, rims, single, tables, pay, *, here):
    rows, cols = up.shape[1], up.shape[2]
    width = pay.shape[3]
    parts = cols // width
    lane = lax.broadcasted_iota(jnp.int32, (1, cols), 1)
    parity = lax.broadcasted_iota(jnp.int32, (8, cols), 0) % 2 == 0
    total = [jnp.zeros((8, cols), f32) for _ in range(here)]
    for c in range(rows // 8):
        cut = slice(c * 8, c * 8 + 8)
        ratio, weight = single[0, cut, :], single[3, cut, :]
        value = up[b, cut, :]
        sums = []
        for v in range(here):
            if v:
                value = ratio * value
            value = value + tables[v, cut, :] * modes[v, b, cut, :]
            sums.append(tables[here + 1 + v, cut, :] * value)
        behind = down[b, cut, :]
        for v in range(here, -1, -1):
            if v < here:
                total[v] = total[v] + weight * (sums[v] + tables[v, cut, :] * behind)
            behind = ratio * (behind + tables[here + 1 + v, cut, :] * modes[v, b, cut, :])

    def put(kind, v, row):
        for n in range(parts):
            pay[b * parts + n, kind, v : v + 1, :] = row[:, n * width : (n + 1) * width]

    for v in range(here):
        even = jnp.sum(jnp.where(parity, total[v], 0.0), axis=0, keepdims=True)
        odd = jnp.sum(jnp.where(parity, 0.0, total[v]), axis=0, keepdims=True)
        put(0, v, even + odd)
        put(1, v, even - odd + rims[b, v : v + 1, :])
        flat = jnp.where(lane == 0, modes[v, b, 0:1, :], 0.0)
        if v == 0:
            beyond = pltpu.roll(modes[here, b, 0:8, :], 1, 1)[0:1]
            flat = flat + jnp.where(lane == 1, beyond, 0.0)
        put(2, v, flat)


def sweep_problem(b, modes, flux, up1, up2, down1, down2, single, tables, wave, *, here, levels):
    rows, cols = up1.shape[1], up1.shape[2]
    first = lax.axis_index("py") * here
    for c in range(rows // 8):
        cut = slice(c * 8, c * 8 + 8)
        ratio, scale, edge = single[0, cut, :], single[2, cut, :], single[4, cut, :]
        sign = jnp.where(
            lax.broadcasted_iota(jnp.int32, (8, cols), 0) % 2 == 0, edge, -edge
        )
        value = up1[b, cut, :] + up2[b, cut, :]
        source, sums = [], []
        for v in range(here + 1):
            now = modes[v, b, cut, :]
            if v < here:
                mine = jnp.broadcast_to(flux[b, v : v + 1, :], (8, cols))
                other = jnp.broadcast_to(flux[b, here + v : here + v + 1, :], (8, cols))
                now = now + (sign * mine - edge * other)
            source.append(now)
            if v:
                value = ratio * value
            value = value + tables[v, cut, :] * now
            sums.append(tables[here + 1 + v, cut, :] * value)
        behind = down1[b, cut, :] + down2[b, cut, :]
        for v in range(here, -1, -1):
            wave[v, b, cut, :] = scale * (sums[v] + tables[v, cut, :] * behind)
            behind = ratio * (behind + tables[here + 1 + v, cut, :] * source[v])
        if c == 0:
            spot = (lax.broadcasted_iota(jnp.int32, (8, 128), 0) == 0) & (
                lax.broadcasted_iota(jnp.int32, (8, 128), 1) == 0
            )
            below = 0.5 * (up1[b, 0:8, 0:128] + up2[b, 0:8, 0:128])
            whole = below + 0.5 * (down1[b, 0:8, 0:128] + down2[b, 0:8, 0:128])
            for v in range(here + 1):
                whole = whole + source[v][:, 0:128]
            mean = whole * (1.0 / levels)
            level_value = jnp.zeros((8, 128), f32)
            for v in range(here + 1):
                wave[v, b, 0:8, 0:128] = jnp.where(spot, level_value, wave[v, b, 0:8, 0:128])
                if v < here:
                    below = below + source[v][:, 0:128]
                    count = (first + (v + 1)).astype(f32)
                    level_value = level_value - (below - count * mean)


def flux_problem(b, flux, tables, up, down, *, here):
    rows, cols = up.shape[1], up.shape[2]
    sign = jnp.where(lax.broadcasted_iota(jnp.int32, (rows, cols), 0) % 2 == 0, 1.0, -1.0)
    base = 2 * (here + 1)
    rise = jnp.zeros((rows, cols), f32)
    fall = jnp.zeros((rows, cols), f32)
    for v in range(here):
        mine = jnp.broadcast_to(flux[b, v : v + 1, :], (rows, cols))
        other = jnp.broadcast_to(flux[b, here + v : here + v + 1, :], (rows, cols))
        both = sign * mine - other
        rise = rise + tables[base + v] * both
        fall = fall + tables[base + here + v] * both
    up[b] = rise
    down[b] = fall


def flat_rows(ref, kind, here):
    devices, width = ref.shape[0], ref.shape[3]
    if here % 8 == 0:
        return ref[:, kind].reshape(devices * here, width)
    return jnp.concatenate([ref[i, kind] for i in range(devices)], axis=0)


SCRATCH = (
    "mult", "aux", "start", "end", "col", "row", "home", "single", "ahead", "after", "mix",
    "mix_back", "ring",
    "prev", "body", "spread", "tail", "rims", "modes", "pay", "recv", "back", "came", "flux",
    "own_up1", "own_down1", "got_up1", "got_down1", "out_up1", "out_down1",
    "own_up2", "own_down2", "got_up2", "got_down2", "out_up2", "out_down2",
    "streamed", "fetched", "moved",
    "sent_up1", "sent_down1", "came_up1", "came_down1",
    "sent_up2", "sent_down2", "came_up2", "came_down2",
    "sent1", "came1", "sent2", "came2", "sent3", "came3",
)


def loop(low, high, action, unroll=1):
    def one(i, carry):
        action(i)
        return carry

    if not (isinstance(low, int) and isinstance(high, int) and high <= low):
        lax.fori_loop(low, high, one, 0, unroll=unroll)


def solve_kernel(
    mult_all, aux_all, start_all, end_all, col_all, row_all, home_all, single_all, ahead_all,
    after_all, mix_all, mix_back_all, ring_all, phi_all, edges, *scratch,
    levels, here, blocks, inner, pieces, delay, depth
):
    s = types.SimpleNamespace(**dict(zip(SCRATCH, scratch)))
    problems, rows, cols = s.start.shape
    devices, width = s.pay.shape[0], s.pay.shape[3]
    chunk, per, half = problems // 2, pieces // 2, devices // 2
    size = problems // pieces
    parts = cols // width
    reach = delay * (blocks - 1)
    me_py = lax.axis_index("py")
    me_space = lax.axis_index("grp") * inner + lax.axis_index("px")
    me = me_space * blocks + me_py
    my_half = me_space % 2
    my_chunk = my_half * half + (me_space // 2) * blocks + me_py
    tables, after = s.ahead, s.after

    def where(flat):
        return {
            "grp": flat // (inner * blocks),
            "px": flat // blocks % inner,
            "py": flat % blocks,
        }

    def solver(c):
        i = c % half
        return (2 * (i // blocks) + c // half) * blocks + i % blocks

    def chain(n):
        part = lambda name: getattr(s, name % n)
        return Chain(
            *((part("own_%s%%d" % way), part("got_%s%%d" % way), part("out_%s%%d" % way),
               part("sent_%s%%d" % way), part("came_%s%%d" % way)) for way in ("up", "down")),
            s.single.at[1], size, blocks,
        )

    chain1, chain2 = chain(1), chain(2)

    def relays(which, i, owner):
        for way in range(2):
            k = i - delay * which.far[way]
            which.relay(way, owner * per + k, owner * per, (owner + 1) * per)

    def stream(g):
        c, t, at = g // here, g % here, g % depth
        cut = pl.ds(c * chunk, chunk)
        return [
            pltpu.make_async_copy(mult_all.at[:, t, cut], s.mult.at[at], s.streamed.at[0, at]),
            pltpu.make_async_copy(aux_all.at[:, t, cut], s.aux.at[at], s.streamed.at[1, at]),
        ]

    pairs = [
        (start_all, s.start), (end_all, s.end), (col_all, s.col), (row_all, s.row),
        (single_all, s.single), (ahead_all.at[me_py], s.ahead), (after_all.at[me_py], s.after),
        (mix_all, s.mix), (mix_back_all, s.mix_back), (ring_all.at[:, my_chunk % parts], s.ring),
        (home_all, s.home),
    ]
    fetches = [pltpu.make_async_copy(x, y, s.fetched.at[i]) for i, (x, y) in enumerate(pairs)]
    early = 6
    for g in range(min(depth, 2 * here)):
        for copy in stream(g):
            copy.start()
        if g == 0:
            for fetch in fetches[:early]:
                fetch.start()
    for fetch in fetches[early:]:
        fetch.start()
    barrier = pltpu.get_barrier_semaphore()

    def hail(i):
        pl.semaphore_signal(
            barrier, inc=1, device_id=where((me + i) % devices), device_id_type=MESH
        )

    loop(1, devices, hail)
    chain1.clear()
    chain2.clear()

    @pl.when(my_chunk % parts != 0)
    def _():
        s.recv[:, 2] = jnp.zeros((devices, here, width), f32)

    for fetch in fetches[:early]:
        fetch.wait()
    row = lax.broadcasted_iota(jnp.int32, (rows, cols), 0)

    def across_rows(c, v):
        base = c * chunk
        s.modes[v, base : base + chunk] = over_rows(s.row, s.spread[...])
        ratio, low, falling = s.single[0], tables[v], tables[2 * (here + 1) + v]
        for b in range(base, base + chunk):
            value = s.modes[v, b]
            s.own_up1[b] = ratio * s.own_up1[b] + low * value
            s.own_down1[b] = s.own_down1[b] + falling * value

    def across_cols(values):
        flat = values[...].reshape(chunk * rows, cols)
        s.spread[...] = times_table(flat, s.col).reshape(chunk, rows, cols)

    def source(c, t):
        g = c * here + t
        at = g % depth
        level = me_py * here + t
        for copy in stream(g):
            copy.wait()
        across_rows(c, jnp.maximum(t - 1, 0))
        keep = jnp.where(level == levels - 1, 0.0, 1.0)
        begin = jnp.where(level == 0, -1.0 / PENALTY, 0.0)
        finish = jnp.where(level == levels - 1, 1.0 / PENALTY, 0.0)
        for b in range(chunk):
            along = s.aux[at, 1, b] - s.mult[at, 1, b] / PENALTY
            s.tail[b, pl.ds(t, 1), :] = along[rows - 1 :, :]
            beside = jnp.where(row == 0, 0.0, pltpu.roll(along, 1, 0))
            along = jnp.where(row == rows - 1, 0.0, along)
            second = s.aux[at, 2, b] - s.mult[at, 2, b] / PENALTY
            side = pltpu.roll(second, 1, 1) - second
            now = (s.aux[at, 0, b] - s.mult[at, 0, b] / PENALTY) * keep
            boundary = begin * s.start[c * chunk + b] + finish * s.end[c * chunk + b]
            s.body[b] = s.prev[b] - now + beside - along + side + boundary
            s.prev[b] = now
        across_cols(s.body)

        @pl.when(g + depth < 2 * here)
        def _():
            for copy in stream(g + depth):
                copy.start()

        if c == 1:
            relays(chain1, t + 1, 0)

    for c in range(2):
        cut = slice(c * chunk, c * chunk + chunk)
        s.prev[...] = jnp.zeros_like(s.prev)
        s.tail[...] = jnp.zeros_like(s.tail)
        s.spread[...] = jnp.zeros_like(s.spread)
        s.own_up1[cut] = jnp.zeros((chunk, rows, cols), f32)
        s.own_down1[cut] = jnp.zeros((chunk, rows, cols), f32)
        loop(0, here, functools.partial(source, c))
        across_rows(c, here - 1)
        across_cols(s.prev)
        across_rows(c, here)
        held = s.tail.shape[1]
        if c == 0:
            pl.semaphore_wait(barrier, devices - 1)
        loop(c * per, (c + 1) * per, chain1.begin)
        if c == 1:
            relays(chain1, here + 1, 0)
        flat = s.tail[...].reshape(chunk * held, cols)
        s.rims[cut] = times_table(flat, s.col).reshape(chunk, held, cols)

    def question(c, flat, source, target):
        kinds = pl.ds(2, 1) if flat else pl.ds(0, 2)
        return pltpu.make_async_remote_copy(
            src_ref=s.pay.at[c, kinds], dst_ref=s.recv.at[source, kinds],
            send_sem=(s.sent3 if flat else s.sent1).at[c],
            recv_sem=(s.came3 if flat else s.came1).at[source],
            device_id=where(target), device_id_type=MESH,
        )

    def ask(c, flat):
        other = solver(c)

        @pl.when(other == me)
        def _():
            s.recv[me] = s.pay[c]

        @pl.when(other != me)
        def _():
            question(c, False, me, other).start()
            if flat:
                question(c, True, me, other).start()

    def trace(k):
        def one(b):
            trace_problem(
                b, s.modes, s.got_up1, s.got_down1, s.rims, s.single, tables, s.pay, here=here
            )
            for n in range(parts):
                ask(b * parts + n, n == 0)

        loop(k * size, k * size + size, one)

    def answer(i):
        other = (me + i) % devices
        return pltpu.make_async_remote_copy(
            src_ref=s.back.at[other], dst_ref=s.came.at[my_chunk], send_sem=s.sent2.at[i],
            recv_sem=s.came2.at[my_chunk], device_id=where(other), device_id_type=MESH,
        )

    def solve_ring(h):
        @pl.when(my_half == h)
        def _():
            def arrive(i):
                other = (me + i) % devices
                question(0, False, other, other).wait_recv()

                @pl.when(my_chunk % parts == 0)
                def _():
                    question(0, True, other, other).wait_recv()

            loop(1, devices, arrive)
            total = devices * here
            lane = lax.broadcasted_iota(jnp.int32, (total, width), 1)
            ahead = total - levels
            jump = pltpu.roll(flat_rows(s.recv, 0, here), ahead, 0) - flat_rows(s.recv, 1, here)
            flat = flat_rows(s.recv, 2, here)
            beyond = pltpu.roll(pltpu.roll(flat, here, 0), width - 1, 1)
            whole = jnp.where(lane == 0, flat + beyond, 0.0)
            jump_flat = pltpu.roll(whole, ahead, 0) - whole
            solved = precise(s.mix[...], jump) * s.ring[0]
            solved = solved + precise(s.mix[...], jump_flat) * s.ring[1]
            mine = precise(s.mix_back[...], solved)
            other = pltpu.roll(mine, levels, 0)
            if here % 8 == 0:
                s.back[:, 0] = mine.reshape(devices, here, width)
                s.back[:, 1] = other.reshape(devices, here, width)
            else:
                for i in range(devices):
                    s.back[i, 0] = mine[i * here : (i + 1) * here]
                    s.back[i, 1] = other[i * here : (i + 1) * here]
            loop(1, devices, lambda i: answer(i).start())
            s.came[my_chunk] = s.back[me]

    def fluxes(h):
        def arrive(c):
            other = solver(c)

            @pl.when(other != me)
            def _():
                pltpu.make_async_remote_copy(
                    src_ref=s.back.at[0], dst_ref=s.came.at[c], send_sem=s.sent2.at[0],
                    recv_sem=s.came2.at[c], device_id=where(other), device_id_type=MESH,
                ).wait_recv()

        loop(h * half, (h + 1) * half, arrive)
        for c in range(h * half, (h + 1) * half):
            b, n = c // parts, c % parts
            for kind in range(2):
                s.flux[b, kind * here : (kind + 1) * here, n * width : (n + 1) * width] = (
                    s.came[c, kind]
                )

        def own(k):
            loop(k * size, k * size + size, lambda b: flux_problem(
                b, s.flux, after, s.own_up2, s.own_down2, here=here))
            chain2.begin(k)

        loop(h * per, (h + 1) * per, own)

    def send_out(k):
        cut = pl.ds(k * size, size)
        return pltpu.make_async_copy(
            s.modes.at[pl.ds(0, here), cut], phi_all.at[pl.ds(0, here), cut], s.moved.at[k]
        )

    def send_tip(h):
        cut = pl.ds(h * chunk, chunk)
        return pltpu.make_async_copy(
            s.modes.at[here, cut], phi_all.at[here, cut], s.moved.at[pieces + h]
        )

    def sweep(k):
        loop(k * size, k * size + size, lambda b: sweep_problem(
            b, s.modes, s.flux, s.got_up1, s.got_up2, s.got_down1, s.got_down2, s.single, after,
            s.modes, here=here, levels=levels))
        cut = pl.ds(k * size, size)
        part = over_rows(s.home, s.modes[0:here, cut].reshape(here * size, rows, cols))
        part = times_table(part.reshape(here * size * rows, cols), s.col)
        s.modes[0:here, cut] = part.reshape(here, size, rows, cols)
        send_out(k).start()

    def tip(h):
        cut = slice(h * chunk, h * chunk + chunk)
        last = over_rows(s.home, s.modes[here, cut])
        last = times_table(last.reshape(chunk * rows, cols), s.col)
        s.modes[here, cut] = last.reshape(chunk, rows, cols)
        send_tip(h).start()
        for b in range(h * chunk, h * chunk + chunk):
            edges[b] = times_table(s.flux[b, 0:here, :] + s.rims[b, 0:here, :], s.col)

    filled = max(per, reach - 1)

    def drain1(i):
        relays(chain1, i, 1)

        @pl.when(i <= per)
        def _():
            trace(i - 1)

    def drain2(k):
        @pl.when(reach + k > filled)
        def _():
            relays(chain1, reach + k, 1)

        trace(per + k)

    loop(here + 2, reach + per, lambda i: relays(chain1, i, 0))
    loop(1, filled + 1, drain1)
    for fetch in fetches[early:]:
        fetch.wait()
    solve_ring(0)
    loop(0, per, drain2)
    fluxes(0)
    loop(1, 3, lambda i: relays(chain2, i, 0))
    solve_ring(1)
    loop(3, reach + per, lambda i: relays(chain2, i, 0))
    fluxes(1)

    def drain3(i):
        relays(chain2, i, 1)

        @pl.when(i <= per)
        def _():
            sweep(i - 1)

    def drain4(k):
        @pl.when(reach + k > filled)
        def _():
            relays(chain2, reach + k, 1)

        sweep(per + k)

    def asked(c):
        other = solver(c)

        @pl.when(other != me)
        def _():
            question(c, False, me, other).wait_send()

            @pl.when(c % parts == 0)
            def _():
                question(c, True, me, other).wait_send()

    loop(1, filled + 1, drain3)
    tip(0)
    chain1.finish(pieces)
    loop(0, devices, asked)
    loop(1, devices, lambda i: answer(i).wait_send())
    loop(0, per, drain4)
    tip(1)

    chain2.finish(pieces)
    loop(0, pieces, lambda k: send_out(k).wait())
    for h in range(2):
        send_tip(h).wait()


def project_kernel(first, following, edges, mult, next_mult, next_aux, phi, *, levels):
    t = pl.program_id(0)
    here = pl.num_programs(0)
    _, problems, rows, cols = first.shape

    @pl.when(t == 0)
    def _():
        phi[...] = first[0]

    moving = jnp.where(lax.axis_index("py") * here + t == levels - 1, 0.0, 1.0)
    row = lax.broadcasted_iota(jnp.int32, (rows, cols), 0)

    def one(b, carry):
        here_phi = phi[b]
        next_phi = following[0, b]
        phi[b] = next_phi
        rim = jnp.broadcast_to(edges[b, pl.ds(t, 1), :], (rows, cols))
        grad_time = (next_phi - here_phi) * moving
        grad_first = jnp.where(
            row == rows - 1, rim, pltpu.roll(here_phi, rows - 1, 0) - here_phi
        )
        grad_second = pltpu.roll(here_phi, cols - 1, 1) - here_phi
        mult_time, mult_first, mult_second = (mult[k, 0, b] for k in range(3))
        time_part = grad_time + mult_time / PENALTY
        along = grad_first + mult_first / PENALTY
        beside = grad_second + mult_second / PENALTY
        kinetic = 0.5 * (along * along + beside * beside)
        offset_one = 1.0 + time_part
        solid = kinetic > 1e-37
        root = jnp.exp(jnp.log(jnp.where(solid, kinetic, 1.0)) * (1.0 / 3.0))
        scaling = jnp.maximum(offset_one, 1.0) + jnp.where(solid, root, 0.0)
        twice = 2.0 * offset_one
        for newton_step in range(NEWTON):
            above = scaling * scaling * (2.0 * scaling - offset_one) + kinetic
            derivative = scaling * (3.0 * scaling - twice)
            scaling = jnp.maximum(above / derivative, 1.0)
        feasible = time_part + kinetic <= 0.0
        shrink = jnp.where(feasible, 1.0, 1.0 / scaling)
        out_time = jnp.where(feasible, time_part, time_part - (scaling - 1.0))
        out_along = along * shrink
        out_beside = beside * shrink
        next_aux[0, 0, b] = out_time
        next_aux[1, 0, b] = out_along
        next_aux[2, 0, b] = out_beside
        next_mult[0, 0, b] = mult_time + PENALTY * (grad_time - out_time)
        next_mult[1, 0, b] = mult_first + PENALTY * (grad_first - out_along)
        next_mult[2, 0, b] = mult_second + PENALTY * (grad_second - out_beside)
        return carry

    lax.fori_loop(0, problems, one, 0, unroll=4)


def params(which=None):
    if which is None:
        return pltpu.CompilerParams(vmem_limit_bytes=VMEM_LIMIT)
    return pltpu.CompilerParams(
        collective_id=which, has_side_effects=True, vmem_limit_bytes=VMEM_LIMIT
    )


def whole_block(shape):
    return pl.BlockSpec(shape, lambda *_: (0,) * len(shape))


def local(multiplier, auxiliary, density_start, density_end):
    _, here, problems, rows, cols = multiplier.shape
    blocks = lax.axis_size("py")
    inner = lax.axis_size("px")
    group = lax.axis_size("grp") * inner
    devices = group * blocks
    levels = here * blocks
    held = -(-here // 8) * 8
    width = problems * cols // devices
    parts = cols // width
    total = devices * here
    delay, depth = 3, 4
    chunk = problems // 2
    pieces = 2 * math.gcd(chunk, 4)
    size = problems // pieces
    fit = max(1, 256 // rows)
    shape = lambda *dims: jax.ShapeDtypeStruct(dims, f32)
    vector = lambda *dims: pltpu.VMEM(dims, f32)
    anywhere = pl.BlockSpec(memory_space=pl.ANY)
    dma = lambda *dims: pltpu.SemaphoreType.DMA(dims)

    col_table = halves(hartley(cols))
    row_table = halves(np.kron(np.eye(math.gcd(chunk, fit)), cosines(rows)))
    row_back = halves(np.kron(np.eye(math.gcd(math.gcd(size * here, chunk), fit)), cosines(rows).T))
    single, ahead, after = slab_tables(rows, cols, here, blocks)
    mix, inverse, extra = ring_tables(rows, cols, group, levels)
    wide = np.zeros((total, cols), np.float32)
    wide[:, :1] = extra
    ring = np.stack([inverse, wide]).reshape(2, total, parts, width).transpose(0, 2, 1, 3).copy()
    tables = [col_table, row_table, row_back, single, ahead, after, mix, mix.T.copy(), ring]

    plane = (problems, rows, cols)
    part = (chunk, rows, cols)
    table = lambda x: pltpu.VMEM(x.shape, x.dtype)
    scratch = [
        vector(depth, 3, *part), vector(depth, 3, *part), vector(*plane), vector(*plane),
        table(col_table), table(row_table), table(row_back), table(single), table(ahead[0]),
        table(after[0]), table(mix), table(mix), table(ring[:, 0]),
        vector(*part), vector(*part), vector(*part), vector(chunk, held, cols),
        vector(problems, held, cols),
        vector(here + 1, *plane), vector(devices, 3, here, width),
        vector(devices, 3, here, width), vector(devices, 2, here, width),
        vector(devices, 2, here, width), vector(problems, 2 * here, cols),
    ] + [vector(*plane)] * 12 + [dma(2, depth), dma(11), dma(pieces + 2)]
    scratch += [dma(pieces)] * 8 + [dma(devices)] * 6
    phi, edges = pl.pallas_call(
        functools.partial(solve_kernel, levels=levels, here=here, blocks=blocks, inner=inner,
                          pieces=pieces, delay=delay, depth=depth),
        out_shape=(shape(here + 1, *plane), shape(problems, here, cols)),
        in_specs=[anywhere] * 13,
        out_specs=(anywhere, pl.BlockSpec(memory_space=pltpu.VMEM)),
        scratch_shapes=scratch,
        compiler_params=params(0),
        name="solve",
    )(multiplier, auxiliary, density_start, density_end, *(jnp.asarray(x) for x in tables))

    out_shape = shape(*multiplier.shape)
    level_block = pl.BlockSpec((3, 1, *plane), lambda t: (0, t, 0, 0, 0))
    phi_block = whole_block((1, *plane))
    next_block = pl.BlockSpec((1, *plane), lambda t: (t + 1, 0, 0, 0))
    return pl.pallas_call(
        functools.partial(project_kernel, levels=levels),
        out_shape=(out_shape, out_shape),
        grid=(here,),
        in_specs=[phi_block, next_block, whole_block(edges.shape), level_block],
        out_specs=(level_block, level_block),
        scratch_shapes=[vector(*plane)],
        compiler_params=params(),
        name="project",
    )(phi, phi, edges, multiplier)


def solution(mesh):
    placed = (
        P(None, "py", None, ("grp", "px"), None),
        P(None, "py", None, ("grp", "px"), None),
        P(None, ("grp", "px"), None),
        P(None, ("grp", "px"), None),
    )
    return jax.shard_map(
        local,
        mesh=mesh,
        in_specs=placed,
        out_specs=(
            P(None, "py", None, ("grp", "px"), None),
            P(None, "py", None, ("grp", "px"), None),
        ),
        check_vma=False,
    )
```

```python
import functools
import math
import types

import jax
import jax.numpy as jnp
import ml_dtypes
import numpy as np
from jax import lax
from jax.experimental import pallas as pl
from jax.experimental.pallas import tpu as pltpu
from jax.sharding import PartitionSpec as P

NEWTON = 4
PENALTY = 1.0
VMEM_LIMIT = 60 * 1024 * 1024
SPACE = ("grp", "px")
EVERY = ("grp", "px", "py")
MESH = pl.DeviceIdType.MESH
bf16 = jnp.bfloat16
f32 = jnp.float32


def halves(table):
    high = table.astype(ml_dtypes.bfloat16)
    low = (table - high.astype(np.float64)).astype(ml_dtypes.bfloat16)
    return np.stack([high, low])


def hartley(length):
    angles = 2.0 * np.pi / length * (np.outer(np.arange(length), np.arange(length)) % length)
    return (np.cos(angles) + np.sin(angles)) / np.sqrt(length)


def cosines(length):
    k = np.arange(length)[:, None]
    x = np.arange(length)[None, :]
    weights = np.where(k == 0, np.sqrt(1.0 / length), np.sqrt(2.0 / length))
    return weights * np.cos(np.pi * k * (2 * x + 1) / (2 * length))


def slab_tables(rows, cols, here, blocks):
    j = np.arange(rows)[:, None]
    n = np.arange(cols)[None, :]
    lam = 4.0 * np.sin(np.pi * j / (2 * rows)) ** 2 + 4.0 * np.sin(np.pi * n / cols) ** 2
    sinh = np.sqrt(lam * (1.0 + 0.25 * lam))
    ratio = 1.0 / (1.0 + 0.5 * lam + sinh)
    positive = lam > 0.0
    full = ratio ** (2 * here * blocks)
    scale = np.where(positive, 0.5 / np.where(positive, sinh * (1.0 - full), 1.0), 0.0)
    edge = cosines(rows)[:, :1]
    low, high, down, low_q, high_q = [], [], [], [], []
    for block in range(blocks):
        first = block * here
        lows = [1.0 + ratio ** (2 * (first + v) + 1) for v in range(here + 1)]
        highs = [1.0 + ratio ** (2.0 * (blocks * here - 1 - first - v) + 1.0) for v in range(here + 1)]
        low.append(lows)
        high.append(highs)
        down.append([ratio**v * highs[v] for v in range(here + 1)])
        low_q.append([edge * ratio ** (here - v) * lows[v] for v in range(here)])
        high_q.append([edge * ratio**v * highs[v] for v in range(here)])
    single = np.stack([ratio, ratio**here, scale, edge * scale, np.broadcast_to(edge, lam.shape)])
    pack = lambda parts: np.asarray(parts, np.float32)
    ahead = np.concatenate([pack(low), pack(high), pack(down)], axis=1)
    after = np.concatenate([pack(low), pack(high), pack(low_q), pack(high_q)], axis=1)
    return single.astype(np.float32), ahead, after


def ring_tables(rows, cols, group, levels):
    r = np.arange(group)[:, None, None]
    k = np.arange(levels)[None, :, None]
    n = np.arange(cols)[None, None, :]
    tau = 4.0 * np.sin(np.pi * k / (2 * levels)) ** 2
    kappa = tau + 4.0 * np.sin(np.pi * n / cols) ** 2
    turn = 2.0 * np.sin(np.pi * r / group) ** 2
    positive = kappa > 0.0
    safe = np.where(positive, kappa, 1.0)
    shrink = 1.0 / (1.0 + 0.5 * safe + np.sqrt(safe * (1.0 + 0.25 * safe)))
    far = shrink**rows
    inverse = (1.0 - shrink) * (1.0 - far * far) / (
        (1.0 + shrink) * ((1.0 - far) ** 2 + 2.0 * far * turn)
    )
    inverse = np.where(positive, inverse, np.where(r == 0, 1.0 / rows, 0.0))
    edge = math.sqrt(1.0 / rows)
    flat = inverse[:, :, :1]
    moving = edge * flat / np.where(tau > 0.0, tau, 1.0)
    still = rows * edge / np.where(r > 0, 2.0 * turn, 1.0) * (r > 0)
    extra = np.where(tau > 0.0, moving, still)
    mix = np.kron(hartley(group), cosines(levels))
    flat_rows = group * levels
    return (
        mix,
        inverse.reshape(flat_rows, cols).astype(np.float32),
        extra.reshape(flat_rows, 1).astype(np.float32),
    )


def split(x):
    high = x.astype(bf16)
    return high, (x - high.astype(f32)).astype(bf16)


def mm(a, b):
    return jnp.dot(a, b, preferred_element_type=f32)


def times_table(x, table):
    high, low = split(x)
    return mm(high, table[0]) + (mm(low, table[0]) + mm(high, table[1]))


def table_times(table, x):
    high, low = split(x)
    return mm(table[0], high) + (mm(table[0], low) + mm(table[1], high))


def over_rows(table, x):
    units, rows, cols = x.shape
    size = table.shape[1]
    bunch = size // rows
    parts = []
    for g in range(units // bunch):
        part = x[g * bunch : (g + 1) * bunch].reshape(size, cols)
        parts.append(table_times(table, part).reshape(bunch, rows, cols))
    return parts[0] if len(parts) == 1 else jnp.concatenate(parts, axis=0)


def steps_from(me, blocks):
    return me, blocks - 1 - me


class Chain:
    def __init__(self, up, down, step, size, blocks):
        self.me = lax.axis_index("py")
        self.blocks, self.size, self.step = blocks, size, step
        self.far = steps_from(self.me, blocks)
        self.next = ((self.me + 1) % blocks, (self.me + blocks - 1) % blocks)
        self.refs = (up, down)

    def copy(self, way, source, k):
        _, got, _, sent, came = self.refs[way]
        cut = pl.ds(k * self.size, self.size)
        return pltpu.make_async_remote_copy(
            src_ref=source.at[cut],
            dst_ref=got.at[cut],
            send_sem=sent.at[k],
            recv_sem=came.at[k],
            device_id={"py": self.next[way]},
            device_id_type=MESH,
        )

    def greet(self):
        barrier = pltpu.get_barrier_semaphore()
        lower, upper = self.me > 0, self.me < self.blocks - 1

        @pl.when(lower)
        def _():
            pl.semaphore_signal(barrier, inc=1, device_id={"py": self.me - 1}, device_id_type=MESH)

        @pl.when(upper)
        def _():
            pl.semaphore_signal(barrier, inc=1, device_id={"py": self.me + 1}, device_id_type=MESH)

        @pl.when(lower & upper)
        def _():
            pl.semaphore_wait(barrier, 2)

        @pl.when(jnp.logical_not(lower & upper))
        def _():
            pl.semaphore_wait(barrier, 1)

    def clear(self):
        for way in range(2):
            got = self.refs[way][1]

            @pl.when(self.far[way] == 0)
            def _():
                got[...] = jnp.zeros_like(got)

    def begin(self, k):
        for way in range(2):

            @pl.when(self.far[way] == 0)
            def _():
                self.copy(way, self.refs[way][0], k).start()

    def relay(self, way, k, low, high):
        own, got, out, _, _ = self.refs[way]

        @pl.when((self.far[way] > 0) & (k >= low) & (k < high))
        def _():
            self.copy(way, out, k).wait_recv()

            @pl.when(self.far[way] < self.blocks - 1)
            def _():
                for q in range(self.size):
                    at = k * self.size + q
                    out[at] = own[at] + self.step[...] * got[at]
                self.copy(way, out, k).start()

    def finish(self, pieces):
        for way in range(2):

            @pl.when(self.far[way] < self.blocks - 1)
            def _():
                def one(k, carry):
                    self.copy(way, self.refs[way][2], k).wait_send()
                    return carry

                lax.fori_loop(0, pieces, one, 0)


def trace_problem(b, modes, up, down, rims, single, tables, pay, *, here):
    rows, cols = up.shape[1], up.shape[2]
    width = pay.shape[3]
    parts = cols // width
    lane = lax.broadcasted_iota(jnp.int32, (1, cols), 1)
    parity = lax.broadcasted_iota(jnp.int32, (8, cols), 0) % 2 == 0
    total = [jnp.zeros((8, cols), f32) for _ in range(here)]
    for c in range(rows // 8):
        cut = slice(c * 8, c * 8 + 8)
        ratio, weight = single[0, cut, :], single[3, cut, :]
        value = up[b, cut, :]
        sums = []
        for v in range(here):
            if v:
                value = ratio * value
            value = value + tables[v, cut, :] * modes[v, b, cut, :]
            sums.append(tables[here + 1 + v, cut, :] * value)
        behind = down[b, cut, :]
        for v in range(here, -1, -1):
            if v < here:
                total[v] = total[v] + weight * (sums[v] + tables[v, cut, :] * behind)
            behind = ratio * (behind + tables[here + 1 + v, cut, :] * modes[v, b, cut, :])

    def put(kind, v, row):
        for n in range(parts):
            pay[b * parts + n, kind, v : v + 1, :] = row[:, n * width : (n + 1) * width]

    for v in range(here):
        even = jnp.sum(jnp.where(parity, total[v], 0.0), axis=0, keepdims=True)
        odd = jnp.sum(jnp.where(parity, 0.0, total[v]), axis=0, keepdims=True)
        put(0, v, even + odd)
        put(1, v, even - odd + rims[b, v : v + 1, :])
        flat = jnp.where(lane == 0, modes[v, b, 0:1, :], 0.0)
        if v == 0:
            beyond = pltpu.roll(modes[here, b, 0:8, :], 1, 1)[0:1]
            flat = flat + jnp.where(lane == 1, beyond, 0.0)
        put(2, v, flat)


def sweep_problem(b, modes, flux, up1, up2, down1, down2, single, tables, wave, *, here, levels):
    rows, cols = up1.shape[1], up1.shape[2]
    first = lax.axis_index("py") * here
    for c in range(rows // 8):
        cut = slice(c * 8, c * 8 + 8)
        ratio, scale, edge = single[0, cut, :], single[2, cut, :], single[4, cut, :]
        sign = jnp.where(
            lax.broadcasted_iota(jnp.int32, (8, cols), 0) % 2 == 0, edge, -edge
        )
        value = up1[b, cut, :] + up2[b, cut, :]
        source, sums = [], []
        for v in range(here + 1):
            now = modes[v, b, cut, :]
            if v < here:
                mine = jnp.broadcast_to(flux[b, v : v + 1, :], (8, cols))
                other = jnp.broadcast_to(flux[b, here + v : here + v + 1, :], (8, cols))
                now = now + (sign * mine - edge * other)
            source.append(now)
            if v:
                value = ratio * value
            value = value + tables[v, cut, :] * now
            sums.append(tables[here + 1 + v, cut, :] * value)
        behind = down1[b, cut, :] + down2[b, cut, :]
        for v in range(here, -1, -1):
            wave[v, b, cut, :] = scale * (sums[v] + tables[v, cut, :] * behind)
            behind = ratio * (behind + tables[here + 1 + v, cut, :] * source[v])
        if c == 0:
            spot = (lax.broadcasted_iota(jnp.int32, (8, 128), 0) == 0) & (
                lax.broadcasted_iota(jnp.int32, (8, 128), 1) == 0
            )
            below = 0.5 * (up1[b, 0:8, 0:128] + up2[b, 0:8, 0:128])
            whole = below + 0.5 * (down1[b, 0:8, 0:128] + down2[b, 0:8, 0:128])
            for v in range(here + 1):
                whole = whole + source[v][:, 0:128]
            mean = whole * (1.0 / levels)
            level_value = jnp.zeros((8, 128), f32)
            for v in range(here + 1):
                wave[v, b, 0:8, 0:128] = jnp.where(spot, level_value, wave[v, b, 0:8, 0:128])
                if v < here:
                    below = below + source[v][:, 0:128]
                    count = (first + (v + 1)).astype(f32)
                    level_value = level_value - (below - count * mean)


def flux_problem(b, flux, tables, up, down, *, here):
    rows, cols = up.shape[1], up.shape[2]
    sign = jnp.where(lax.broadcasted_iota(jnp.int32, (rows, cols), 0) % 2 == 0, 1.0, -1.0)
    base = 2 * (here + 1)
    rise = jnp.zeros((rows, cols), f32)
    fall = jnp.zeros((rows, cols), f32)
    for v in range(here):
        mine = jnp.broadcast_to(flux[b, v : v + 1, :], (rows, cols))
        other = jnp.broadcast_to(flux[b, here + v : here + v + 1, :], (rows, cols))
        both = sign * mine - other
        rise = rise + tables[base + v] * both
        fall = fall + tables[base + here + v] * both
    up[b] = rise
    down[b] = fall


def flat_rows(ref, kind, here):
    devices, width = ref.shape[0], ref.shape[3]
    if here % 8 == 0:
        return ref[:, kind].reshape(devices * here, width)
    return jnp.concatenate([ref[i, kind] for i in range(devices)], axis=0)


SCRATCH = (
    "mult", "aux", "start", "end", "col", "row", "home", "single", "ahead", "after", "mix",
    "mix_back", "ring",
    "prev", "body", "spread", "tail", "rims", "modes", "pay", "recv", "back", "came", "flux",
    "own_up1", "own_down1", "got_up1", "got_down1", "out_up1", "out_down1",
    "own_up2", "own_down2", "got_up2", "got_down2", "out_up2", "out_down2",
    "streamed", "fetched", "moved",
    "sent_up1", "sent_down1", "came_up1", "came_down1",
    "sent_up2", "sent_down2", "came_up2", "came_down2",
    "sent1", "came1", "sent2", "came2", "sent3", "came3",
)


def loop(low, high, action, unroll=1):
    def one(i, carry):
        action(i)
        return carry

    if not (isinstance(low, int) and isinstance(high, int) and high <= low):
        lax.fori_loop(low, high, one, 0, unroll=unroll)


def solve_kernel(
    mult_all, aux_all, start_all, end_all, col_all, row_all, home_all, single_all, ahead_all,
    after_all, mix_all, mix_back_all, ring_all, phi_all, edges, *scratch,
    levels, here, blocks, inner, pieces, delay, depth
):
    s = types.SimpleNamespace(**dict(zip(SCRATCH, scratch)))
    problems, rows, cols = s.start.shape
    devices, width = s.pay.shape[0], s.pay.shape[3]
    chunk, per, half = problems // 2, pieces // 2, devices // 2
    size = problems // pieces
    parts = cols // width
    reach = delay * (blocks - 1)
    me_py = lax.axis_index("py")
    me_space = lax.axis_index("grp") * inner + lax.axis_index("px")
    me = me_space * blocks + me_py
    my_half = me_space % 2
    my_chunk = my_half * half + (me_space // 2) * blocks + me_py
    tables, after = s.ahead, s.after

    def where(flat):
        return {
            "grp": flat // (inner * blocks),
            "px": flat // blocks % inner,
            "py": flat % blocks,
        }

    def solver(c):
        i = c % half
        return (2 * (i // blocks) + c // half) * blocks + i % blocks

    def chain(n):
        part = lambda name: getattr(s, name % n)
        return Chain(
            *((part("own_%s%%d" % way), part("got_%s%%d" % way), part("out_%s%%d" % way),
               part("sent_%s%%d" % way), part("came_%s%%d" % way)) for way in ("up", "down")),
            s.single.at[1], size, blocks,
        )

    chain1, chain2 = chain(1), chain(2)

    def relays(which, i, owner):
        for way in range(2):
            k = i - delay * which.far[way]
            which.relay(way, owner * per + k, owner * per, (owner + 1) * per)

    def stream(g):
        c, t, at = g // here, g % here, g % depth
        cut = pl.ds(c * chunk, chunk)
        return [
            pltpu.make_async_copy(mult_all.at[:, t, cut], s.mult.at[at], s.streamed.at[0, at]),
            pltpu.make_async_copy(aux_all.at[:, t, cut], s.aux.at[at], s.streamed.at[1, at]),
        ]

    pairs = [
        (start_all, s.start), (end_all, s.end), (col_all, s.col), (row_all, s.row),
        (single_all, s.single), (ahead_all.at[me_py], s.ahead), (after_all.at[me_py], s.after),
        (mix_all, s.mix), (mix_back_all, s.mix_back), (ring_all.at[:, my_chunk % parts], s.ring),
        (home_all, s.home),
    ]
    fetches = [pltpu.make_async_copy(x, y, s.fetched.at[i]) for i, (x, y) in enumerate(pairs)]
    early = 6
    for g in range(min(depth, 2 * here)):
        for copy in stream(g):
            copy.start()
        if g == 0:
            for fetch in fetches[:early]:
                fetch.start()
    for fetch in fetches[early:]:
        fetch.start()
    barrier = pltpu.get_barrier_semaphore()

    def hail(i):
        pl.semaphore_signal(
            barrier, inc=1, device_id=where((me + i) % devices), device_id_type=MESH
        )

    loop(1, devices, hail)
    chain1.clear()
    chain2.clear()

    @pl.when(my_chunk % parts != 0)
    def _():
        s.recv[:, 2] = jnp.zeros((devices, here, width), f32)

    for fetch in fetches[:early]:
        fetch.wait()
    row = lax.broadcasted_iota(jnp.int32, (rows, cols), 0)

    def across_rows(c, v):
        base = c * chunk
        s.modes[v, base : base + chunk] = over_rows(s.row, s.spread[...])
        ratio, low, falling = s.single[0], tables[v], tables[2 * (here + 1) + v]
        for b in range(base, base + chunk):
            value = s.modes[v, b]
            s.own_up1[b] = ratio * s.own_up1[b] + low * value
            s.own_down1[b] = s.own_down1[b] + falling * value

    def across_cols(values):
        flat = values[...].reshape(chunk * rows, cols)
        s.spread[...] = times_table(flat, s.col).reshape(chunk, rows, cols)

    def source(c, t):
        g = c * here + t
        at = g % depth
        level = me_py * here + t
        for copy in stream(g):
            copy.wait()
        across_rows(c, jnp.maximum(t - 1, 0))
        keep = jnp.where(level == levels - 1, 0.0, 1.0)
        begin = jnp.where(level == 0, -1.0 / PENALTY, 0.0)
        finish = jnp.where(level == levels - 1, 1.0 / PENALTY, 0.0)
        for b in range(chunk):
            along = s.aux[at, 1, b] - s.mult[at, 1, b] / PENALTY
            s.tail[b, pl.ds(t, 1), :] = along[rows - 1 :, :]
            beside = jnp.where(row == 0, 0.0, pltpu.roll(along, 1, 0))
            along = jnp.where(row == rows - 1, 0.0, along)
            second = s.aux[at, 2, b] - s.mult[at, 2, b] / PENALTY
            side = pltpu.roll(second, 1, 1) - second
            now = (s.aux[at, 0, b] - s.mult[at, 0, b] / PENALTY) * keep
            boundary = begin * s.start[c * chunk + b] + finish * s.end[c * chunk + b]
            s.body[b] = s.prev[b] - now + beside - along + side + boundary
            s.prev[b] = now
        across_cols(s.body)

        @pl.when(g + depth < 2 * here)
        def _():
            for copy in stream(g + depth):
                copy.start()

        if c == 1:
            relays(chain1, t + 1, 0)

    for c in range(2):
        cut = slice(c * chunk, c * chunk + chunk)
        s.prev[...] = jnp.zeros_like(s.prev)
        s.tail[...] = jnp.zeros_like(s.tail)
        s.spread[...] = jnp.zeros_like(s.spread)
        s.own_up1[cut] = jnp.zeros((chunk, rows, cols), f32)
        s.own_down1[cut] = jnp.zeros((chunk, rows, cols), f32)
        loop(0, here, functools.partial(source, c))
        across_rows(c, here - 1)
        across_cols(s.prev)
        across_rows(c, here)
        held = s.tail.shape[1]
        if c == 0:
            pl.semaphore_wait(barrier, devices - 1)
        loop(c * per, (c + 1) * per, chain1.begin)
        if c == 1:
            relays(chain1, here + 1, 0)
        flat = s.tail[...].reshape(chunk * held, cols)
        s.rims[cut] = times_table(flat, s.col).reshape(chunk, held, cols)

    def question(c, flat, source, target):
        kinds = pl.ds(2, 1) if flat else pl.ds(0, 2)
        return pltpu.make_async_remote_copy(
            src_ref=s.pay.at[c, kinds], dst_ref=s.recv.at[source, kinds],
            send_sem=(s.sent3 if flat else s.sent1).at[c],
            recv_sem=(s.came3 if flat else s.came1).at[source],
            device_id=where(target), device_id_type=MESH,
        )

    def ask(c, flat):
        other = solver(c)

        @pl.when(other == me)
        def _():
            s.recv[me] = s.pay[c]

        @pl.when(other != me)
        def _():
            question(c, False, me, other).start()
            if flat:
                question(c, True, me, other).start()

    def trace(k):
        def one(b):
            trace_problem(
                b, s.modes, s.got_up1, s.got_down1, s.rims, s.single, tables, s.pay, here=here
            )
            for n in range(parts):
                ask(b * parts + n, n == 0)

        loop(k * size, k * size + size, one)

    def answer(i):
        other = (me + i) % devices
        return pltpu.make_async_remote_copy(
            src_ref=s.back.at[other], dst_ref=s.came.at[my_chunk], send_sem=s.sent2.at[i],
            recv_sem=s.came2.at[my_chunk], device_id=where(other), device_id_type=MESH,
        )

    def solve_ring(h):
        @pl.when(my_half == h)
        def _():
            def arrive(i):
                other = (me + i) % devices
                question(0, False, other, other).wait_recv()

                @pl.when(my_chunk % parts == 0)
                def _():
                    question(0, True, other, other).wait_recv()

            loop(1, devices, arrive)
            total = devices * here
            lane = lax.broadcasted_iota(jnp.int32, (total, width), 1)
            ahead = total - levels
            jump = pltpu.roll(flat_rows(s.recv, 0, here), ahead, 0) - flat_rows(s.recv, 1, here)
            flat = flat_rows(s.recv, 2, here)
            beyond = pltpu.roll(pltpu.roll(flat, here, 0), width - 1, 1)
            whole = jnp.where(lane == 0, flat + beyond, 0.0)
            jump_flat = pltpu.roll(whole, ahead, 0) - whole
            both = table_times(s.mix, jnp.concatenate([jump, jump_flat], axis=1))
            solved = both[:, :width] * s.ring[0] + both[:, width:] * s.ring[1]
            mine = table_times(s.mix_back, solved)
            other = pltpu.roll(mine, levels, 0)
            if here % 8 == 0:
                s.back[:, 0] = mine.reshape(devices, here, width)
                s.back[:, 1] = other.reshape(devices, here, width)
            else:
                for i in range(devices):
                    s.back[i, 0] = mine[i * here : (i + 1) * here]
                    s.back[i, 1] = other[i * here : (i + 1) * here]
            loop(1, devices, lambda i: answer(i).start())
            s.came[my_chunk] = s.back[me]

    def fluxes(h):
        def arrive(c):
            other = solver(c)

            @pl.when(other != me)
            def _():
                pltpu.make_async_remote_copy(
                    src_ref=s.back.at[0], dst_ref=s.came.at[c], send_sem=s.sent2.at[0],
                    recv_sem=s.came2.at[c], device_id=where(other), device_id_type=MESH,
                ).wait_recv()

        loop(h * half, (h + 1) * half, arrive)
        for c in range(h * half, (h + 1) * half):
            b, n = c // parts, c % parts
            for kind in range(2):
                s.flux[b, kind * here : (kind + 1) * here, n * width : (n + 1) * width] = (
                    s.came[c, kind]
                )

        def own(k):
            loop(k * size, k * size + size, lambda b: flux_problem(
                b, s.flux, after, s.own_up2, s.own_down2, here=here))
            chain2.begin(k)

        loop(h * per, (h + 1) * per, own)

    def send_out(k):
        cut = pl.ds(k * size, size)
        return pltpu.make_async_copy(
            s.modes.at[pl.ds(0, here), cut], phi_all.at[pl.ds(0, here), cut], s.moved.at[k]
        )

    def send_tip(h):
        cut = pl.ds(h * chunk, chunk)
        return pltpu.make_async_copy(
            s.modes.at[here, cut], phi_all.at[here, cut], s.moved.at[pieces + h]
        )

    def sweep(k):
        loop(k * size, k * size + size, lambda b: sweep_problem(
            b, s.modes, s.flux, s.got_up1, s.got_up2, s.got_down1, s.got_down2, s.single, after,
            s.modes, here=here, levels=levels))
        cut = pl.ds(k * size, size)
        part = over_rows(s.home, s.modes[0:here, cut].reshape(here * size, rows, cols))
        part = times_table(part.reshape(here * size * rows, cols), s.col)
        s.modes[0:here, cut] = part.reshape(here, size, rows, cols)
        send_out(k).start()

    def tip(h):
        cut = slice(h * chunk, h * chunk + chunk)
        last = over_rows(s.home, s.modes[here, cut])
        last = times_table(last.reshape(chunk * rows, cols), s.col)
        s.modes[here, cut] = last.reshape(chunk, rows, cols)
        send_tip(h).start()

    def rim(h):
        cut = slice(h * chunk, h * chunk + chunk)
        if here % 8 == 0:
            flat = (s.flux[cut, 0:here, :] + s.rims[cut, 0:here, :]).reshape(chunk * here, cols)
            edges[cut] = times_table(flat, s.col).reshape(chunk, here, cols)
        else:
            for b in range(h * chunk, h * chunk + chunk):
                edges[b] = times_table(s.flux[b, 0:here, :] + s.rims[b, 0:here, :], s.col)

    filled = max(per, reach - 1)

    def drain1(i):
        relays(chain1, i, 1)

        @pl.when(i <= per)
        def _():
            trace(i - 1)

    def drain2(k):
        @pl.when(reach + k > filled)
        def _():
            relays(chain1, reach + k, 1)

        trace(per + k)

    def asked(c):
        other = solver(c)

        @pl.when(other != me)
        def _():
            question(c, False, me, other).wait_send()

            @pl.when(c % parts == 0)
            def _():
                question(c, True, me, other).wait_send()

    loop(here + 2, reach, lambda i: relays(chain1, i, 0))
    def traces0(k):
        @pl.when(reach + k >= here + 2)
        def _():
            relays(chain1, reach + k, 0)

        trace(k)

    loop(0, per, traces0)
    for fetch in fetches[early:]:
        fetch.wait()
    loop(1, reach, lambda i: relays(chain1, i, 1))
    solve_ring(0)
    def traces1(k):
        @pl.when(reach + k >= reach)
        def _():
            relays(chain1, reach + k, 1)

        trace(per + k)

    loop(0, per, traces1)
    fluxes(0)
    solve_ring(1)
    loop(1, reach - 2, lambda i: relays(chain2, i, 0))
    fluxes(1)
    loop(reach - 2, reach + 1, lambda i: relays(chain2, i, 0))
    loop(reach + 1, reach + per, lambda i: relays(chain2, i, 0))
    def drain3(i):
        relays(chain2, i, 1)

        @pl.when(i <= per)
        def _():
            sweep(i - 1)

    loop(1, reach, drain3)
    loop(max(reach, 1), per + 1, lambda i: sweep(i - 1))
    tip(0)
    rim(0)
    rim(1)
    chain1.finish(pieces)
    loop(0, devices, asked)
    loop(1, devices, lambda i: answer(i).wait_send())
    def sweeps1(k):
        @pl.when(reach + k >= reach)
        def _():
            relays(chain2, reach + k, 1)

        sweep(per + k)

    loop(0, per, sweeps1)
    tip(1)

    chain2.finish(pieces)
    loop(0, pieces, lambda k: send_out(k).wait())
    for h in range(2):
        send_tip(h).wait()


def project_kernel(first, following, edges, mult, next_mult, next_aux, phi, *, levels):
    t = pl.program_id(0)
    here = pl.num_programs(0)
    _, problems, rows, cols = first.shape

    @pl.when(t == 0)
    def _():
        phi[...] = first[0]

    moving = jnp.where(lax.axis_index("py") * here + t == levels - 1, 0.0, 1.0)
    row = lax.broadcasted_iota(jnp.int32, (rows, cols), 0)

    def one(b, carry):
        here_phi = phi[b]
        next_phi = following[0, b]
        phi[b] = next_phi
        rim = jnp.broadcast_to(edges[b, pl.ds(t, 1), :], (rows, cols))
        grad_time = (next_phi - here_phi) * moving
        grad_first = jnp.where(
            row == rows - 1, rim, pltpu.roll(here_phi, rows - 1, 0) - here_phi
        )
        grad_second = pltpu.roll(here_phi, cols - 1, 1) - here_phi
        mult_time, mult_first, mult_second = (mult[k, 0, b] for k in range(3))
        time_part = grad_time + mult_time / PENALTY
        along = grad_first + mult_first / PENALTY
        beside = grad_second + mult_second / PENALTY
        kinetic = 0.5 * (along * along + beside * beside)
        offset_one = 1.0 + time_part
        solid = kinetic > 1e-37
        root = jnp.exp(jnp.log(jnp.where(solid, kinetic, 1.0)) * (1.0 / 3.0))
        scaling = jnp.maximum(offset_one, 1.0) + jnp.where(solid, root, 0.0)
        twice = 2.0 * offset_one
        for newton_step in range(NEWTON):
            above = scaling * scaling * (2.0 * scaling - offset_one) + kinetic
            derivative = scaling * (3.0 * scaling - twice)
            scaling = jnp.maximum(above / derivative, 1.0)
        feasible = time_part + kinetic <= 0.0
        shrink = jnp.where(feasible, 1.0, 1.0 / scaling)
        out_time = jnp.where(feasible, time_part, time_part - (scaling - 1.0))
        out_along = along * shrink
        out_beside = beside * shrink
        next_aux[0, 0, b] = out_time
        next_aux[1, 0, b] = out_along
        next_aux[2, 0, b] = out_beside
        next_mult[0, 0, b] = mult_time + PENALTY * (grad_time - out_time)
        next_mult[1, 0, b] = mult_first + PENALTY * (grad_first - out_along)
        next_mult[2, 0, b] = mult_second + PENALTY * (grad_second - out_beside)
        return carry

    lax.fori_loop(0, problems, one, 0, unroll=4)


def params(which=None):
    if which is None:
        return pltpu.CompilerParams(vmem_limit_bytes=VMEM_LIMIT)
    return pltpu.CompilerParams(
        collective_id=which, has_side_effects=True, vmem_limit_bytes=VMEM_LIMIT
    )


def whole_block(shape):
    return pl.BlockSpec(shape, lambda *_: (0,) * len(shape))


def local(multiplier, auxiliary, density_start, density_end):
    _, here, problems, rows, cols = multiplier.shape
    blocks = lax.axis_size("py")
    inner = lax.axis_size("px")
    group = lax.axis_size("grp") * inner
    devices = group * blocks
    levels = here * blocks
    held = -(-here // 8) * 8
    width = problems * cols // devices
    parts = cols // width
    total = devices * here
    delay, depth = 3, 4
    chunk = problems // 2
    pieces = 2 * math.gcd(chunk, 4)
    size = problems // pieces
    fit = max(1, 256 // rows)
    shape = lambda *dims: jax.ShapeDtypeStruct(dims, f32)
    vector = lambda *dims: pltpu.VMEM(dims, f32)
    anywhere = pl.BlockSpec(memory_space=pl.ANY)
    dma = lambda *dims: pltpu.SemaphoreType.DMA(dims)

    col_table = halves(hartley(cols))
    row_table = halves(np.kron(np.eye(math.gcd(chunk, fit)), cosines(rows)))
    row_back = halves(np.kron(np.eye(math.gcd(math.gcd(size * here, chunk), fit)), cosines(rows).T))
    single, ahead, after = slab_tables(rows, cols, here, blocks)
    mix, inverse, extra = ring_tables(rows, cols, group, levels)
    wide = np.zeros((total, cols), np.float32)
    wide[:, :1] = extra
    ring = np.stack([inverse, wide]).reshape(2, total, parts, width).transpose(0, 2, 1, 3).copy()
    mix_back = halves(mix.T.astype(np.float64))
    mix = halves(mix.astype(np.float64))
    tables = [col_table, row_table, row_back, single, ahead, after, mix, mix_back, ring]

    plane = (problems, rows, cols)
    part = (chunk, rows, cols)
    table = lambda x: pltpu.VMEM(x.shape, x.dtype)
    scratch = [
        vector(depth, 3, *part), vector(depth, 3, *part), vector(*plane), vector(*plane),
        table(col_table), table(row_table), table(row_back), table(single), table(ahead[0]),
        table(after[0]), table(mix), table(mix), table(ring[:, 0]),
        vector(*part), vector(*part), vector(*part), vector(chunk, held, cols),
        vector(problems, held, cols),
        vector(here + 1, *plane), vector(devices, 3, here, width),
        vector(devices, 3, here, width), vector(devices, 2, here, width),
        vector(devices, 2, here, width), vector(problems, 2 * here, cols),
    ] + [vector(*plane)] * 12 + [dma(2, depth), dma(11), dma(pieces + 2)]
    scratch += [dma(pieces)] * 8 + [dma(devices)] * 6
    phi, edges = pl.pallas_call(
        functools.partial(solve_kernel, levels=levels, here=here, blocks=blocks, inner=inner,
                          pieces=pieces, delay=delay, depth=depth),
        out_shape=(shape(here + 1, *plane), shape(problems, here, cols)),
        in_specs=[anywhere] * 13,
        out_specs=(anywhere, pl.BlockSpec(memory_space=pltpu.VMEM)),
        scratch_shapes=scratch,
        compiler_params=params(0),
        name="solve",
    )(multiplier, auxiliary, density_start, density_end, *(jnp.asarray(x) for x in tables))

    out_shape = shape(*multiplier.shape)
    level_block = pl.BlockSpec((3, 1, *plane), lambda t: (0, t, 0, 0, 0))
    phi_block = whole_block((1, *plane))
    next_block = pl.BlockSpec((1, *plane), lambda t: (t + 1, 0, 0, 0))
    return pl.pallas_call(
        functools.partial(project_kernel, levels=levels),
        out_shape=(out_shape, out_shape),
        grid=(here,),
        in_specs=[phi_block, next_block, whole_block(edges.shape), level_block],
        out_specs=(level_block, level_block),
        scratch_shapes=[vector(*plane)],
        compiler_params=params(),
        name="project",
    )(phi, phi, edges, multiplier)


def solution(mesh):
    placed = (
        P(None, "py", None, ("grp", "px"), None),
        P(None, "py", None, ("grp", "px"), None),
        P(None, ("grp", "px"), None),
        P(None, ("grp", "px"), None),
    )
    return jax.shard_map(
        local,
        mesh=mesh,
        in_specs=placed,
        out_specs=(
            P(None, "py", None, ("grp", "px"), None),
            P(None, "py", None, ("grp", "px"), None),
        ),
        check_vma=False,
    )
```

```python
import functools
import math
import types

import jax
import jax.numpy as jnp
import ml_dtypes
import numpy as np
from jax import lax
from jax.experimental import pallas as pl
from jax.experimental.pallas import tpu as pltpu
from jax.sharding import PartitionSpec as P

NEWTON = 4
PENALTY = 1.0
VMEM_LIMIT = 60 * 1024 * 1024
SPACE = ("grp", "px")
EVERY = ("grp", "px", "py")
MESH = pl.DeviceIdType.MESH
bf16 = jnp.bfloat16
f32 = jnp.float32


def halves(table):
    high = table.astype(ml_dtypes.bfloat16)
    low = (table - high.astype(np.float64)).astype(ml_dtypes.bfloat16)
    return np.stack([high, low])


def hartley(length):
    angles = 2.0 * np.pi / length * (np.outer(np.arange(length), np.arange(length)) % length)
    return (np.cos(angles) + np.sin(angles)) / np.sqrt(length)


def cosines(length):
    k = np.arange(length)[:, None]
    x = np.arange(length)[None, :]
    weights = np.where(k == 0, np.sqrt(1.0 / length), np.sqrt(2.0 / length))
    return weights * np.cos(np.pi * k * (2 * x + 1) / (2 * length))


def slab_tables(rows, cols, here, blocks):
    j = np.arange(rows)[:, None]
    n = np.arange(cols)[None, :]
    lam = 4.0 * np.sin(np.pi * j / (2 * rows)) ** 2 + 4.0 * np.sin(np.pi * n / cols) ** 2
    sinh = np.sqrt(lam * (1.0 + 0.25 * lam))
    ratio = 1.0 / (1.0 + 0.5 * lam + sinh)
    positive = lam > 0.0
    full = ratio ** (2 * here * blocks)
    scale = np.where(positive, 0.5 / np.where(positive, sinh * (1.0 - full), 1.0), 0.0)
    edge = cosines(rows)[:, :1]
    low, high, down, low_q, high_q = [], [], [], [], []
    for block in range(blocks):
        first = block * here
        lows = [1.0 + ratio ** (2 * (first + v) + 1) for v in range(here + 1)]
        highs = [1.0 + ratio ** (2.0 * (blocks * here - 1 - first - v) + 1.0) for v in range(here + 1)]
        low.append(lows)
        high.append(highs)
        down.append([ratio**v * highs[v] for v in range(here + 1)])
        low_q.append([edge * ratio ** (here - v) * lows[v] for v in range(here)])
        high_q.append([edge * ratio**v * highs[v] for v in range(here)])
    single = np.stack([ratio, ratio**here, scale, edge * scale, np.broadcast_to(edge, lam.shape)])
    pack = lambda parts: np.asarray(parts, np.float32)
    ahead = np.concatenate([pack(low), pack(high), pack(down)], axis=1)
    after = np.concatenate([pack(low), pack(high), pack(low_q), pack(high_q)], axis=1)
    return single.astype(np.float32), ahead, after


def ring_tables(rows, cols, group, levels):
    r = np.arange(group)[:, None, None]
    k = np.arange(levels)[None, :, None]
    n = np.arange(cols)[None, None, :]
    tau = 4.0 * np.sin(np.pi * k / (2 * levels)) ** 2
    kappa = tau + 4.0 * np.sin(np.pi * n / cols) ** 2
    turn = 2.0 * np.sin(np.pi * r / group) ** 2
    positive = kappa > 0.0
    safe = np.where(positive, kappa, 1.0)
    shrink = 1.0 / (1.0 + 0.5 * safe + np.sqrt(safe * (1.0 + 0.25 * safe)))
    far = shrink**rows
    inverse = (1.0 - shrink) * (1.0 - far * far) / (
        (1.0 + shrink) * ((1.0 - far) ** 2 + 2.0 * far * turn)
    )
    inverse = np.where(positive, inverse, np.where(r == 0, 1.0 / rows, 0.0))
    edge = math.sqrt(1.0 / rows)
    flat = inverse[:, :, :1]
    moving = edge * flat / np.where(tau > 0.0, tau, 1.0)
    still = rows * edge / np.where(r > 0, 2.0 * turn, 1.0) * (r > 0)
    extra = np.where(tau > 0.0, moving, still)
    mix = np.kron(hartley(group), cosines(levels))
    flat_rows = group * levels
    return (
        mix,
        inverse.reshape(flat_rows, cols).astype(np.float32),
        extra.reshape(flat_rows, 1).astype(np.float32),
    )


def split(x):
    high = x.astype(bf16)
    return high, (x - high.astype(f32)).astype(bf16)


def mm(a, b):
    return jnp.dot(a, b, preferred_element_type=f32)


def times_table(x, table):
    high, low = split(x)
    return mm(high, table[0]) + (mm(low, table[0]) + mm(high, table[1]))


def table_times(table, x):
    high, low = split(x)
    return mm(table[0], high) + (mm(table[0], low) + mm(table[1], high))


def over_rows(table, x):
    units, rows, cols = x.shape
    size = table.shape[1]
    bunch = size // rows
    parts = []
    for g in range(units // bunch):
        part = x[g * bunch : (g + 1) * bunch].reshape(size, cols)
        parts.append(table_times(table, part).reshape(bunch, rows, cols))
    return parts[0] if len(parts) == 1 else jnp.concatenate(parts, axis=0)


def steps_from(me, blocks):
    return me, blocks - 1 - me


class Chain:
    def __init__(self, up, down, step, size, blocks):
        self.me = lax.axis_index("py")
        self.blocks, self.size, self.step = blocks, size, step
        self.far = steps_from(self.me, blocks)
        self.next = ((self.me + 1) % blocks, (self.me + blocks - 1) % blocks)
        self.refs = (up, down)

    def copy(self, way, source, k):
        _, got, _, sent, came = self.refs[way]
        cut = pl.ds(k * self.size, self.size)
        return pltpu.make_async_remote_copy(
            src_ref=source.at[cut],
            dst_ref=got.at[cut],
            send_sem=sent.at[k],
            recv_sem=came.at[k],
            device_id={"py": self.next[way]},
            device_id_type=MESH,
        )

    def greet(self):
        barrier = pltpu.get_barrier_semaphore()
        lower, upper = self.me > 0, self.me < self.blocks - 1

        @pl.when(lower)
        def _():
            pl.semaphore_signal(barrier, inc=1, device_id={"py": self.me - 1}, device_id_type=MESH)

        @pl.when(upper)
        def _():
            pl.semaphore_signal(barrier, inc=1, device_id={"py": self.me + 1}, device_id_type=MESH)

        @pl.when(lower & upper)
        def _():
            pl.semaphore_wait(barrier, 2)

        @pl.when(jnp.logical_not(lower & upper))
        def _():
            pl.semaphore_wait(barrier, 1)

    def clear(self):
        for way in range(2):
            got = self.refs[way][1]

            @pl.when(self.far[way] == 0)
            def _():
                got[...] = jnp.zeros_like(got)

    def begin(self, k):
        for way in range(2):

            @pl.when(self.far[way] == 0)
            def _():
                self.copy(way, self.refs[way][0], k).start()

    def relay(self, way, k, low, high):
        own, got, out, _, _ = self.refs[way]

        @pl.when((self.far[way] > 0) & (k >= low) & (k < high))
        def _():
            self.copy(way, out, k).wait_recv()

            @pl.when(self.far[way] < self.blocks - 1)
            def _():
                for q in range(self.size):
                    at = k * self.size + q
                    out[at] = own[at] + self.step[...] * got[at]
                self.copy(way, out, k).start()

    def finish(self, pieces):
        for way in range(2):

            @pl.when(self.far[way] < self.blocks - 1)
            def _():
                def one(k, carry):
                    self.copy(way, self.refs[way][2], k).wait_send()
                    return carry

                lax.fori_loop(0, pieces, one, 0)


def trace_problem(b, modes, up, down, rims, single, tables, pay, *, here):
    rows, cols = up.shape[1], up.shape[2]
    width = pay.shape[3]
    parts = cols // width
    lane = lax.broadcasted_iota(jnp.int32, (1, cols), 1)
    parity = lax.broadcasted_iota(jnp.int32, (8, cols), 0) % 2 == 0
    total = [jnp.zeros((8, cols), f32) for _ in range(here)]
    for c in range(rows // 8):
        cut = slice(c * 8, c * 8 + 8)
        ratio, weight = single[0, cut, :], single[3, cut, :]
        value = up[b, cut, :]
        sums = []
        for v in range(here):
            if v:
                value = ratio * value
            value = value + tables[v, cut, :] * modes[v, b, cut, :]
            sums.append(tables[here + 1 + v, cut, :] * value)
        behind = down[b, cut, :]
        for v in range(here, -1, -1):
            if v < here:
                total[v] = total[v] + weight * (sums[v] + tables[v, cut, :] * behind)
            behind = ratio * (behind + tables[here + 1 + v, cut, :] * modes[v, b, cut, :])

    def put(kind, v, row):
        for n in range(parts):
            pay[b * parts + n, kind, v : v + 1, :] = row[:, n * width : (n + 1) * width]

    for v in range(here):
        even = jnp.sum(jnp.where(parity, total[v], 0.0), axis=0, keepdims=True)
        odd = jnp.sum(jnp.where(parity, 0.0, total[v]), axis=0, keepdims=True)
        put(0, v, even + odd)
        put(1, v, even - odd + rims[b, v : v + 1, :])
        flat = jnp.where(lane == 0, modes[v, b, 0:1, :], 0.0)
        if v == 0:
            beyond = pltpu.roll(modes[here, b, 0:8, :], 1, 1)[0:1]
            flat = flat + jnp.where(lane == 1, beyond, 0.0)
        put(2, v, flat)


def sweep_problem(b, modes, flux, up1, up2, down1, down2, single, tables, wave, *, here, levels):
    rows, cols = up1.shape[1], up1.shape[2]
    first = lax.axis_index("py") * here
    for c in range(rows // 8):
        cut = slice(c * 8, c * 8 + 8)
        ratio, scale, edge = single[0, cut, :], single[2, cut, :], single[4, cut, :]
        sign = jnp.where(
            lax.broadcasted_iota(jnp.int32, (8, cols), 0) % 2 == 0, edge, -edge
        )
        value = up1[b, cut, :] + up2[b, cut, :]
        source, sums = [], []
        for v in range(here + 1):
            now = modes[v, b, cut, :]
            if v < here:
                mine = jnp.broadcast_to(flux[b, v : v + 1, :], (8, cols))
                other = jnp.broadcast_to(flux[b, here + v : here + v + 1, :], (8, cols))
                now = now + (sign * mine - edge * other)
            source.append(now)
            if v:
                value = ratio * value
            value = value + tables[v, cut, :] * now
            sums.append(tables[here + 1 + v, cut, :] * value)
        behind = down1[b, cut, :] + down2[b, cut, :]
        for v in range(here, -1, -1):
            wave[v, b, cut, :] = scale * (sums[v] + tables[v, cut, :] * behind)
            behind = ratio * (behind + tables[here + 1 + v, cut, :] * source[v])
        if c == 0:
            spot = (lax.broadcasted_iota(jnp.int32, (8, 128), 0) == 0) & (
                lax.broadcasted_iota(jnp.int32, (8, 128), 1) == 0
            )
            below = 0.5 * (up1[b, 0:8, 0:128] + up2[b, 0:8, 0:128])
            whole = below + 0.5 * (down1[b, 0:8, 0:128] + down2[b, 0:8, 0:128])
            for v in range(here + 1):
                whole = whole + source[v][:, 0:128]
            mean = whole * (1.0 / levels)
            level_value = jnp.zeros((8, 128), f32)
            for v in range(here + 1):
                wave[v, b, 0:8, 0:128] = jnp.where(spot, level_value, wave[v, b, 0:8, 0:128])
                if v < here:
                    below = below + source[v][:, 0:128]
                    count = (first + (v + 1)).astype(f32)
                    level_value = level_value - (below - count * mean)


def flux_problem(b, flux, tables, up, down, *, here):
    rows, cols = up.shape[1], up.shape[2]
    sign = jnp.where(lax.broadcasted_iota(jnp.int32, (rows, cols), 0) % 2 == 0, 1.0, -1.0)
    base = 2 * (here + 1)
    rise = jnp.zeros((rows, cols), f32)
    fall = jnp.zeros((rows, cols), f32)
    for v in range(here):
        mine = jnp.broadcast_to(flux[b, v : v + 1, :], (rows, cols))
        other = jnp.broadcast_to(flux[b, here + v : here + v + 1, :], (rows, cols))
        both = sign * mine - other
        rise = rise + tables[base + v] * both
        fall = fall + tables[base + here + v] * both
    up[b] = rise
    down[b] = fall


def flat_rows(ref, kind, here):
    devices, width = ref.shape[0], ref.shape[3]
    if here % 8 == 0:
        return ref[:, kind].reshape(devices * here, width)
    return jnp.concatenate([ref[i, kind] for i in range(devices)], axis=0)


SCRATCH = (
    "mult", "aux", "start", "end", "col", "row", "home", "single", "ahead", "after", "mix",
    "mix_back", "ring",
    "prev", "body", "spread", "tail", "rims", "modes", "pay", "recv", "back", "came", "flux",
    "own_up1", "own_down1", "got_up1", "got_down1", "out_up1", "out_down1",
    "own_up2", "own_down2", "got_up2", "got_down2", "out_up2", "out_down2",
    "streamed", "fetched", "moved",
    "sent_up1", "sent_down1", "came_up1", "came_down1",
    "sent_up2", "sent_down2", "came_up2", "came_down2",
    "sent1", "came1", "sent2", "came2", "sent3", "came3",
)


def loop(low, high, action, unroll=1):
    def one(i, carry):
        action(i)
        return carry

    if not (isinstance(low, int) and isinstance(high, int) and high <= low):
        lax.fori_loop(low, high, one, 0, unroll=unroll)


def solve_kernel(
    mult_all, aux_all, start_all, end_all, col_all, row_all, home_all, single_all, ahead_all,
    after_all, mix_all, mix_back_all, ring_all, phi_all, edges, *scratch,
    levels, here, blocks, inner, pieces, delay, depth
):
    s = types.SimpleNamespace(**dict(zip(SCRATCH, scratch)))
    problems, rows, cols = s.start.shape
    devices, width = s.pay.shape[0], s.pay.shape[3]
    chunk, per, half = problems // 2, pieces // 2, devices // 2
    size = problems // pieces
    parts = cols // width
    reach = delay * (blocks - 1)
    me_py = lax.axis_index("py")
    me_space = lax.axis_index("grp") * inner + lax.axis_index("px")
    me = me_space * blocks + me_py
    my_half = me_space % 2
    my_chunk = my_half * half + (me_space // 2) * blocks + me_py
    tables, after = s.ahead, s.after

    def where(flat):
        return {
            "grp": flat // (inner * blocks),
            "px": flat // blocks % inner,
            "py": flat % blocks,
        }

    def solver(c):
        i = c % half
        return (2 * (i // blocks) + c // half) * blocks + i % blocks

    def chain(n):
        part = lambda name: getattr(s, name % n)
        return Chain(
            *((part("own_%s%%d" % way), part("got_%s%%d" % way), part("out_%s%%d" % way),
               part("sent_%s%%d" % way), part("came_%s%%d" % way)) for way in ("up", "down")),
            s.single.at[1], size, blocks,
        )

    chain1, chain2 = chain(1), chain(2)

    def relays(which, i, owner):
        for way in range(2):
            k = i - delay * which.far[way]
            which.relay(way, owner * per + k, owner * per, (owner + 1) * per)

    def stream(g):
        c, t, at = g // here, g % here, g % depth
        cut = pl.ds(c * chunk, chunk)
        return [
            pltpu.make_async_copy(mult_all.at[:, t, cut], s.mult.at[at], s.streamed.at[0, at]),
            pltpu.make_async_copy(aux_all.at[:, t, cut], s.aux.at[at], s.streamed.at[1, at]),
        ]

    pairs = [
        (start_all, s.start), (end_all, s.end), (col_all, s.col), (row_all, s.row),
        (single_all, s.single), (ahead_all.at[me_py], s.ahead), (after_all.at[me_py], s.after),
        (mix_all, s.mix), (mix_back_all, s.mix_back), (ring_all.at[:, my_chunk % parts], s.ring),
        (home_all, s.home),
    ]
    fetches = [pltpu.make_async_copy(x, y, s.fetched.at[i]) for i, (x, y) in enumerate(pairs)]
    early = 6
    for g in range(min(depth, 2 * here)):
        for copy in stream(g):
            copy.start()
        if g == 0:
            for fetch in fetches[:early]:
                fetch.start()
    for fetch in fetches[early:]:
        fetch.start()
    barrier = pltpu.get_barrier_semaphore()

    def hail(i):
        pl.semaphore_signal(
            barrier, inc=1, device_id=where((me + i) % devices), device_id_type=MESH
        )

    loop(1, devices, hail)
    chain1.clear()
    chain2.clear()

    @pl.when(my_chunk % parts != 0)
    def _():
        s.recv[:, 2] = jnp.zeros((devices, here, width), f32)

    for fetch in fetches[:early]:
        fetch.wait()
    row = lax.broadcasted_iota(jnp.int32, (rows, cols), 0)

    def across_rows(c, v):
        base = c * chunk
        s.modes[v, base : base + chunk] = over_rows(s.row, s.spread[...])
        ratio, low, falling = s.single[0], tables[v], tables[2 * (here + 1) + v]
        for b in range(base, base + chunk):
            value = s.modes[v, b]
            s.own_up1[b] = ratio * s.own_up1[b] + low * value
            s.own_down1[b] = s.own_down1[b] + falling * value

    def across_cols(values):
        flat = values[...].reshape(chunk * rows, cols)
        s.spread[...] = times_table(flat, s.col).reshape(chunk, rows, cols)

    def source(c, t):
        g = c * here + t
        at = g % depth
        level = me_py * here + t
        for copy in stream(g):
            copy.wait()
        across_rows(c, jnp.maximum(t - 1, 0))
        keep = jnp.where(level == levels - 1, 0.0, 1.0)
        begin = jnp.where(level == 0, -1.0 / PENALTY, 0.0)
        finish = jnp.where(level == levels - 1, 1.0 / PENALTY, 0.0)
        for b in range(chunk):
            along = s.aux[at, 1, b] - s.mult[at, 1, b] / PENALTY
            s.tail[b, pl.ds(t, 1), :] = along[rows - 1 :, :]
            beside = jnp.where(row == 0, 0.0, pltpu.roll(along, 1, 0))
            along = jnp.where(row == rows - 1, 0.0, along)
            second = s.aux[at, 2, b] - s.mult[at, 2, b] / PENALTY
            side = pltpu.roll(second, 1, 1) - second
            now = (s.aux[at, 0, b] - s.mult[at, 0, b] / PENALTY) * keep
            boundary = begin * s.start[c * chunk + b] + finish * s.end[c * chunk + b]
            s.body[b] = s.prev[b] - now + beside - along + side + boundary
            s.prev[b] = now
        across_cols(s.body)

        @pl.when(g + depth < 2 * here)
        def _():
            for copy in stream(g + depth):
                copy.start()

        if c == 1:
            relays(chain1, t + 1, 0)

    for c in range(2):
        cut = slice(c * chunk, c * chunk + chunk)
        s.prev[...] = jnp.zeros_like(s.prev)
        s.tail[...] = jnp.zeros_like(s.tail)
        s.spread[...] = jnp.zeros_like(s.spread)
        s.own_up1[cut] = jnp.zeros((chunk, rows, cols), f32)
        s.own_down1[cut] = jnp.zeros((chunk, rows, cols), f32)
        loop(0, here, functools.partial(source, c))
        across_rows(c, here - 1)
        across_cols(s.prev)
        across_rows(c, here)
        held = s.tail.shape[1]
        if c == 0:
            pl.semaphore_wait(barrier, devices - 1)
        loop(c * per, (c + 1) * per, chain1.begin)
        if c == 1:
            relays(chain1, here + 1, 0)
        flat = s.tail[...].reshape(chunk * held, cols)
        s.rims[cut] = times_table(flat, s.col).reshape(chunk, held, cols)

    def question(c, flat, source, target):
        kinds = pl.ds(2, 1) if flat else pl.ds(0, 2)
        return pltpu.make_async_remote_copy(
            src_ref=s.pay.at[c, kinds], dst_ref=s.recv.at[source, kinds],
            send_sem=(s.sent3 if flat else s.sent1).at[c],
            recv_sem=(s.came3 if flat else s.came1).at[source],
            device_id=where(target), device_id_type=MESH,
        )

    def ask(c, flat):
        other = solver(c)

        @pl.when(other == me)
        def _():
            s.recv[me] = s.pay[c]

        @pl.when(other != me)
        def _():
            question(c, False, me, other).start()
            if flat:
                question(c, True, me, other).start()

    def trace(k):
        def one(b):
            trace_problem(
                b, s.modes, s.got_up1, s.got_down1, s.rims, s.single, tables, s.pay, here=here
            )
            for n in range(parts):
                ask(b * parts + n, n == 0)

        loop(k * size, k * size + size, one)

    def answer(i):
        other = (me + i) % devices
        return pltpu.make_async_remote_copy(
            src_ref=s.back.at[other], dst_ref=s.came.at[my_chunk], send_sem=s.sent2.at[i],
            recv_sem=s.came2.at[my_chunk], device_id=where(other), device_id_type=MESH,
        )

    def solve_ring(h):
        @pl.when(my_half == h)
        def _():
            def arrive(i):
                other = (me + i) % devices
                question(0, False, other, other).wait_recv()

                @pl.when(my_chunk % parts == 0)
                def _():
                    question(0, True, other, other).wait_recv()

            loop(1, devices, arrive)
            total = devices * here
            lane = lax.broadcasted_iota(jnp.int32, (total, width), 1)
            ahead = total - levels
            jump = pltpu.roll(flat_rows(s.recv, 0, here), ahead, 0) - flat_rows(s.recv, 1, here)
            flat = flat_rows(s.recv, 2, here)
            beyond = pltpu.roll(pltpu.roll(flat, here, 0), width - 1, 1)
            whole = jnp.where(lane == 0, flat + beyond, 0.0)
            jump_flat = pltpu.roll(whole, ahead, 0) - whole
            both = table_times(s.mix, jnp.concatenate([jump, jump_flat], axis=1))
            solved = both[:, :width] * s.ring[0] + both[:, width:] * s.ring[1]
            mine = table_times(s.mix_back, solved)
            other = pltpu.roll(mine, levels, 0)
            if here % 8 == 0:
                s.back[:, 0] = mine.reshape(devices, here, width)
                s.back[:, 1] = other.reshape(devices, here, width)
            else:
                for i in range(devices):
                    s.back[i, 0] = mine[i * here : (i + 1) * here]
                    s.back[i, 1] = other[i * here : (i + 1) * here]
            loop(1, devices, lambda i: answer(i).start())
            s.came[my_chunk] = s.back[me]

    def fluxes(h):
        def arrive(c):
            other = solver(c)

            @pl.when(other != me)
            def _():
                pltpu.make_async_remote_copy(
                    src_ref=s.back.at[0], dst_ref=s.came.at[c], send_sem=s.sent2.at[0],
                    recv_sem=s.came2.at[c], device_id=where(other), device_id_type=MESH,
                ).wait_recv()

        loop(h * half, (h + 1) * half, arrive)
        for c in range(h * half, (h + 1) * half):
            b, n = c // parts, c % parts
            for kind in range(2):
                s.flux[b, kind * here : (kind + 1) * here, n * width : (n + 1) * width] = (
                    s.came[c, kind]
                )

        def own(k):
            loop(k * size, k * size + size, lambda b: flux_problem(
                b, s.flux, after, s.own_up2, s.own_down2, here=here))
            chain2.begin(k)

        loop(h * per, (h + 1) * per, own)

    def send_out(k):
        cut = pl.ds(k * size, size)
        return pltpu.make_async_copy(
            s.modes.at[pl.ds(0, here), cut], phi_all.at[pl.ds(0, here), cut], s.moved.at[k]
        )

    def send_tip(h):
        cut = pl.ds(h * chunk, chunk)
        return pltpu.make_async_copy(
            s.modes.at[here, cut], phi_all.at[here, cut], s.moved.at[pieces + h]
        )

    def sweep(k):
        loop(k * size, k * size + size, lambda b: sweep_problem(
            b, s.modes, s.flux, s.got_up1, s.got_up2, s.got_down1, s.got_down2, s.single, after,
            s.modes, here=here, levels=levels))
        cut = pl.ds(k * size, size)
        part = over_rows(s.home, s.modes[0:here, cut].reshape(here * size, rows, cols))
        part = times_table(part.reshape(here * size * rows, cols), s.col)
        s.modes[0:here, cut] = part.reshape(here, size, rows, cols)
        send_out(k).start()

    def tip(h):
        cut = slice(h * chunk, h * chunk + chunk)
        last = over_rows(s.home, s.modes[here, cut])
        last = times_table(last.reshape(chunk * rows, cols), s.col)
        s.modes[here, cut] = last.reshape(chunk, rows, cols)
        send_tip(h).start()

    def rim(h):
        cut = slice(h * chunk, h * chunk + chunk)
        if here % 8 == 0:
            flat = (s.flux[cut, 0:here, :] + s.rims[cut, 0:here, :]).reshape(chunk * here, cols)
            edges[cut] = times_table(flat, s.col).reshape(chunk, here, cols)
        else:
            for b in range(h * chunk, h * chunk + chunk):
                edges[b] = times_table(s.flux[b, 0:here, :] + s.rims[b, 0:here, :], s.col)

    filled = max(per, reach - 1)

    def drain1(i):
        relays(chain1, i, 1)

        @pl.when(i <= per)
        def _():
            trace(i - 1)

    def drain2(k):
        @pl.when(reach + k > filled)
        def _():
            relays(chain1, reach + k, 1)

        trace(per + k)

    def asked(c):
        other = solver(c)

        @pl.when(other != me)
        def _():
            question(c, False, me, other).wait_send()

            @pl.when(c % parts == 0)
            def _():
                question(c, True, me, other).wait_send()

    loop(here + 2, reach, lambda i: relays(chain1, i, 0))
    def traces0(k):
        @pl.when(reach + k >= here + 2)
        def _():
            relays(chain1, reach + k, 0)

        trace(k)

    loop(0, per, traces0)
    for fetch in fetches[early:]:
        fetch.wait()
    loop(1, reach, lambda i: relays(chain1, i, 1))
    solve_ring(0)
    def traces1(k):
        @pl.when(reach + k >= reach)
        def _():
            relays(chain1, reach + k, 1)

        trace(per + k)

    loop(0, per, traces1)
    solve_ring(1)
    fluxes(0)
    loop(1, reach - 2, lambda i: relays(chain2, i, 0))
    fluxes(1)
    loop(reach - 2, reach + 1, lambda i: relays(chain2, i, 0))
    loop(reach + 1, reach + per, lambda i: relays(chain2, i, 0))
    def drain3(i):
        relays(chain2, i, 1)

        @pl.when(i <= per)
        def _():
            sweep(i - 1)

    loop(1, reach, drain3)
    loop(max(reach, 1), per + 1, lambda i: sweep(i - 1))
    tip(0)
    rim(0)
    rim(1)
    chain1.finish(pieces)
    loop(0, devices, asked)
    loop(1, devices, lambda i: answer(i).wait_send())
    def sweeps1(k):
        @pl.when(reach + k >= reach)
        def _():
            relays(chain2, reach + k, 1)

        sweep(per + k)

    loop(0, per, sweeps1)
    tip(1)

    chain2.finish(pieces)
    loop(0, pieces, lambda k: send_out(k).wait())
    for h in range(2):
        send_tip(h).wait()


def project_kernel(first, following, edges, mult, next_mult, next_aux, phi, *, levels):
    t = pl.program_id(0)
    here = pl.num_programs(0)
    _, problems, rows, cols = first.shape

    @pl.when(t == 0)
    def _():
        phi[...] = first[0]

    moving = jnp.where(lax.axis_index("py") * here + t == levels - 1, 0.0, 1.0)
    row = lax.broadcasted_iota(jnp.int32, (rows, cols), 0)

    def one(b, carry):
        here_phi = phi[b]
        next_phi = following[0, b]
        phi[b] = next_phi
        rim = jnp.broadcast_to(edges[b, pl.ds(t, 1), :], (rows, cols))
        grad_time = (next_phi - here_phi) * moving
        grad_first = jnp.where(
            row == rows - 1, rim, pltpu.roll(here_phi, rows - 1, 0) - here_phi
        )
        grad_second = pltpu.roll(here_phi, cols - 1, 1) - here_phi
        mult_time, mult_first, mult_second = (mult[k, 0, b] for k in range(3))
        time_part = grad_time + mult_time / PENALTY
        along = grad_first + mult_first / PENALTY
        beside = grad_second + mult_second / PENALTY
        kinetic = 0.5 * (along * along + beside * beside)
        offset_one = 1.0 + time_part
        solid = kinetic > 1e-37
        root = jnp.exp(jnp.log(jnp.where(solid, kinetic, 1.0)) * (1.0 / 3.0))
        scaling = jnp.maximum(offset_one, 1.0) + jnp.where(solid, root, 0.0)
        twice = 2.0 * offset_one
        for newton_step in range(NEWTON):
            above = scaling * scaling * (2.0 * scaling - offset_one) + kinetic
            derivative = scaling * (3.0 * scaling - twice)
            scaling = jnp.maximum(above / derivative, 1.0)
        feasible = time_part + kinetic <= 0.0
        shrink = jnp.where(feasible, 1.0, 1.0 / scaling)
        out_time = jnp.where(feasible, time_part, time_part - (scaling - 1.0))
        out_along = along * shrink
        out_beside = beside * shrink
        next_aux[0, 0, b] = out_time
        next_aux[1, 0, b] = out_along
        next_aux[2, 0, b] = out_beside
        next_mult[0, 0, b] = mult_time + PENALTY * (grad_time - out_time)
        next_mult[1, 0, b] = mult_first + PENALTY * (grad_first - out_along)
        next_mult[2, 0, b] = mult_second + PENALTY * (grad_second - out_beside)
        return carry

    lax.fori_loop(0, problems, one, 0, unroll=4)


def params(which=None):
    if which is None:
        return pltpu.CompilerParams(vmem_limit_bytes=VMEM_LIMIT)
    return pltpu.CompilerParams(
        collective_id=which, has_side_effects=True, vmem_limit_bytes=VMEM_LIMIT
    )


def whole_block(shape):
    return pl.BlockSpec(shape, lambda *_: (0,) * len(shape))


def local(multiplier, auxiliary, density_start, density_end):
    _, here, problems, rows, cols = multiplier.shape
    blocks = lax.axis_size("py")
    inner = lax.axis_size("px")
    group = lax.axis_size("grp") * inner
    devices = group * blocks
    levels = here * blocks
    held = -(-here // 8) * 8
    width = problems * cols // devices
    parts = cols // width
    total = devices * here
    delay, depth = 3, 4
    chunk = problems // 2
    pieces = 2 * math.gcd(chunk, 4)
    size = problems // pieces
    fit = max(1, 256 // rows)
    shape = lambda *dims: jax.ShapeDtypeStruct(dims, f32)
    vector = lambda *dims: pltpu.VMEM(dims, f32)
    anywhere = pl.BlockSpec(memory_space=pl.ANY)
    dma = lambda *dims: pltpu.SemaphoreType.DMA(dims)

    col_table = halves(hartley(cols))
    row_table = halves(np.kron(np.eye(math.gcd(chunk, fit)), cosines(rows)))
    row_back = halves(np.kron(np.eye(math.gcd(math.gcd(size * here, chunk), fit)), cosines(rows).T))
    single, ahead, after = slab_tables(rows, cols, here, blocks)
    mix, inverse, extra = ring_tables(rows, cols, group, levels)
    wide = np.zeros((total, cols), np.float32)
    wide[:, :1] = extra
    ring = np.stack([inverse, wide]).reshape(2, total, parts, width).transpose(0, 2, 1, 3).copy()
    mix_back = halves(mix.T.astype(np.float64))
    mix = halves(mix.astype(np.float64))
    tables = [col_table, row_table, row_back, single, ahead, after, mix, mix_back, ring]

    plane = (problems, rows, cols)
    part = (chunk, rows, cols)
    table = lambda x: pltpu.VMEM(x.shape, x.dtype)
    scratch = [
        vector(depth, 3, *part), vector(depth, 3, *part), vector(*plane), vector(*plane),
        table(col_table), table(row_table), table(row_back), table(single), table(ahead[0]),
        table(after[0]), table(mix), table(mix), table(ring[:, 0]),
        vector(*part), vector(*part), vector(*part), vector(chunk, held, cols),
        vector(problems, held, cols),
        vector(here + 1, *plane), vector(devices, 3, here, width),
        vector(devices, 3, here, width), vector(devices, 2, here, width),
        vector(devices, 2, here, width), vector(problems, 2 * here, cols),
    ] + [vector(*plane)] * 12 + [dma(2, depth), dma(11), dma(pieces + 2)]
    scratch += [dma(pieces)] * 8 + [dma(devices)] * 6
    phi, edges = pl.pallas_call(
        functools.partial(solve_kernel, levels=levels, here=here, blocks=blocks, inner=inner,
                          pieces=pieces, delay=delay, depth=depth),
        out_shape=(shape(here + 1, *plane), shape(problems, here, cols)),
        in_specs=[anywhere] * 13,
        out_specs=(anywhere, pl.BlockSpec(memory_space=pltpu.VMEM)),
        scratch_shapes=scratch,
        compiler_params=params(0),
        name="solve",
    )(multiplier, auxiliary, density_start, density_end, *(jnp.asarray(x) for x in tables))

    out_shape = shape(*multiplier.shape)
    level_block = pl.BlockSpec((3, 1, *plane), lambda t: (0, t, 0, 0, 0))
    phi_block = whole_block((1, *plane))
    next_block = pl.BlockSpec((1, *plane), lambda t: (t + 1, 0, 0, 0))
    return pl.pallas_call(
        functools.partial(project_kernel, levels=levels),
        out_shape=(out_shape, out_shape),
        grid=(here,),
        in_specs=[phi_block, next_block, whole_block(edges.shape), level_block],
        out_specs=(level_block, level_block),
        scratch_shapes=[vector(*plane)],
        compiler_params=params(),
        name="project",
    )(phi, phi, edges, multiplier)


def solution(mesh):
    placed = (
        P(None, "py", None, ("grp", "px"), None),
        P(None, "py", None, ("grp", "px"), None),
        P(None, ("grp", "px"), None),
        P(None, ("grp", "px"), None),
    )
    return jax.shard_map(
        local,
        mesh=mesh,
        in_specs=placed,
        out_specs=(
            P(None, "py", None, ("grp", "px"), None),
            P(None, "py", None, ("grp", "px"), None),
        ),
        check_vma=False,
    )
```

```python
import functools
import math
import types

import jax
import jax.numpy as jnp
import ml_dtypes
import numpy as np
from jax import lax
from jax.experimental import pallas as pl
from jax.experimental.pallas import tpu as pltpu
from jax.sharding import PartitionSpec as P

NEWTON = 4
PENALTY = 1.0
VMEM_LIMIT = 60 * 1024 * 1024
SPACE = ("grp", "px")
EVERY = ("grp", "px", "py")
MESH = pl.DeviceIdType.MESH
bf16 = jnp.bfloat16
f32 = jnp.float32


def halves(table):
    high = table.astype(ml_dtypes.bfloat16)
    low = (table - high.astype(np.float64)).astype(ml_dtypes.bfloat16)
    return np.stack([high, low])


def hartley(length):
    angles = 2.0 * np.pi / length * (np.outer(np.arange(length), np.arange(length)) % length)
    return (np.cos(angles) + np.sin(angles)) / np.sqrt(length)


def cosines(length):
    k = np.arange(length)[:, None]
    x = np.arange(length)[None, :]
    weights = np.where(k == 0, np.sqrt(1.0 / length), np.sqrt(2.0 / length))
    return weights * np.cos(np.pi * k * (2 * x + 1) / (2 * length))


def slab_tables(rows, cols, here, blocks):
    j = np.arange(rows)[:, None]
    n = np.arange(cols)[None, :]
    lam = 4.0 * np.sin(np.pi * j / (2 * rows)) ** 2 + 4.0 * np.sin(np.pi * n / cols) ** 2
    sinh = np.sqrt(lam * (1.0 + 0.25 * lam))
    ratio = 1.0 / (1.0 + 0.5 * lam + sinh)
    positive = lam > 0.0
    full = ratio ** (2 * here * blocks)
    scale = np.where(positive, 0.5 / np.where(positive, sinh * (1.0 - full), 1.0), 0.0)
    edge = cosines(rows)[:, :1]
    low, high, down, low_q, high_q = [], [], [], [], []
    for block in range(blocks):
        first = block * here
        lows = [1.0 + ratio ** (2 * (first + v) + 1) for v in range(here + 1)]
        highs = [1.0 + ratio ** (2.0 * (blocks * here - 1 - first - v) + 1.0) for v in range(here + 1)]
        low.append(lows)
        high.append(highs)
        down.append([ratio**v * highs[v] for v in range(here + 1)])
        low_q.append([edge * ratio ** (here - v) * lows[v] for v in range(here)])
        high_q.append([edge * ratio**v * highs[v] for v in range(here)])
    single = np.stack([ratio, ratio**here, scale, edge * scale, np.broadcast_to(edge, lam.shape)])
    pack = lambda parts: np.asarray(parts, np.float32)
    ahead = np.concatenate([pack(low), pack(high), pack(down)], axis=1)
    after = np.concatenate([pack(low), pack(high), pack(low_q), pack(high_q)], axis=1)
    return single.astype(np.float32), ahead, after


def ring_tables(rows, cols, group, levels):
    r = np.arange(group)[:, None, None]
    k = np.arange(levels)[None, :, None]
    n = np.arange(cols)[None, None, :]
    tau = 4.0 * np.sin(np.pi * k / (2 * levels)) ** 2
    kappa = tau + 4.0 * np.sin(np.pi * n / cols) ** 2
    turn = 2.0 * np.sin(np.pi * r / group) ** 2
    positive = kappa > 0.0
    safe = np.where(positive, kappa, 1.0)
    shrink = 1.0 / (1.0 + 0.5 * safe + np.sqrt(safe * (1.0 + 0.25 * safe)))
    far = shrink**rows
    inverse = (1.0 - shrink) * (1.0 - far * far) / (
        (1.0 + shrink) * ((1.0 - far) ** 2 + 2.0 * far * turn)
    )
    inverse = np.where(positive, inverse, np.where(r == 0, 1.0 / rows, 0.0))
    edge = math.sqrt(1.0 / rows)
    flat = inverse[:, :, :1]
    moving = edge * flat / np.where(tau > 0.0, tau, 1.0)
    still = rows * edge / np.where(r > 0, 2.0 * turn, 1.0) * (r > 0)
    extra = np.where(tau > 0.0, moving, still)
    mix = np.kron(hartley(group), cosines(levels))
    flat_rows = group * levels
    return (
        mix,
        inverse.reshape(flat_rows, cols).astype(np.float32),
        extra.reshape(flat_rows, 1).astype(np.float32),
    )


def split(x):
    high = x.astype(bf16)
    return high, (x - high.astype(f32)).astype(bf16)


def mm(a, b):
    return jnp.dot(a, b, preferred_element_type=f32)


def times_table(x, table):
    high, low = split(x)
    return mm(high, table[0]) + (mm(low, table[0]) + mm(high, table[1]))


def table_times(table, x):
    high, low = split(x)
    return mm(table[0], high) + (mm(table[0], low) + mm(table[1], high))


def over_rows(table, x):
    units, rows, cols = x.shape
    size = table.shape[1]
    bunch = size // rows
    parts = []
    for g in range(units // bunch):
        part = x[g * bunch : (g + 1) * bunch].reshape(size, cols)
        parts.append(table_times(table, part).reshape(bunch, rows, cols))
    return parts[0] if len(parts) == 1 else jnp.concatenate(parts, axis=0)


def steps_from(me, blocks):
    return me, blocks - 1 - me


class Chain:
    def __init__(self, up, down, step, size, blocks):
        self.me = lax.axis_index("py")
        self.blocks, self.size, self.step = blocks, size, step
        self.far = steps_from(self.me, blocks)
        self.next = ((self.me + 1) % blocks, (self.me + blocks - 1) % blocks)
        self.refs = (up, down)

    def copy(self, way, source, k):
        _, got, _, sent, came = self.refs[way]
        cut = pl.ds(k * self.size, self.size)
        return pltpu.make_async_remote_copy(
            src_ref=source.at[cut],
            dst_ref=got.at[cut],
            send_sem=sent.at[k],
            recv_sem=came.at[k],
            device_id={"py": self.next[way]},
            device_id_type=MESH,
        )

    def greet(self):
        barrier = pltpu.get_barrier_semaphore()
        lower, upper = self.me > 0, self.me < self.blocks - 1

        @pl.when(lower)
        def _():
            pl.semaphore_signal(barrier, inc=1, device_id={"py": self.me - 1}, device_id_type=MESH)

        @pl.when(upper)
        def _():
            pl.semaphore_signal(barrier, inc=1, device_id={"py": self.me + 1}, device_id_type=MESH)

        @pl.when(lower & upper)
        def _():
            pl.semaphore_wait(barrier, 2)

        @pl.when(jnp.logical_not(lower & upper))
        def _():
            pl.semaphore_wait(barrier, 1)

    def clear(self):
        for way in range(2):
            got = self.refs[way][1]

            @pl.when(self.far[way] == 0)
            def _():
                got[...] = jnp.zeros_like(got)

    def begin(self, k):
        for way in range(2):

            @pl.when(self.far[way] == 0)
            def _():
                self.copy(way, self.refs[way][0], k).start()

    def relay(self, way, k, low, high):
        own, got, out, _, _ = self.refs[way]

        @pl.when((self.far[way] > 0) & (k >= low) & (k < high))
        def _():
            self.copy(way, out, k).wait_recv()

            @pl.when(self.far[way] < self.blocks - 1)
            def _():
                for q in range(self.size):
                    at = k * self.size + q
                    out[at] = own[at] + self.step[...] * got[at]
                self.copy(way, out, k).start()

    def finish(self, pieces):
        for way in range(2):

            @pl.when(self.far[way] < self.blocks - 1)
            def _():
                def one(k, carry):
                    self.copy(way, self.refs[way][2], k).wait_send()
                    return carry

                lax.fori_loop(0, pieces, one, 0)


def trace_problem(b, modes, up, down, rims, single, tables, pay, *, here):
    rows, cols = up.shape[1], up.shape[2]
    width = pay.shape[3]
    parts = cols // width
    lane = lax.broadcasted_iota(jnp.int32, (1, cols), 1)
    parity = lax.broadcasted_iota(jnp.int32, (8, cols), 0) % 2 == 0
    total = [jnp.zeros((8, cols), f32) for _ in range(here)]
    for c in range(rows // 8):
        cut = slice(c * 8, c * 8 + 8)
        ratio, weight = single[0, cut, :], single[3, cut, :]
        value = up[b, cut, :]
        sums = []
        for v in range(here):
            if v:
                value = ratio * value
            value = value + tables[v, cut, :] * modes[v, b, cut, :]
            sums.append(tables[here + 1 + v, cut, :] * value)
        behind = down[b, cut, :]
        for v in range(here, -1, -1):
            if v < here:
                total[v] = total[v] + weight * (sums[v] + tables[v, cut, :] * behind)
            behind = ratio * (behind + tables[here + 1 + v, cut, :] * modes[v, b, cut, :])

    def put(kind, v, row):
        for n in range(parts):
            pay[b * parts + n, kind, v : v + 1, :] = row[:, n * width : (n + 1) * width]

    for v in range(here):
        even = jnp.sum(jnp.where(parity, total[v], 0.0), axis=0, keepdims=True)
        odd = jnp.sum(jnp.where(parity, 0.0, total[v]), axis=0, keepdims=True)
        put(0, v, even + odd)
        put(1, v, even - odd + rims[b, v : v + 1, :])
        flat = jnp.where(lane == 0, modes[v, b, 0:1, :], 0.0)
        if v == 0:
            beyond = pltpu.roll(modes[here, b, 0:8, :], 1, 1)[0:1]
            flat = flat + jnp.where(lane == 1, beyond, 0.0)
        put(2, v, flat)


def sweep_problem(b, modes, flux, up1, up2, down1, down2, single, tables, wave, *, here, levels):
    rows, cols = up1.shape[1], up1.shape[2]
    first = lax.axis_index("py") * here
    for c in range(rows // 8):
        cut = slice(c * 8, c * 8 + 8)
        ratio, scale, edge = single[0, cut, :], single[2, cut, :], single[4, cut, :]
        sign = jnp.where(
            lax.broadcasted_iota(jnp.int32, (8, cols), 0) % 2 == 0, edge, -edge
        )
        value = up1[b, cut, :] + up2[b, cut, :]
        source, sums = [], []
        for v in range(here + 1):
            now = modes[v, b, cut, :]
            if v < here:
                mine = jnp.broadcast_to(flux[b, v : v + 1, :], (8, cols))
                other = jnp.broadcast_to(flux[b, here + v : here + v + 1, :], (8, cols))
                now = now + (sign * mine - edge * other)
            source.append(now)
            if v:
                value = ratio * value
            value = value + tables[v, cut, :] * now
            sums.append(tables[here + 1 + v, cut, :] * value)
        behind = down1[b, cut, :] + down2[b, cut, :]
        for v in range(here, -1, -1):
            wave[v, b, cut, :] = scale * (sums[v] + tables[v, cut, :] * behind)
            behind = ratio * (behind + tables[here + 1 + v, cut, :] * source[v])
        if c == 0:
            spot = (lax.broadcasted_iota(jnp.int32, (8, 128), 0) == 0) & (
                lax.broadcasted_iota(jnp.int32, (8, 128), 1) == 0
            )
            below = 0.5 * (up1[b, 0:8, 0:128] + up2[b, 0:8, 0:128])
            whole = below + 0.5 * (down1[b, 0:8, 0:128] + down2[b, 0:8, 0:128])
            for v in range(here + 1):
                whole = whole + source[v][:, 0:128]
            mean = whole * (1.0 / levels)
            level_value = jnp.zeros((8, 128), f32)
            for v in range(here + 1):
                wave[v, b, 0:8, 0:128] = jnp.where(spot, level_value, wave[v, b, 0:8, 0:128])
                if v < here:
                    below = below + source[v][:, 0:128]
                    count = (first + (v + 1)).astype(f32)
                    level_value = level_value - (below - count * mean)


def flux_problem(b, flux, tables, up, down, *, here):
    rows, cols = up.shape[1], up.shape[2]
    sign = jnp.where(lax.broadcasted_iota(jnp.int32, (rows, cols), 0) % 2 == 0, 1.0, -1.0)
    base = 2 * (here + 1)
    rise = jnp.zeros((rows, cols), f32)
    fall = jnp.zeros((rows, cols), f32)
    for v in range(here):
        mine = jnp.broadcast_to(flux[b, v : v + 1, :], (rows, cols))
        other = jnp.broadcast_to(flux[b, here + v : here + v + 1, :], (rows, cols))
        both = sign * mine - other
        rise = rise + tables[base + v] * both
        fall = fall + tables[base + here + v] * both
    up[b] = rise
    down[b] = fall


def flat_rows(ref, kind, here):
    devices, width = ref.shape[0], ref.shape[3]
    if here % 8 == 0:
        return ref[:, kind].reshape(devices * here, width)
    return jnp.concatenate([ref[i, kind] for i in range(devices)], axis=0)


SCRATCH = (
    "mult", "aux", "start", "end", "col", "row", "home", "single", "ahead", "after", "mix",
    "mix_back", "ring",
    "prev", "body", "spread", "tail", "rims", "modes", "pay", "recv", "back", "came", "flux",
    "own_up1", "own_down1", "got_up1", "got_down1", "out_up1", "out_down1",
    "own_up2", "own_down2", "got_up2", "got_down2", "out_up2", "out_down2",
    "streamed", "fetched", "moved",
    "sent_up1", "sent_down1", "came_up1", "came_down1",
    "sent_up2", "sent_down2", "came_up2", "came_down2",
    "sent1", "came1", "sent2", "came2", "sent3", "came3",
)


def loop(low, high, action, unroll=1):
    def one(i, carry):
        action(i)
        return carry

    if not (isinstance(low, int) and isinstance(high, int) and high <= low):
        lax.fori_loop(low, high, one, 0, unroll=unroll)


def solve_kernel(
    mult_all, aux_all, start_all, end_all, col_all, row_all, home_all, single_all, ahead_all,
    after_all, mix_all, mix_back_all, ring_all, phi_all, edges, *scratch,
    levels, here, blocks, inner, pieces, delay, depth
):
    s = types.SimpleNamespace(**dict(zip(SCRATCH, scratch)))
    problems, rows, cols = s.start.shape
    devices, width = s.pay.shape[0], s.pay.shape[3]
    chunk, per, half = problems // 2, pieces // 2, devices // 2
    size = problems // pieces
    parts = cols // width
    reach = delay * (blocks - 1)
    me_py = lax.axis_index("py")
    me_space = lax.axis_index("grp") * inner + lax.axis_index("px")
    me = me_space * blocks + me_py
    my_half = me_space % 2
    my_chunk = my_half * half + (me_space // 2) * blocks + me_py
    tables, after = s.ahead, s.after

    def where(flat):
        return {
            "grp": flat // (inner * blocks),
            "px": flat // blocks % inner,
            "py": flat % blocks,
        }

    def solver(c):
        i = c % half
        return (2 * (i // blocks) + c // half) * blocks + i % blocks

    def chain(n):
        part = lambda name: getattr(s, name % n)
        return Chain(
            *((part("own_%s%%d" % way), part("got_%s%%d" % way), part("out_%s%%d" % way),
               part("sent_%s%%d" % way), part("came_%s%%d" % way)) for way in ("up", "down")),
            s.single.at[1], size, blocks,
        )

    chain1, chain2 = chain(1), chain(2)

    def relays(which, i, owner):
        for way in range(2):
            k = i - delay * which.far[way]
            which.relay(way, owner * per + k, owner * per, (owner + 1) * per)

    def stream(g):
        c, t, at = g // here, g % here, g % depth
        cut = pl.ds(c * chunk, chunk)
        return [
            pltpu.make_async_copy(mult_all.at[:, t, cut], s.mult.at[at], s.streamed.at[0, at]),
            pltpu.make_async_copy(aux_all.at[:, t, cut], s.aux.at[at], s.streamed.at[1, at]),
        ]

    pairs = [
        (start_all, s.start), (end_all, s.end), (col_all, s.col), (row_all, s.row),
        (single_all, s.single), (ahead_all.at[me_py], s.ahead), (after_all.at[me_py], s.after),
        (mix_all, s.mix), (mix_back_all, s.mix_back), (ring_all.at[:, my_chunk % parts], s.ring),
        (home_all, s.home),
    ]
    fetches = [pltpu.make_async_copy(x, y, s.fetched.at[i]) for i, (x, y) in enumerate(pairs)]
    early = 6
    for g in range(min(depth, 2 * here)):
        for copy in stream(g):
            copy.start()
        if g == 0:
            for fetch in fetches[:early]:
                fetch.start()
    for fetch in fetches[early:]:
        fetch.start()
    barrier = pltpu.get_barrier_semaphore()

    def hail(i):
        pl.semaphore_signal(
            barrier, inc=1, device_id=where((me + i) % devices), device_id_type=MESH
        )

    loop(1, devices, hail)
    chain1.clear()
    chain2.clear()

    @pl.when(my_chunk % parts != 0)
    def _():
        s.recv[:, 2] = jnp.zeros((devices, here, width), f32)

    for fetch in fetches[:early]:
        fetch.wait()
    row = lax.broadcasted_iota(jnp.int32, (rows, cols), 0)

    def across_rows(c, v):
        base = c * chunk
        s.modes[v, base : base + chunk] = over_rows(s.row, s.spread[...])
        ratio, low, falling = s.single[0], tables[v], tables[2 * (here + 1) + v]
        for b in range(base, base + chunk):
            value = s.modes[v, b]
            s.own_up1[b] = ratio * s.own_up1[b] + low * value
            s.own_down1[b] = s.own_down1[b] + falling * value

    def across_cols(values):
        flat = values[...].reshape(chunk * rows, cols)
        s.spread[...] = times_table(flat, s.col).reshape(chunk, rows, cols)

    def source(c, t):
        g = c * here + t
        at = g % depth
        level = me_py * here + t
        for copy in stream(g):
            copy.wait()
        across_rows(c, jnp.maximum(t - 1, 0))
        keep = jnp.where(level == levels - 1, 0.0, 1.0)
        begin = jnp.where(level == 0, -1.0 / PENALTY, 0.0)
        finish = jnp.where(level == levels - 1, 1.0 / PENALTY, 0.0)
        for b in range(chunk):
            along = s.aux[at, 1, b] - s.mult[at, 1, b] / PENALTY
            s.tail[b, pl.ds(t, 1), :] = along[rows - 1 :, :]
            beside = jnp.where(row == 0, 0.0, pltpu.roll(along, 1, 0))
            along = jnp.where(row == rows - 1, 0.0, along)
            second = s.aux[at, 2, b] - s.mult[at, 2, b] / PENALTY
            side = pltpu.roll(second, 1, 1) - second
            now = (s.aux[at, 0, b] - s.mult[at, 0, b] / PENALTY) * keep
            boundary = begin * s.start[c * chunk + b] + finish * s.end[c * chunk + b]
            s.body[b] = s.prev[b] - now + beside - along + side + boundary
            s.prev[b] = now
        across_cols(s.body)

        @pl.when(g + depth < 2 * here)
        def _():
            for copy in stream(g + depth):
                copy.start()

        if c == 1:
            relays(chain1, t + 1, 0)

    for c in range(2):
        cut = slice(c * chunk, c * chunk + chunk)
        s.prev[...] = jnp.zeros_like(s.prev)
        s.tail[...] = jnp.zeros_like(s.tail)
        s.spread[...] = jnp.zeros_like(s.spread)
        s.own_up1[cut] = jnp.zeros((chunk, rows, cols), f32)
        s.own_down1[cut] = jnp.zeros((chunk, rows, cols), f32)
        loop(0, here, functools.partial(source, c))
        across_rows(c, here - 1)
        across_cols(s.prev)
        across_rows(c, here)
        held = s.tail.shape[1]
        if c == 0:
            pl.semaphore_wait(barrier, devices - 1)
        loop(c * per, (c + 1) * per, chain1.begin)
        if c == 1:
            relays(chain1, here + 1, 0)
        flat = s.tail[...].reshape(chunk * held, cols)
        s.rims[cut] = times_table(flat, s.col).reshape(chunk, held, cols)

    def question(c, flat, source, target):
        kinds = pl.ds(2, 1) if flat else pl.ds(0, 2)
        return pltpu.make_async_remote_copy(
            src_ref=s.pay.at[c, kinds], dst_ref=s.recv.at[source, kinds],
            send_sem=(s.sent3 if flat else s.sent1).at[c],
            recv_sem=(s.came3 if flat else s.came1).at[source],
            device_id=where(target), device_id_type=MESH,
        )

    def ask(c, flat):
        other = solver(c)

        @pl.when(other == me)
        def _():
            s.recv[me] = s.pay[c]

        @pl.when(other != me)
        def _():
            question(c, False, me, other).start()
            if flat:
                question(c, True, me, other).start()

    def trace(k):
        def one(b):
            trace_problem(
                b, s.modes, s.got_up1, s.got_down1, s.rims, s.single, tables, s.pay, here=here
            )
            for n in range(parts):
                ask(b * parts + n, n == 0)

        loop(k * size, k * size + size, one)

    def answer(i):
        other = (me + i) % devices
        return pltpu.make_async_remote_copy(
            src_ref=s.back.at[other], dst_ref=s.came.at[my_chunk], send_sem=s.sent2.at[i],
            recv_sem=s.came2.at[my_chunk], device_id=where(other), device_id_type=MESH,
        )

    def solve_ring(h):
        @pl.when(my_half == h)
        def _():
            def arrive(i):
                other = (me + i) % devices
                question(0, False, other, other).wait_recv()

                @pl.when(my_chunk % parts == 0)
                def _():
                    question(0, True, other, other).wait_recv()

            loop(1, devices, arrive)
            total = devices * here
            lane = lax.broadcasted_iota(jnp.int32, (total, width), 1)
            ahead = total - levels
            jump = pltpu.roll(flat_rows(s.recv, 0, here), ahead, 0) - flat_rows(s.recv, 1, here)
            flat = flat_rows(s.recv, 2, here)
            beyond = pltpu.roll(pltpu.roll(flat, here, 0), width - 1, 1)
            whole = jnp.where(lane == 0, flat + beyond, 0.0)
            jump_flat = pltpu.roll(whole, ahead, 0) - whole
            both = table_times(s.mix, jnp.concatenate([jump, jump_flat], axis=1))
            solved = both[:, :width] * s.ring[0] + both[:, width:] * s.ring[1]
            mine = table_times(s.mix_back, solved)
            other = pltpu.roll(mine, levels, 0)
            if here % 8 == 0:
                s.back[:, 0] = mine.reshape(devices, here, width)
                s.back[:, 1] = other.reshape(devices, here, width)
            else:
                for i in range(devices):
                    s.back[i, 0] = mine[i * here : (i + 1) * here]
                    s.back[i, 1] = other[i * here : (i + 1) * here]
            loop(1, devices, lambda i: answer(i).start())
            s.came[my_chunk] = s.back[me]

    def fluxes(h):
        def arrive(c):
            other = solver(c)

            @pl.when(other != me)
            def _():
                pltpu.make_async_remote_copy(
                    src_ref=s.back.at[0], dst_ref=s.came.at[c], send_sem=s.sent2.at[0],
                    recv_sem=s.came2.at[c], device_id=where(other), device_id_type=MESH,
                ).wait_recv()

        loop(h * half, (h + 1) * half, arrive)
        for c in range(h * half, (h + 1) * half):
            b, n = c // parts, c % parts
            for kind in range(2):
                s.flux[b, kind * here : (kind + 1) * here, n * width : (n + 1) * width] = (
                    s.came[c, kind]
                )

        def own(k):
            loop(k * size, k * size + size, lambda b: flux_problem(
                b, s.flux, after, s.own_up2, s.own_down2, here=here))
            chain2.begin(k)

        loop(h * per, (h + 1) * per, own)

    def send_out(k):
        cut = pl.ds(k * size, size)
        return pltpu.make_async_copy(
            s.modes.at[pl.ds(0, here), cut], phi_all.at[pl.ds(0, here), cut], s.moved.at[k]
        )

    def send_tip(h):
        cut = pl.ds(h * chunk, chunk)
        return pltpu.make_async_copy(
            s.modes.at[here, cut], phi_all.at[here, cut], s.moved.at[pieces + h]
        )

    def sweep(k):
        loop(k * size, k * size + size, lambda b: sweep_problem(
            b, s.modes, s.flux, s.got_up1, s.got_up2, s.got_down1, s.got_down2, s.single, after,
            s.modes, here=here, levels=levels))
        cut = pl.ds(k * size, size)
        part = over_rows(s.home, s.modes[0:here, cut].reshape(here * size, rows, cols))
        part = times_table(part.reshape(here * size * rows, cols), s.col)
        s.modes[0:here, cut] = part.reshape(here, size, rows, cols)
        send_out(k).start()

    def tip(h):
        cut = slice(h * chunk, h * chunk + chunk)
        last = over_rows(s.home, s.modes[here, cut])
        last = times_table(last.reshape(chunk * rows, cols), s.col)
        s.modes[here, cut] = last.reshape(chunk, rows, cols)
        send_tip(h).start()

    def rim(h):
        cut = slice(h * chunk, h * chunk + chunk)
        if here % 8 == 0:
            flat = (s.flux[cut, 0:here, :] + s.rims[cut, 0:here, :]).reshape(chunk * here, cols)
            edges[cut] = times_table(flat, s.col).reshape(chunk, here, cols)
        else:
            for b in range(h * chunk, h * chunk + chunk):
                edges[b] = times_table(s.flux[b, 0:here, :] + s.rims[b, 0:here, :], s.col)

    filled = max(per, reach - 1)

    def drain1(i):
        relays(chain1, i, 1)

        @pl.when(i <= per)
        def _():
            trace(i - 1)

    def drain2(k):
        @pl.when(reach + k > filled)
        def _():
            relays(chain1, reach + k, 1)

        trace(per + k)

    def asked(c):
        other = solver(c)

        @pl.when(other != me)
        def _():
            question(c, False, me, other).wait_send()

            @pl.when(c % parts == 0)
            def _():
                question(c, True, me, other).wait_send()

    loop(here + 2, reach, lambda i: relays(chain1, i, 0))
    def traces0(k):
        @pl.when(reach + k >= here + 2)
        def _():
            relays(chain1, reach + k, 0)

        trace(k)

    loop(0, per, traces0)
    for fetch in fetches[early:]:
        fetch.wait()
    loop(1, reach, lambda i: relays(chain1, i, 1))
    solve_ring(0)
    def traces1(k):
        @pl.when(reach + k >= reach)
        def _():
            relays(chain1, reach + k, 1)

        trace(per + k)

    loop(0, per, traces1)
    solve_ring(1)
    fluxes(0)
    loop(1, reach - 2, lambda i: relays(chain2, i, 0))
    fluxes(1)
    loop(reach - 2, reach + 1, lambda i: relays(chain2, i, 0))
    loop(reach + 1, reach + per, lambda i: relays(chain2, i, 0))
    def drain3(i):
        relays(chain2, i, 1)

        @pl.when(i <= per)
        def _():
            sweep(i - 1)

    loop(1, reach, drain3)
    loop(max(reach, 1), per + 1, lambda i: sweep(i - 1))
    tip(0)
    rim(0)
    rim(1)
    chain1.finish(pieces)
    loop(0, devices, asked)
    loop(1, devices, lambda i: answer(i).wait_send())
    def sweeps1(k):
        @pl.when(reach + k >= reach)
        def _():
            relays(chain2, reach + k, 1)

        sweep(per + k)

    loop(0, per, sweeps1)
    tip(1)

    chain2.finish(pieces)
    loop(0, pieces, lambda k: send_out(k).wait())
    for h in range(2):
        send_tip(h).wait()


def project_kernel(first, following, edges, mult, next_mult, next_aux, phi, *, levels):
    t = pl.program_id(0)
    here = pl.num_programs(0)
    _, problems, rows, cols = first.shape

    @pl.when(t == 0)
    def _():
        phi[...] = first[0]

    moving = jnp.where(lax.axis_index("py") * here + t == levels - 1, 0.0, 1.0)
    row = lax.broadcasted_iota(jnp.int32, (rows, cols), 0)

    def one(b, carry):
        here_phi = phi[b]
        next_phi = following[0, b]
        phi[b] = next_phi
        rim = jnp.broadcast_to(edges[b, pl.ds(t, 1), :], (rows, cols))
        grad_time = (next_phi - here_phi) * moving
        grad_first = jnp.where(
            row == rows - 1, rim, pltpu.roll(here_phi, rows - 1, 0) - here_phi
        )
        grad_second = pltpu.roll(here_phi, cols - 1, 1) - here_phi
        mult_time, mult_first, mult_second = (mult[k, 0, b] for k in range(3))
        time_part = grad_time + mult_time / PENALTY
        along = grad_first + mult_first / PENALTY
        beside = grad_second + mult_second / PENALTY
        kinetic = 0.5 * (along * along + beside * beside)
        offset_one = 1.0 + time_part
        solid = kinetic > 1e-37
        root = jnp.exp(jnp.log(jnp.where(solid, kinetic, 1.0)) * (1.0 / 3.0))
        scaling = jnp.maximum(offset_one, 1.0) + jnp.where(solid, root, 0.0)
        twice = 2.0 * offset_one
        for newton_step in range(NEWTON):
            above = scaling * scaling * (2.0 * scaling - offset_one) + kinetic
            derivative = scaling * (3.0 * scaling - twice)
            scaling = jnp.maximum(above / derivative, 1.0)
        feasible = time_part + kinetic <= 0.0
        shrink = jnp.where(feasible, 1.0, 1.0 / scaling)
        out_time = jnp.where(feasible, time_part, time_part - (scaling - 1.0))
        out_along = along * shrink
        out_beside = beside * shrink
        next_aux[0, 0, b] = out_time
        next_aux[1, 0, b] = out_along
        next_aux[2, 0, b] = out_beside
        next_mult[0, 0, b] = mult_time + PENALTY * (grad_time - out_time)
        next_mult[1, 0, b] = mult_first + PENALTY * (grad_first - out_along)
        next_mult[2, 0, b] = mult_second + PENALTY * (grad_second - out_beside)
        return carry

    lax.fori_loop(0, problems, one, 0, unroll=16)


def params(which=None):
    if which is None:
        return pltpu.CompilerParams(vmem_limit_bytes=VMEM_LIMIT)
    return pltpu.CompilerParams(
        collective_id=which, has_side_effects=True, vmem_limit_bytes=VMEM_LIMIT
    )


def whole_block(shape):
    return pl.BlockSpec(shape, lambda *_: (0,) * len(shape))


def local(multiplier, auxiliary, density_start, density_end):
    _, here, problems, rows, cols = multiplier.shape
    blocks = lax.axis_size("py")
    inner = lax.axis_size("px")
    group = lax.axis_size("grp") * inner
    devices = group * blocks
    levels = here * blocks
    held = -(-here // 8) * 8
    width = problems * cols // devices
    parts = cols // width
    total = devices * here
    delay, depth = 3, 4
    chunk = problems // 2
    pieces = 2 * math.gcd(chunk, 4)
    size = problems // pieces
    fit = max(1, 256 // rows)
    shape = lambda *dims: jax.ShapeDtypeStruct(dims, f32)
    vector = lambda *dims: pltpu.VMEM(dims, f32)
    anywhere = pl.BlockSpec(memory_space=pl.ANY)
    dma = lambda *dims: pltpu.SemaphoreType.DMA(dims)

    col_table = halves(hartley(cols))
    row_table = halves(np.kron(np.eye(math.gcd(chunk, fit)), cosines(rows)))
    row_back = halves(np.kron(np.eye(math.gcd(math.gcd(size * here, chunk), fit)), cosines(rows).T))
    single, ahead, after = slab_tables(rows, cols, here, blocks)
    mix, inverse, extra = ring_tables(rows, cols, group, levels)
    wide = np.zeros((total, cols), np.float32)
    wide[:, :1] = extra
    ring = np.stack([inverse, wide]).reshape(2, total, parts, width).transpose(0, 2, 1, 3).copy()
    mix_back = halves(mix.T.astype(np.float64))
    mix = halves(mix.astype(np.float64))
    tables = [col_table, row_table, row_back, single, ahead, after, mix, mix_back, ring]

    plane = (problems, rows, cols)
    part = (chunk, rows, cols)
    table = lambda x: pltpu.VMEM(x.shape, x.dtype)
    scratch = [
        vector(depth, 3, *part), vector(depth, 3, *part), vector(*plane), vector(*plane),
        table(col_table), table(row_table), table(row_back), table(single), table(ahead[0]),
        table(after[0]), table(mix), table(mix), table(ring[:, 0]),
        vector(*part), vector(*part), vector(*part), vector(chunk, held, cols),
        vector(problems, held, cols),
        vector(here + 1, *plane), vector(devices, 3, here, width),
        vector(devices, 3, here, width), vector(devices, 2, here, width),
        vector(devices, 2, here, width), vector(problems, 2 * here, cols),
    ] + [vector(*plane)] * 12 + [dma(2, depth), dma(11), dma(pieces + 2)]
    scratch += [dma(pieces)] * 8 + [dma(devices)] * 6
    phi, edges = pl.pallas_call(
        functools.partial(solve_kernel, levels=levels, here=here, blocks=blocks, inner=inner,
                          pieces=pieces, delay=delay, depth=depth),
        out_shape=(shape(here + 1, *plane), shape(problems, here, cols)),
        in_specs=[anywhere] * 13,
        out_specs=(anywhere, pl.BlockSpec(memory_space=pltpu.VMEM)),
        scratch_shapes=scratch,
        compiler_params=params(0),
        name="solve",
    )(multiplier, auxiliary, density_start, density_end, *(jnp.asarray(x) for x in tables))

    out_shape = shape(*multiplier.shape)
    level_block = pl.BlockSpec((3, 1, *plane), lambda t: (0, t, 0, 0, 0))
    phi_block = whole_block((1, *plane))
    next_block = pl.BlockSpec((1, *plane), lambda t: (t + 1, 0, 0, 0))
    return pl.pallas_call(
        functools.partial(project_kernel, levels=levels),
        out_shape=(out_shape, out_shape),
        grid=(here,),
        in_specs=[phi_block, next_block, whole_block(edges.shape), level_block],
        out_specs=(level_block, level_block),
        scratch_shapes=[vector(*plane)],
        compiler_params=params(),
        name="project",
    )(phi, phi, edges, multiplier)


def solution(mesh):
    placed = (
        P(None, "py", None, ("grp", "px"), None),
        P(None, "py", None, ("grp", "px"), None),
        P(None, ("grp", "px"), None),
        P(None, ("grp", "px"), None),
    )
    return jax.shard_map(
        local,
        mesh=mesh,
        in_specs=placed,
        out_specs=(
            P(None, "py", None, ("grp", "px"), None),
            P(None, "py", None, ("grp", "px"), None),
        ),
        check_vma=False,
    )
```
